256 devices in a mesh: seg: 32 (over x, z), tp: 8 (over y, core).
Axes of the slice: x: 4, y: 4, z: 8, core: 2. Of those that a mesh axis runs over, the one named last changes fastest.
Arguments:
- queries: bfloat16 [8192, 8192], P('seg', 'tp'), may hold values from -8 to 8
- keys_own: bfloat16 [8192, 1024], P('seg', 'tp'), may hold values from -8 to 8
- values_own: bfloat16 [8192, 1024], P('seg', 'tp'), may hold values from -6 to 6
- out_grad: bfloat16 [8192, 8192], P('seg', 'tp'), may hold values from -6 to 6
- summary_states: bfloat16 [1600, 8192], P('seg'), may hold values from -6 to 6
- w_key: bfloat16 [8192, 1024], P(None, 'tp'), may hold values from -0.0625 to 0.0625
- w_value: bfloat16 [8192, 1024], P(None, 'tp'), may hold values from -0.0625 to 0.0625
- summary_grad: bfloat16 [1600, 8192], P('seg', 'tp'), may hold values from -6 to 6
Outputs:
- query_grad: bfloat16 [8192, 8192], P('seg', 'tp')
- key_grad: bfloat16 [8192, 1024], P('seg', 'tp')
- value_grad: bfloat16 [8192, 1024], P('seg', 'tp')
- state_grad: bfloat16 [1600, 8192], P('seg', 'tp')
The draws below stay inside these ranges and needn't reach their ends.
All inputs are finite; a program needn't handle non-finite values.
Results may differ from the reference program's by a relative error of at most 0.023.
Values may be sent and summed in bfloat16 or wider, within the bound.
A program may use at most 256 MiB of HBM per device.

```python
import jax
import jax.numpy as jnp
from jax import lax

D = 8192
HEADS = 64
KVH = 8
HD = 128
M = 50
TOK_DEV = 256
TOKENS = 8192
NSUM = 1600
N_SEG = 32


def noise_field(key, width):
    return jnp.clip(jax.random.normal(key, (TOKENS, width), jnp.float32), -6.0, 6.0)


def draw_queries(key, part):
    base_noise = noise_field(jax.random.fold_in(key, 11), HEADS * HD)
    return base_noise.astype(jnp.bfloat16)


def draw_keys_own(key, part):
    base_noise = noise_field(jax.random.fold_in(key, 12), KVH * HD)
    return base_noise.astype(jnp.bfloat16)


def levels(key, shape, pieces, smallest, high):
    def one(axis_at, parts):
        heights = jax.random.uniform(jax.random.fold_in(jax.random.fold_in(key, 6), axis_at), (parts,), jnp.float32, smallest / len(pieces), high / len(pieces))
        return jnp.repeat(jnp.exp(heights), shape[axis_at] // parts).reshape((-1,) + (1,) * (len(shape) - axis_at - 1))

    level = one(*pieces[0])
    for cut in pieces[1:]:
        level = level * one(*cut)
    return level


def noise(own_key, shape, scale, most, split=(), dtype=jnp.bfloat16):
    level = levels(own_key, shape, split, -0.22, 0.18) if split else 1.0
    result = jax.random.normal(own_key, shape, jnp.float32) * scale * level
    return jnp.minimum(jnp.maximum(result, -most), most).astype(dtype)


def setup_inputs(seed: int = 0) -> dict:
    arg_keys = jax.random.split(jax.random.key(seed), 9)
    queries = draw_queries(jax.random.fold_in(arg_keys[8], 71), 0)
    keys_own = draw_keys_own(jax.random.fold_in(arg_keys[8], 71), 0)
    values_own = noise(arg_keys[2], (TOKENS, KVH * HD), 1.0, 6.0, ((0, 32), (1, 8)))
    out_grad = noise(arg_keys[3], (TOKENS, HEADS * HD), 1.0, 6.0, ((0, 32), (1, 8)))
    summary_states = noise(arg_keys[4], (NSUM, D), 1.0, 6.0, ((0, 32),))
    w_key = noise(arg_keys[5], (D, KVH * HD), D ** -0.5, 0.0625, ((1, 8),))
    w_value = noise(arg_keys[6], (D, KVH * HD), D ** -0.5, 0.0625, ((1, 8),))
    summary_grad = noise(arg_keys[7], (NSUM, D), 1.0, 6.0, ((0, 32), (1, 8)))
    return dict(queries=queries, keys_own=keys_own, values_own=values_own, out_grad=out_grad, summary_states=summary_states, w_key=w_key, w_value=w_value, summary_grad=summary_grad)


def reference(queries, keys_own, values_own, out_grad, summary_states, w_key, w_value, summary_grad):
    group = HEADS // KVH
    scale = HD ** -0.5
    nsum = M * N_SEG
    nkeys = nsum + TOK_DEV
    sum_keys = jnp.dot(summary_states, w_key, preferred_element_type=jnp.float32).astype(jnp.bfloat16)
    sum_vals = jnp.dot(summary_states, w_value, preferred_element_type=jnp.float32).astype(jnp.bfloat16)
    row_pos = jnp.arange(TOK_DEV)[:, None]
    col_pos = jnp.arange(nkeys)[None, :]
    acc_keys = jnp.zeros((nsum, KVH, HD), jnp.float32)
    acc_vals = jnp.zeros((nsum, KVH, HD), jnp.float32)
    query_parts = []
    key_parts = []
    value_parts = []
    for segment in range(N_SEG):
        lo = segment * TOK_DEV
        hi = lo + TOK_DEV
        keyset = jnp.concatenate([sum_keys, keys_own[lo:hi]], 0).reshape(nkeys, KVH, HD).astype(jnp.float32)
        valset = jnp.concatenate([sum_vals, values_own[lo:hi]], 0).reshape(nkeys, KVH, HD).astype(jnp.float32)
        query = queries[lo:hi].reshape(TOK_DEV, KVH, group, HD).astype(jnp.float32)
        grad = out_grad[lo:hi].reshape(TOK_DEV, KVH, group, HD).astype(jnp.float32)
        visible = jnp.where(col_pos < nsum, col_pos < segment * M, (col_pos - nsum) <= row_pos)
        scores = jnp.einsum('snhd,knd->nhsk', query, keyset) * scale
        scores = jnp.where(visible, scores, -jnp.inf)
        probs = jnp.exp(scores - jnp.max(scores, axis=-1, keepdims=True))
        probs = probs / jnp.sum(probs, axis=-1, keepdims=True)
        probs_b = probs.astype(jnp.bfloat16).astype(jnp.float32)
        attn = jnp.einsum('nhsk,knd->snhd', probs_b, valset)
        delta = jnp.einsum('snhd,snhd->nhs', grad, attn)
        dprobs = jnp.einsum('snhd,knd->nhsk', grad, valset)
        dscores = (probs * (dprobs - delta[..., None])).astype(jnp.bfloat16).astype(jnp.float32)
        dquery = (jnp.einsum('nhsk,knd->snhd', dscores, keyset) * scale).astype(jnp.bfloat16)
        query_parts.append(dquery.reshape(TOK_DEV, HEADS * HD))
        dkey = jnp.einsum('nhsk,snhd->knd', dscores, query) * scale
        dval = jnp.einsum('nhsk,snhd->knd', probs_b, grad)
        key_parts.append(dkey[nsum:].astype(jnp.bfloat16).reshape(TOK_DEV, KVH * HD))
        value_parts.append(dval[nsum:].astype(jnp.bfloat16).reshape(TOK_DEV, KVH * HD))
        acc_keys = acc_keys + dkey[:nsum]
        acc_vals = acc_vals + dval[:nsum]
    sum_key_grad = acc_keys.reshape(nsum, KVH * HD).astype(jnp.bfloat16)
    sum_value_grad = acc_vals.reshape(nsum, KVH * HD).astype(jnp.bfloat16)
    dims = (((1,), (1,)), ((), ()))
    state = lax.dot_general(sum_key_grad, w_key, dims, preferred_element_type=jnp.float32)
    state = state + lax.dot_general(sum_value_grad, w_value, dims, preferred_element_type=jnp.float32)
    state_grad = (state + summary_grad.astype(jnp.float32)).astype(jnp.bfloat16)
    return (jnp.concatenate(query_parts, 0), jnp.concatenate(key_parts, 0), jnp.concatenate(value_parts, 0), state_grad)
```

```python
import functools
import math

import jax
import jax.numpy as jnp
from jax import lax
from jax.experimental import pallas as pl
from jax.experimental.pallas import tpu as pltpu
from jax.sharding import PartitionSpec as P

HD = 128
HEADS = 8
TOK = 256
M = 50
MAIN = 48
REM = M - MAIN
TILE = 16
NX, NZ = 4, 8
NTP = 8
GROUP = NZ * M
REM0 = NZ * MAIN
BLOCK = MAIN + TILE
D = 8192
W2 = 2 * HD
SCALE = HD ** (-0.5)
SCALE2 = SCALE * math.log2(math.e)
NEG = -1e30
F32 = jnp.float32
BF16 = jnp.bfloat16
MESH = pl.DeviceIdType.MESH
LAST = (((1,), (1,)), ((), ()))
PLAIN = (((1,), (0,)), ((), ()))
WCHUNK = 4


def dot(a, b, dims=PLAIN):
    return lax.dot_general(a, b, dims, preferred_element_type=F32)


def seg_place():
    seg = lax.axis_index("seg")
    return seg // NZ, lax.rem(seg, NZ)


def z_peer(x, z, d):
    other = lax.rem(z + d, NZ)
    return other, x * NZ + other


def x_peer(x, z, d):
    other = lax.rem(x + d, NX)
    return other, other * NZ + z


def greet(peers):
    barrier = pltpu.get_barrier_semaphore()
    for peer in peers:
        pl.semaphore_signal(barrier, inc=1, device_id=peer, device_id_type=MESH)
    return barrier, len(peers)


def load_weights(wk_hbm, wv_hbm, w, sems):
    rows = D // WCHUNK
    copies = []
    for c in range(WCHUNK):
        part = pl.ds(c * rows, rows)
        for i, src in enumerate((wk_hbm, wv_hbm)):
            copy = pltpu.make_async_copy(
                src.at[part], w.at[part, pl.ds(i * HD, HD)], sems.at[c, i]
            )
            copy.start()
            copies.append(copy)
    return copies


def gather_kernel(
    st_hbm, wk_hbm, wv_hbm, out_ref, st, w, mine, zrecv, grp, wsem, stsem, zs, zr, xs, xr
):
    x, z = seg_place()
    peers = [{"seg": z_peer(x, z, d)[1]} for d in range(1, NZ)]
    peers += [{"seg": x_peer(x, z, d)[1]} for d in range(1, NX)]
    barrier, count = greet(peers)
    stcopy = pltpu.make_async_copy(st_hbm, st, stsem)
    stcopy.start()
    wcopies = load_weights(wk_hbm, wv_hbm, w, wsem)
    stcopy.wait()
    rows = D // WCHUNK
    total = jnp.zeros((M, W2), F32)
    for c in range(WCHUNK):
        wcopies[2 * c].wait()
        wcopies[2 * c + 1].wait()
        part = pl.ds(c * rows, rows)
        total = total + dot(st[:, part], w[part, :])
    mine[0:MAIN, :] = total[0:MAIN].astype(BF16)
    row = lax.broadcasted_iota(jnp.int32, (TILE, W2), 0)
    rem = jnp.where(
        row == REM * z,
        total[MAIN : MAIN + 1],
        jnp.where(row == REM * z + 1, total[MAIN + 1 : MAIN + 2], 0.0),
    )
    mine[MAIN:BLOCK, :] = rem.astype(BF16)
    pl.semaphore_wait(barrier, count)

    def zcopy(d, peer, slot):
        return pltpu.make_async_remote_copy(
            src_ref=mine,
            dst_ref=zrecv.at[slot],
            send_sem=zs.at[d - 1],
            recv_sem=zr.at[d - 1],
            device_id={"seg": peer},
            device_id_type=MESH,
        )

    sends = []
    for d in range(1, NZ):
        copy = zcopy(d, z_peer(x, z, d)[1], z)
        copy.start()
        sends.append(copy)
    grp[x, pl.ds(pl.multiple_of(z * MAIN, TILE), MAIN), :] = mine[0:MAIN, :]
    shared = mine[MAIN:BLOCK, :].astype(F32)
    for d in range(1, NZ):
        other, peer = z_peer(x, z, NZ - d)
        zcopy(d, peer, other).wait_recv()
        grp[x, pl.ds(pl.multiple_of(other * MAIN, TILE), MAIN), :] = zrecv[other, 0:MAIN, :]
        shared = shared + zrecv[other, MAIN:BLOCK, :].astype(F32)
    grp[x, REM0:GROUP, :] = shared.astype(BF16)

    def xcopy(d, peer, g):
        return pltpu.make_async_remote_copy(
            src_ref=grp.at[g],
            dst_ref=grp.at[g],
            send_sem=xs.at[d - 1],
            recv_sem=xr.at[d - 1],
            device_id={"seg": peer},
            device_id_type=MESH,
        )

    for d in range(1, NX):

        @pl.when(x + d < NX)
        def _(d=d):
            xcopy(d, x_peer(x, z, d)[1], x).start()

    for copy in sends:
        copy.wait_send()
    out_ref[x] = grp[x]
    for d in range(1, NX):

        @pl.when(x >= d)
        def _(d=d):
            other, peer = x_peer(x, z, NX - d)
            xcopy(d, peer, other).wait_recv()
            out_ref[other] = grp[other]

    for d in range(1, NX):

        @pl.when(x + d < NX)
        def _(d=d):
            xcopy(d, x_peer(x, z, d)[1], x).wait_send()


def gather(states, w_key, w_value):
    return pl.pallas_call(
        gather_kernel,
        name="gather",
        out_shape=jax.ShapeDtypeStruct((NX, GROUP, W2), BF16),
        in_specs=[pl.BlockSpec(memory_space=pl.ANY)] * 3,
        out_specs=pl.BlockSpec(memory_space=pltpu.VMEM),
        scratch_shapes=[
            pltpu.VMEM((M, D), BF16),
            pltpu.VMEM((D, W2), BF16),
            pltpu.VMEM((BLOCK, W2), BF16),
            pltpu.VMEM((NZ, BLOCK, W2), BF16),
            pltpu.VMEM((NX, GROUP, W2), BF16),
            pltpu.SemaphoreType.DMA((WCHUNK, 2)),
            pltpu.SemaphoreType.DMA,
            pltpu.SemaphoreType.DMA((NZ - 1,)),
            pltpu.SemaphoreType.DMA((NZ - 1,)),
            pltpu.SemaphoreType.DMA((NX - 1,)),
            pltpu.SemaphoreType.DMA((NX - 1,)),
        ],
        compiler_params=pltpu.CompilerParams(
            collective_id=0, has_side_effects=True, vmem_limit_bytes=24 << 20
        ),
    )(states, w_key, w_value)


def attention_kernel(
    q_ref, g_ref, ko_ref, vo_ref, grp_ref, dq_ref, dko_ref, dvo_ref, part_ref,
    s_own, p_own, s_all, p_all, m_ref, l_ref, d_ref, dqt, kt_own, kt, dk_acc, dv_acc,
):
    x, z = seg_place()
    groups = x + jnp.minimum(z, 1)

    def head(ref, h):
        return ref[:, pl.ds(pl.multiple_of(h * HD, HD), HD)]

    def lanes(h):
        return pl.ds(pl.multiple_of(h * TOK, TOK), TOK)

    def sweep_one(keys, vals, s_ref, p_ref, mask, first):
        def step(h, carry):
            s = dot(keys, head(q_ref, h), LAST)
            if mask is not None:
                s = jnp.where(mask, s, NEG)
            s_ref[:, lanes(h)] = s
            top = jnp.max(s, axis=0, keepdims=True)
            p = dot(vals, head(g_ref, h), LAST)
            p_ref[:, lanes(h)] = p
            if not first:
                old = m_ref[:, lanes(h)]
                top = jnp.maximum(old, top)
            e = jnp.exp2(s * SCALE2 - top * SCALE2)
            total = jnp.sum(e, axis=0, keepdims=True)
            inner = jnp.sum(e * p, axis=0, keepdims=True)
            if not first:
                fade = jnp.exp2((old - top) * SCALE2)
                total = total + l_ref[:, lanes(h)] * fade
                inner = inner + d_ref[:, lanes(h)] * fade
            m_ref[:, lanes(h)] = top
            l_ref[:, lanes(h)] = total
            d_ref[:, lanes(h)] = inner
            return carry

        lax.fori_loop(0, HEADS, step, 0)

    def sweep_two(s_ref, p_ref, keys_t, first):
        dk_acc_n = dk_acc.at[0 : s_ref.shape[0]]
        dv_acc_n = dv_acc.at[0 : s_ref.shape[0]]
        dk_acc_n[...] = jnp.zeros_like(dk_acc_n)
        dv_acc_n[...] = jnp.zeros_like(dv_acc_n)

        def step(h, carry):
            probs = jnp.exp2(s_ref[:, lanes(h)] * SCALE2 - m_ref[:, lanes(h)])
            ds = (probs * (p_ref[:, lanes(h)] - d_ref[:, lanes(h)])).astype(BF16)
            dv_acc_n[...] += dot(probs.astype(BF16), head(g_ref, h))
            dk_acc_n[...] += dot(ds, head(q_ref, h))
            update = dot(keys_t[...], ds)
            if first:
                dqt[:, lanes(h)] = update
            else:
                dqt[:, lanes(h)] += update
            return carry

        lax.fori_loop(0, HEADS, step, 0)
        return dk_acc_n[...] * SCALE, dv_acc_n[...]

    tri = lax.broadcasted_iota(jnp.int32, (TOK, TOK), 0) <= lax.broadcasted_iota(
        jnp.int32, (TOK, TOK), 1
    )
    kt_own[...] = ko_ref[...].astype(F32).T.astype(BF16)
    sweep_one(ko_ref[...], vo_ref[...], s_own, p_own, tri, True)

    def full_group(g, carry):
        sweep_one(
            grp_ref[g, :, 0:HD], grp_ref[g, :, HD:W2], s_all.at[g], p_all.at[g], None, False
        )
        return carry

    lax.fori_loop(0, x, full_group, 0)

    @pl.when(z > 0)
    def _():
        r = lax.broadcasted_iota(jnp.int32, (GROUP, TOK), 0)
        mask = (r < MAIN * z) | ((r >= REM0) & (r < REM0 + REM * z))
        sweep_one(
            grp_ref[x, :, 0:HD], grp_ref[x, :, HD:W2], s_all.at[x], p_all.at[x], mask, False
        )

    d_ref[...] = d_ref[...] / l_ref[...]
    m_ref[...] = m_ref[...] * SCALE2 + jnp.log2(l_ref[...])

    dk, dv = sweep_two(s_own, p_own, kt_own, True)
    dko_ref[...] = dk.astype(BF16)
    dvo_ref[...] = dv.astype(BF16)
    part_ref[x] = jnp.zeros((GROUP, W2), BF16)

    def back_group(g, carry):
        kt[...] = grp_ref[g, :, 0:HD].astype(F32).T.astype(BF16)
        dk, dv = sweep_two(s_all.at[g], p_all.at[g], kt, False)
        part_ref[g, :, 0:HD] = dk.astype(BF16)
        part_ref[g, :, HD:W2] = dv.astype(BF16)
        return carry

    lax.fori_loop(0, groups, back_group, 0)
    for h in range(HEADS):
        dq_ref[:, h * HD : (h + 1) * HD] = (
            (dqt[:, h * TOK : (h + 1) * TOK] * SCALE).T.astype(BF16)
        )


def attention(queries, out_grad, keys_own, values_own, grp):
    vmem = pl.BlockSpec(memory_space=pltpu.VMEM)
    rows = HEADS * TOK
    return pl.pallas_call(
        attention_kernel,
        name="attention",
        out_shape=(
            jax.ShapeDtypeStruct((TOK, HEADS * HD), BF16),
            jax.ShapeDtypeStruct((TOK, HD), BF16),
            jax.ShapeDtypeStruct((TOK, HD), BF16),
            jax.ShapeDtypeStruct((NX, GROUP, W2), BF16),
        ),
        in_specs=[vmem] * 5,
        out_specs=(vmem,) * 4,
        scratch_shapes=[
            pltpu.VMEM((TOK, rows), F32),
            pltpu.VMEM((TOK, rows), F32),
            pltpu.VMEM((NX, GROUP, rows), F32),
            pltpu.VMEM((NX, GROUP, rows), F32),
            pltpu.VMEM((1, rows), F32),
            pltpu.VMEM((1, rows), F32),
            pltpu.VMEM((1, rows), F32),
            pltpu.VMEM((HD, rows), F32),
            pltpu.VMEM((HD, TOK), BF16),
            pltpu.VMEM((HD, GROUP), BF16),
            pltpu.VMEM((GROUP, HD), F32),
            pltpu.VMEM((GROUP, HD), F32),
        ],
        compiler_params=pltpu.CompilerParams(vmem_limit_bytes=56 << 20),
    )(queries, out_grad, keys_own, values_own, grp)


def scatter_kernel(
    part_ref, wk_hbm, wv_hbm, sg_ref, out_ref,
    w, xrecv, zsend, zrecv, em, tsend, trecv, wsem, xs, xr, zs, zr, ts, tr,
):
    x, z = seg_place()
    tp = lax.axis_index("tp")
    peers = [{"seg": z_peer(x, z, d)[1]} for d in range(1, NZ)]
    peers += [{"seg": x_peer(x, z, d)[1]} for d in range(1, NX)]
    peers += [{"tp": lax.rem(tp + d, NTP)} for d in range(1, NTP)]
    barrier, count = greet(peers)
    wcopies = load_weights(wk_hbm, wv_hbm, w, wsem)
    pl.semaphore_wait(barrier, count)

    def xcopy(d, peer, g, slot):
        return pltpu.make_async_remote_copy(
            src_ref=part_ref.at[g],
            dst_ref=xrecv.at[slot],
            send_sem=xs.at[d - 1],
            recv_sem=xr.at[d - 1],
            device_id={"seg": peer},
            device_id_type=MESH,
        )

    for d in range(1, NX):

        @pl.when(x >= d)
        def _(d=d):
            other, peer = x_peer(x, z, NX - d)
            xcopy(d, peer, other, d - 1).start()

    xrecv[NX - 1] = part_ref[x]
    for d in range(1, NX):

        @pl.when(x + d < NX)
        def _(d=d):
            other, peer = x_peer(x, z, d)
            xcopy(d, peer, other, d - 1).wait_recv()
            xrecv[NX - 1] = (xrecv[NX - 1].astype(F32) + xrecv[d - 1].astype(F32)).astype(BF16)

    for i in range(NZ):
        zsend[i, 0:MAIN, :] = xrecv[NX - 1, i * MAIN : (i + 1) * MAIN, :]
        zsend[i, MAIN:BLOCK, :] = xrecv[NX - 1, REM0:GROUP, :]

    def zcopy(d, other, peer):
        return pltpu.make_async_remote_copy(
            src_ref=zsend.at[other],
            dst_ref=zrecv.at[d - 1],
            send_sem=zs.at[d - 1],
            recv_sem=zr.at[d - 1],
            device_id={"seg": peer},
            device_id_type=MESH,
        )

    for d in range(1, NZ):
        zcopy(d, *z_peer(x, z, d)).start()
    total = zsend[z].astype(F32)
    for d in range(1, NZ):
        zcopy(d, *z_peer(x, z, NZ - d)).wait_recv()
        total = total + zrecv[d - 1].astype(F32)
    row = lax.broadcasted_iota(jnp.int32, (TILE, W2), 0)
    rem = total[MAIN:BLOCK]
    one = jnp.sum(jnp.where(row == REM * z, rem, 0.0), axis=0, keepdims=True)
    two = jnp.sum(jnp.where(row == REM * z + 1, rem, 0.0), axis=0, keepdims=True)
    em[0:MAIN, :] = total[0:MAIN].astype(BF16)
    em[MAIN:BLOCK, :] = jnp.where(row == 0, one, jnp.where(row == 1, two, 0.0)).astype(BF16)
    for copy in wcopies:
        copy.wait()
    cols = D // NTP

    def state(target):
        part = pl.ds(pl.multiple_of(target * cols, cols), cols)
        return dot(em[...], w[part, :], LAST)[0:M]

    def tcopy(d, target):
        return pltpu.make_async_remote_copy(
            src_ref=tsend.at[d - 1],
            dst_ref=trecv.at[d - 1],
            send_sem=ts.at[d - 1],
            recv_sem=tr.at[d - 1],
            device_id={"tp": target},
            device_id_type=MESH,
        )

    def send_state(d):
        target = lax.rem(tp + d, NTP)
        tsend[d - 1] = state(target).astype(BF16)
        tcopy(d, target).start()

    for d in range(1, NTP):
        send_state(d)
    out = state(tp) + sg_ref[...].astype(F32)
    for d in range(1, NTP):
        tcopy(d, lax.rem(tp + NTP - d, NTP)).wait_recv()
        out = out + trecv[d - 1].astype(F32)
    out_ref[...] = out.astype(BF16)
    for d in range(1, NX):

        @pl.when(x >= d)
        def _(d=d):
            other, peer = x_peer(x, z, NX - d)
            xcopy(d, peer, other, d - 1).wait_send()

    for d in range(1, NZ):
        zcopy(d, *z_peer(x, z, d)).wait_send()
    for d in range(1, NTP):
        tcopy(d, lax.rem(tp + d, NTP)).wait_send()


def scatter(part, w_key, w_value, summary_grad):
    vmem = pl.BlockSpec(memory_space=pltpu.VMEM)
    anywhere = pl.BlockSpec(memory_space=pl.ANY)
    cols = D // NTP
    return pl.pallas_call(
        scatter_kernel,
        name="scatter",
        out_shape=jax.ShapeDtypeStruct((M, cols), BF16),
        in_specs=[vmem, anywhere, anywhere, vmem],
        out_specs=vmem,
        scratch_shapes=[
            pltpu.VMEM((D, W2), BF16),
            pltpu.VMEM((NX, GROUP, W2), BF16),
            pltpu.VMEM((NZ, BLOCK, W2), BF16),
            pltpu.VMEM((NZ - 1, BLOCK, W2), BF16),
            pltpu.VMEM((BLOCK, W2), BF16),
            pltpu.VMEM((NTP - 1, M, cols), BF16),
            pltpu.VMEM((NTP - 1, M, cols), BF16),
            pltpu.SemaphoreType.DMA((WCHUNK, 2)),
            pltpu.SemaphoreType.DMA((NX - 1,)),
            pltpu.SemaphoreType.DMA((NX - 1,)),
            pltpu.SemaphoreType.DMA((NZ - 1,)),
            pltpu.SemaphoreType.DMA((NZ - 1,)),
            pltpu.SemaphoreType.DMA((NTP - 1,)),
            pltpu.SemaphoreType.DMA((NTP - 1,)),
        ],
        compiler_params=pltpu.CompilerParams(
            collective_id=1, has_side_effects=True, vmem_limit_bytes=24 << 20
        ),
    )(part, w_key, w_value, summary_grad)


def per_device(
    queries, keys_own, values_own, out_grad, summary_states, w_key, w_value, summary_grad
):
    grp = gather(summary_states, w_key, w_value)
    query_grad, key_grad, value_grad, part = attention(
        queries, out_grad, keys_own, values_own, grp
    )
    state_grad = scatter(part, w_key, w_value, summary_grad)
    return (query_grad, key_grad, value_grad, state_grad)


def solution(mesh):
    placed = (
        P("seg", "tp"),
        P("seg", "tp"),
        P("seg", "tp"),
        P("seg", "tp"),
        P("seg", None),
        P(None, "tp"),
        P(None, "tp"),
        P("seg", "tp"),
    )
    return jax.shard_map(
        per_device,
        mesh=mesh,
        in_specs=placed,
        out_specs=(P("seg", "tp"), P("seg", "tp"), P("seg", "tp"), P("seg", "tp")),
        check_vma=False,
    )
```

```python
import math

import jax
import jax.numpy as jnp
from jax import lax
from jax.experimental import pallas as pl
from jax.experimental.pallas import tpu as pltpu
from jax.sharding import PartitionSpec as P

HD = 128
HEADS = 8
TOK = 256
M = 50
MAIN = 48
REM = M - MAIN
TILE = 16
NX, NZ = 4, 8
NTP = 8
GROUP = NZ * M
REM0 = NZ * MAIN
BLOCK = MAIN + TILE
D = 8192
W2 = 2 * HD
SCALE = HD ** (-0.5)
SCALE2 = SCALE * math.log2(math.e)
NEG = -1e30
F32 = jnp.float32
BF16 = jnp.bfloat16
MESH = pl.DeviceIdType.MESH
LAST = (((1,), (1,)), ((), ()))
PLAIN = (((1,), (0,)), ((), ()))
WCHUNK = 4


def dot(a, b, dims=PLAIN):
    return lax.dot_general(a, b, dims, preferred_element_type=F32)


def seg_place():
    seg = lax.axis_index("seg")
    return seg // NZ, lax.rem(seg, NZ)


def z_peer(x, z, d):
    other = lax.rem(z + d, NZ)
    return other, x * NZ + other


def x_peer(x, z, d):
    other = lax.rem(x + d, NX)
    return other, other * NZ + z


def greet(peers):
    barrier = pltpu.get_barrier_semaphore()
    for peer in peers:
        pl.semaphore_signal(barrier, inc=1, device_id=peer, device_id_type=MESH)
    return barrier, len(peers)


def load_weights(wk_hbm, wv_hbm, w, sems):
    rows = D // WCHUNK
    copies = []
    for c in range(WCHUNK):
        part = pl.ds(c * rows, rows)
        for i, src in enumerate((wk_hbm, wv_hbm)):
            copy = pltpu.make_async_copy(
                src.at[part], w.at[part, pl.ds(i * HD, HD)], sems.at[c, i]
            )
            copy.start()
            copies.append(copy)
    return copies


def layer_kernel(
    q_hbm, g_hbm, ko_hbm, vo_hbm, st_hbm, wk_hbm, wv_hbm, sg_hbm,
    dq_hbm, dko_hbm, dvo_hbm, out_ref,
    q_ref, g_ref, ko_ref, vo_ref, st, w, sg_ref,
    mine, zrecv, grp, s_own, p_own, s_all, p_all, m_ref, l_ref, d_ref, dqt, kt_own, kt,
    dk_acc, dv_acc, part, xback, acc, zsend, zback, em, tsend, trecv, dq_ref, dko_ref, dvo_ref,
    wsem, insem, outsem, zs, zr, xs, xr, xbs, xbr, zbs, zbr, ts, tr,
):
    x, z = seg_place()
    tp = lax.axis_index("tp")
    peers = [{"seg": z_peer(x, z, d)[1]} for d in range(1, NZ)]
    peers += [{"seg": x_peer(x, z, d)[1]} for d in range(1, NX)]
    peers += [{"tp": lax.rem(tp + d, NTP)} for d in range(1, NTP)]
    barrier, count = greet(peers)

    loads = []
    for i, (src, dst) in enumerate(
        (
            (st_hbm, st),
            (q_hbm, q_ref),
            (ko_hbm, ko_ref),
            (g_hbm, g_ref),
            (vo_hbm, vo_ref),
            (sg_hbm, sg_ref),
        )
    ):
        loads.append(pltpu.make_async_copy(src, dst, insem.at[i]))
    loads[0].start()
    wcopies = load_weights(wk_hbm, wv_hbm, w, wsem)
    for copy in loads[1:]:
        copy.start()

    loads[0].wait()
    rows = D // WCHUNK
    total = jnp.zeros((M, W2), F32)
    for c in range(WCHUNK):
        wcopies[2 * c].wait()
        wcopies[2 * c + 1].wait()
        chunk = pl.ds(c * rows, rows)
        total = total + dot(st[:, chunk], w[chunk, :])
    mine[0:MAIN, :] = total[0:MAIN].astype(BF16)
    row = lax.broadcasted_iota(jnp.int32, (TILE, W2), 0)
    shared = jnp.where(
        row == REM * z,
        total[MAIN : MAIN + 1],
        jnp.where(row == REM * z + 1, total[MAIN + 1 : MAIN + 2], 0.0),
    )
    mine[MAIN:BLOCK, :] = shared.astype(BF16)
    pl.semaphore_wait(barrier, count)

    def zcopy(d, peer, slot):
        return pltpu.make_async_remote_copy(
            src_ref=mine,
            dst_ref=zrecv.at[slot],
            send_sem=zs.at[d - 1],
            recv_sem=zr.at[d - 1],
            device_id={"seg": peer},
            device_id_type=MESH,
        )

    for d in range(1, NZ):
        zcopy(d, z_peer(x, z, d)[1], z).start()

    def head(ref, h):
        return ref[:, h * HD : (h + 1) * HD]

    def lanes(h):
        return slice(h * TOK, (h + 1) * TOK)

    def sweep_one(keys, vals, s_ref, p_ref, mask, first):
        for h in range(HEADS):
            s = dot(keys, head(q_ref, h), LAST)
            if mask is not None:
                s = jnp.where(mask, s, NEG)
            s_ref[:, lanes(h)] = s
            top = jnp.max(s, axis=0, keepdims=True)
            p = dot(vals, head(g_ref, h), LAST)
            p_ref[:, lanes(h)] = p
            if not first:
                old = m_ref[:, lanes(h)]
                top = jnp.maximum(old, top)
            e = jnp.exp2(s * SCALE2 - top * SCALE2)
            total = jnp.sum(e, axis=0, keepdims=True)
            inner = jnp.sum(e * p, axis=0, keepdims=True)
            if not first:
                fade = jnp.exp2((old - top) * SCALE2)
                total = total + l_ref[:, lanes(h)] * fade
                inner = inner + d_ref[:, lanes(h)] * fade
            m_ref[:, lanes(h)] = top
            l_ref[:, lanes(h)] = total
            d_ref[:, lanes(h)] = inner

    def sweep_two(s_ref, p_ref, keys_t):
        count = s_ref.shape[0]
        dk = dk_acc.at[0:count]
        dv = dv_acc.at[0:count]
        for h in range(HEADS):
            probs = jnp.exp2(s_ref[:, lanes(h)] * SCALE2 - m_ref[:, lanes(h)])
            ds = (probs * (p_ref[:, lanes(h)] - d_ref[:, lanes(h)])).astype(BF16)
            dv_new = dot(probs.astype(BF16), head(g_ref, h))
            dk_new = dot(ds, head(q_ref, h))
            if h:
                dv[...] += dv_new
                dk[...] += dk_new
            else:
                dv[...] = dv_new
                dk[...] = dk_new
            dqt[:, lanes(h)] += dot(keys_t[...], ds)
        return dk[...] * SCALE, dv[...]

    tri = lax.broadcasted_iota(jnp.int32, (TOK, TOK), 0) <= lax.broadcasted_iota(
        jnp.int32, (TOK, TOK), 1
    )
    for copy in loads[1:]:
        copy.wait()
    kt_own[...] = ko_ref[...].astype(F32).T.astype(BF16)
    dqt[...] = jnp.zeros_like(dqt)
    sweep_one(ko_ref[...], vo_ref[...], s_own, p_own, tri, True)

    grp[x, pl.ds(pl.multiple_of(z * MAIN, TILE), MAIN), :] = mine[0:MAIN, :]
    shared = mine[MAIN:BLOCK, :].astype(F32)
    for d in range(1, NZ):
        other, peer = z_peer(x, z, NZ - d)
        zcopy(d, peer, other).wait_recv()
        grp[x, pl.ds(pl.multiple_of(other * MAIN, TILE), MAIN), :] = zrecv[other, 0:MAIN, :]
        shared = shared + zrecv[other, MAIN:BLOCK, :].astype(F32)
    grp[x, REM0:GROUP, :] = shared.astype(BF16)

    def xcopy(d, g):
        other = lax.rem(x + d + NX, NX)
        return pltpu.make_async_remote_copy(
            src_ref=grp.at[g],
            dst_ref=grp.at[g],
            send_sem=xs.at[jnp.abs(d) - 1],
            recv_sem=xr.at[jnp.abs(d) - 1],
            device_id={"seg": other * NZ + z},
            device_id_type=MESH,
        )

    lax.fori_loop(1, NX - x, lambda d, c: (xcopy(d, x).start(), c)[1], 0)

    @pl.when(z > 0)
    def _():
        r = lax.broadcasted_iota(jnp.int32, (GROUP, TOK), 0)
        mask = (r < MAIN * z) | ((r >= REM0) & (r < REM0 + REM * z))
        sweep_one(grp[x, :, 0:HD], grp[x, :, HD:W2], s_all.at[x], p_all.at[x], mask, False)

    def full_group(d, carry):
        g = x - d
        xcopy(-d, g).wait_recv()
        sweep_one(grp[g, :, 0:HD], grp[g, :, HD:W2], s_all.at[g], p_all.at[g], None, False)
        return carry

    lax.fori_loop(1, x + 1, full_group, 0)
    d_ref[...] = d_ref[...] / l_ref[...]
    m_ref[...] = m_ref[...] * SCALE2 + jnp.log2(l_ref[...])

    def xback_copy(d, g):
        other = lax.rem(x + d + NX, NX)
        slot = jnp.abs(d) - 1
        return pltpu.make_async_remote_copy(
            src_ref=part.at[g],
            dst_ref=xback.at[slot],
            send_sem=xbs.at[slot],
            recv_sem=xbr.at[slot],
            device_id={"seg": other * NZ + z},
            device_id_type=MESH,
        )

    acc[...] = jnp.zeros_like(acc)

    def back_group(g, carry):
        kt[...] = grp[g, :, 0:HD].astype(F32).T.astype(BF16)
        dk, dv = sweep_two(s_all.at[g], p_all.at[g], kt)

        @pl.when(g < x)
        def _():
            part[g, :, 0:HD] = dk.astype(BF16)
            part[g, :, HD:W2] = dv.astype(BF16)
            xback_copy(g - x, g).start()

        @pl.when(g == x)
        def _():
            acc[:, 0:HD] = dk
            acc[:, HD:W2] = dv

        return carry

    lax.fori_loop(0, x + jnp.minimum(z, 1), back_group, 0)

    def add_group(d, carry):
        xback_copy(d, x).wait_recv()
        acc[...] += xback[d - 1].astype(F32)
        return carry

    lax.fori_loop(1, NX - x, add_group, 0)

    for i in range(NZ):
        zsend[i, 0:MAIN, :] = acc[i * MAIN : (i + 1) * MAIN, :].astype(BF16)
        zsend[i, MAIN:BLOCK, :] = acc[REM0:GROUP, :].astype(BF16)

    def zback_copy(d, other, peer):
        return pltpu.make_async_remote_copy(
            src_ref=zsend.at[other],
            dst_ref=zback.at[d - 1],
            send_sem=zbs.at[d - 1],
            recv_sem=zbr.at[d - 1],
            device_id={"seg": peer},
            device_id_type=MESH,
        )

    for d in range(1, NZ):
        zback_copy(d, *z_peer(x, z, d)).start()

    dk, dv = sweep_two(s_own, p_own, kt_own)
    dko_ref[...] = dk.astype(BF16)
    dvo_ref[...] = dv.astype(BF16)
    for h in range(HEADS):
        dq_ref[:, h * HD : (h + 1) * HD] = (dqt[:, lanes(h)] * SCALE).T.astype(BF16)
    stores = [
        pltpu.make_async_copy(src, dst, outsem.at[i])
        for i, (src, dst) in enumerate(((dq_ref, dq_hbm), (dko_ref, dko_hbm), (dvo_ref, dvo_hbm)))
    ]
    for copy in stores:
        copy.start()

    total = zsend[z].astype(F32)
    for d in range(1, NZ):
        zback_copy(d, *z_peer(x, z, NZ - d)).wait_recv()
        total = total + zback[d - 1].astype(F32)
    rem = total[MAIN:BLOCK]
    one = jnp.sum(jnp.where(row == REM * z, rem, 0.0), axis=0, keepdims=True)
    two = jnp.sum(jnp.where(row == REM * z + 1, rem, 0.0), axis=0, keepdims=True)
    em[0:MAIN, :] = total[0:MAIN].astype(BF16)
    em[MAIN:BLOCK, :] = jnp.where(row == 0, one, jnp.where(row == 1, two, 0.0)).astype(BF16)

    cols = D // NTP

    def state(target):
        chunk = pl.ds(pl.multiple_of(target * cols, cols), cols)
        return dot(em[...], w[chunk, :], LAST)[0:M]

    def tcopy(d, target):
        return pltpu.make_async_remote_copy(
            src_ref=tsend.at[d - 1],
            dst_ref=trecv.at[d - 1],
            send_sem=ts.at[d - 1],
            recv_sem=tr.at[d - 1],
            device_id={"tp": target},
            device_id_type=MESH,
        )

    for d in range(1, NTP):
        target = lax.rem(tp + d, NTP)
        tsend[d - 1] = state(target).astype(BF16)
        tcopy(d, target).start()
    out = state(tp) + sg_ref[...].astype(F32)
    for d in range(1, NTP):
        tcopy(d, lax.rem(tp + NTP - d, NTP)).wait_recv()
        out = out + trecv[d - 1].astype(F32)
    out_ref[...] = out.astype(BF16)

    for copy in stores:
        copy.wait()
    for d in range(1, NZ):
        other, peer = z_peer(x, z, d)
        zcopy(d, peer, z).wait_send()
        zback_copy(d, other, peer).wait_send()
    lax.fori_loop(1, NX - x, lambda d, c: (xcopy(d, x).wait_send(), c)[1], 0)
    lax.fori_loop(1, x + 1, lambda d, c: (xback_copy(-d, x - d).wait_send(), c)[1], 0)
    for d in range(1, NTP):
        tcopy(d, lax.rem(tp + d, NTP)).wait_send()


def per_device(
    queries, keys_own, values_own, out_grad, summary_states, w_key, w_value, summary_grad
):
    anywhere = pl.BlockSpec(memory_space=pl.ANY)
    rows = HEADS * TOK
    cols = D // NTP
    dma = pltpu.SemaphoreType.DMA
    return pl.pallas_call(
        layer_kernel,
        name="layer",
        out_shape=(
            jax.ShapeDtypeStruct((TOK, HEADS * HD), BF16),
            jax.ShapeDtypeStruct((TOK, HD), BF16),
            jax.ShapeDtypeStruct((TOK, HD), BF16),
            jax.ShapeDtypeStruct((M, cols), BF16),
        ),
        in_specs=[anywhere] * 8,
        out_specs=(anywhere,) * 3 + (pl.BlockSpec(memory_space=pltpu.VMEM),),
        scratch_shapes=[
            pltpu.VMEM((TOK, HEADS * HD), BF16),
            pltpu.VMEM((TOK, HEADS * HD), BF16),
            pltpu.VMEM((TOK, HD), BF16),
            pltpu.VMEM((TOK, HD), BF16),
            pltpu.VMEM((M, D), BF16),
            pltpu.VMEM((D, W2), BF16),
            pltpu.VMEM((M, cols), BF16),
            pltpu.VMEM((BLOCK, W2), BF16),
            pltpu.VMEM((NZ, BLOCK, W2), BF16),
            pltpu.VMEM((NX, GROUP, W2), BF16),
            pltpu.VMEM((TOK, rows), F32),
            pltpu.VMEM((TOK, rows), F32),
            pltpu.VMEM((NX, GROUP, rows), F32),
            pltpu.VMEM((NX, GROUP, rows), F32),
            pltpu.VMEM((1, rows), F32),
            pltpu.VMEM((1, rows), F32),
            pltpu.VMEM((1, rows), F32),
            pltpu.VMEM((HD, rows), F32),
            pltpu.VMEM((HD, TOK), BF16),
            pltpu.VMEM((HD, GROUP), BF16),
            pltpu.VMEM((GROUP, HD), F32),
            pltpu.VMEM((GROUP, HD), F32),
            pltpu.VMEM((NX, GROUP, W2), BF16),
            pltpu.VMEM((NX - 1, GROUP, W2), BF16),
            pltpu.VMEM((GROUP, W2), F32),
            pltpu.VMEM((NZ, BLOCK, W2), BF16),
            pltpu.VMEM((NZ - 1, BLOCK, W2), BF16),
            pltpu.VMEM((BLOCK, W2), BF16),
            pltpu.VMEM((NTP - 1, M, cols), BF16),
            pltpu.VMEM((NTP - 1, M, cols), BF16),
            pltpu.VMEM((TOK, HEADS * HD), BF16),
            pltpu.VMEM((TOK, HD), BF16),
            pltpu.VMEM((TOK, HD), BF16),
            dma((WCHUNK, 2)),
            dma((6,)),
            dma((3,)),
            dma((NZ - 1,)),
            dma((NZ - 1,)),
            dma((NX - 1,)),
            dma((NX - 1,)),
            dma((NX - 1,)),
            dma((NX - 1,)),
            dma((NZ - 1,)),
            dma((NZ - 1,)),
            dma((NTP - 1,)),
            dma((NTP - 1,)),
        ],
        compiler_params=pltpu.CompilerParams(
            collective_id=0, has_side_effects=True, vmem_limit_bytes=58 << 20
        ),
    )(
        queries, out_grad, keys_own, values_own, summary_states, w_key, w_value, summary_grad
    )


def solution(mesh):
    placed = (
        P("seg", "tp"),
        P("seg", "tp"),
        P("seg", "tp"),
        P("seg", "tp"),
        P("seg", None),
        P(None, "tp"),
        P(None, "tp"),
        P("seg", "tp"),
    )
    return jax.shard_map(
        per_device,
        mesh=mesh,
        in_specs=placed,
        out_specs=(P("seg", "tp"), P("seg", "tp"), P("seg", "tp"), P("seg", "tp")),
        check_vma=False,
    )
```

```python
import math

import jax
import jax.numpy as jnp
from jax import lax
from jax.experimental import pallas as pl
from jax.experimental.pallas import tpu as pltpu
from jax.sharding import PartitionSpec as P

HD = 128
HEADS = 8
TOK = 256
M = 50
MAIN = 48
REM = M - MAIN
TILE = 16
NX, NZ = 4, 8
NTP = 8
NY = NTP // 2
GROUP = NZ * M
REM0 = NZ * MAIN
BLOCK = MAIN + TILE
D = 8192
W2 = 2 * HD
SCALE = HD ** (-0.5)
SCALE2 = SCALE * math.log2(math.e)
NEG = -1e30
F32 = jnp.float32
BF16 = jnp.bfloat16
MESH = pl.DeviceIdType.MESH
LAST = (((1,), (1,)), ((), ()))
PLAIN = (((1,), (0,)), ((), ()))
WCHUNK = 4


def dot(a, b, dims=PLAIN):
    return lax.dot_general(a, b, dims, preferred_element_type=F32)


def seg_place():
    seg = lax.axis_index("seg")
    return seg // NZ, lax.rem(seg, NZ)


def z_peer(x, z, d):
    other = lax.rem(z + d, NZ)
    return other, x * NZ + other


def x_peer(x, z, d):
    other = lax.rem(x + d, NX)
    return other, other * NZ + z


def greet(peers):
    barrier = pltpu.get_barrier_semaphore()
    for peer in peers:
        pl.semaphore_signal(barrier, inc=1, device_id=peer, device_id_type=MESH)
    return barrier, len(peers)


def load_weights(wk_hbm, wv_hbm, w, sems):
    rows = D // WCHUNK
    copies = []
    for c in range(WCHUNK):
        part = pl.ds(c * rows, rows)
        for i, src in enumerate((wk_hbm, wv_hbm)):
            copy = pltpu.make_async_copy(
                src.at[part], w.at[part, pl.ds(i * HD, HD)], sems.at[c, i]
            )
            copy.start()
            copies.append(copy)
    return copies


def layer_kernel(
    q_hbm, g_hbm, ko_hbm, vo_hbm, st_hbm, wk_hbm, wv_hbm, sg_hbm,
    dq_hbm, dko_hbm, dvo_hbm, out_ref,
    q_ref, g_ref, ko_ref, vo_ref, st, w, sg_ref,
    mine, zrecv, grp, s_own, p_own, s_all, p_all, m_ref, l_ref, d_ref, dqt, kt_own, kt,
    dk_acc, dv_acc, part, xback, acc, zsend, zback, em, etwin, wtwin, state, tsend, trecv, dq_ref, dko_ref, dvo_ref,
    wsem, insem, outsem, zs, zr, xs, xr, xbs, xbr, zbs, zbr, ts, tr, ws, wr, es, er,
):
    x, z = seg_place()
    tp = lax.axis_index("tp")
    peers = [{"seg": z_peer(x, z, d)[1]} for d in range(1, NZ)]
    peers += [{"seg": x_peer(x, z, d)[1]} for d in range(1, NX)]
    core = lax.rem(tp, 2)
    y = tp // 2
    twin = tp + 1 - 2 * core

    def y_peer(d):
        other = lax.rem(y + d, NY)
        return other, 2 * other + core

    peers += [{"tp": twin}] + [{"tp": y_peer(d)[1]} for d in range(1, NY)]
    last = x == NX - 1
    barrier, count = greet(peers)

    loads = []
    for i, (src, dst) in enumerate(
        (
            (st_hbm, st),
            (q_hbm, q_ref),
            (ko_hbm, ko_ref),
            (g_hbm, g_ref),
            (vo_hbm, vo_ref),
            (sg_hbm, sg_ref),
        )
    ):
        loads.append(pltpu.make_async_copy(src, dst, insem.at[i]))
    loads[0].start()
    wcopies = load_weights(wk_hbm, wv_hbm, w, wsem)
    for copy in loads[1:]:
        copy.start()

    loads[0].wait()
    rows = D // WCHUNK
    total = jnp.zeros((M, W2), F32)
    for c in range(WCHUNK):
        wcopies[2 * c].wait()
        wcopies[2 * c + 1].wait()
        chunk = pl.ds(c * rows, rows)
        total = total + dot(st[:, chunk], w[chunk, :])
    mine[0:MAIN, :] = total[0:MAIN].astype(BF16)
    row = lax.broadcasted_iota(jnp.int32, (TILE, W2), 0)
    shared = jnp.where(
        row == REM * z,
        total[MAIN : MAIN + 1],
        jnp.where(row == REM * z + 1, total[MAIN + 1 : MAIN + 2], 0.0),
    )
    mine[MAIN:BLOCK, :] = shared.astype(BF16)
    pl.semaphore_wait(barrier, count)

    def zcopy(d, peer, slot):
        return pltpu.make_async_remote_copy(
            src_ref=mine,
            dst_ref=zrecv.at[slot],
            send_sem=zs.at[d - 1],
            recv_sem=zr.at[d - 1],
            device_id={"seg": peer},
            device_id_type=MESH,
        )

    for d in range(1, NZ):
        other, peer = z_peer(x, z, d)

        @pl.when(jnp.logical_not(last) | (other > z))
        def _(d=d, peer=peer):
            zcopy(d, peer, z).start()

    cols = D // NTP

    def wcopy(i):
        rows_out = pl.ds(pl.multiple_of((2 * i + 1 - core) * cols, cols), cols)
        return pltpu.make_async_remote_copy(
            src_ref=w.at[rows_out],
            dst_ref=wtwin.at[i],
            send_sem=ws.at[i],
            recv_sem=wr.at[i],
            device_id={"tp": twin},
            device_id_type=MESH,
        )

    for i in range(NY):
        wcopy(i).start()

    def head(ref, h):
        return ref[:, h * HD : (h + 1) * HD]

    def lanes(h):
        return slice(h * TOK, (h + 1) * TOK)

    def sweep_one(keys, vals, s_ref, p_ref, mask, first):
        for h in range(HEADS):
            s = dot(keys, head(q_ref, h), LAST) * SCALE2
            if mask is not None:
                s = jnp.where(mask, s, NEG)
            s_ref[:, lanes(h)] = s
            top = jnp.max(s, axis=0, keepdims=True)
            p = dot(vals, head(g_ref, h), LAST)
            p_ref[:, lanes(h)] = p
            if not first:
                old = m_ref[:, lanes(h)]
                top = jnp.maximum(old, top)
            e = jnp.exp2(s - top)
            total = jnp.sum(e, axis=0, keepdims=True)
            inner = jnp.sum(e * p, axis=0, keepdims=True)
            if not first:
                fade = jnp.exp2(old - top)
                total = total + l_ref[:, lanes(h)] * fade
                inner = inner + d_ref[:, lanes(h)] * fade
            m_ref[:, lanes(h)] = top
            l_ref[:, lanes(h)] = total
            d_ref[:, lanes(h)] = inner

    def sweep_two(s_ref, p_ref, keys_t):
        count = s_ref.shape[0]
        dk = dk_acc.at[0:count]
        dv = dv_acc.at[0:count]
        for h in range(HEADS):
            probs = jnp.exp2(s_ref[:, lanes(h)] - m_ref[:, lanes(h)])
            ds = (probs * (p_ref[:, lanes(h)] - d_ref[:, lanes(h)])).astype(BF16)
            dv_new = dot(probs.astype(BF16), head(g_ref, h))
            dk_new = dot(ds, head(q_ref, h))
            if h:
                dv[...] += dv_new
                dk[...] += dk_new
            else:
                dv[...] = dv_new
                dk[...] = dk_new
            dqt[:, lanes(h)] += dot(keys_t[...], ds)
        return dk[...] * SCALE, dv[...]

    tri = lax.broadcasted_iota(jnp.int32, (TOK, TOK), 0) <= lax.broadcasted_iota(
        jnp.int32, (TOK, TOK), 1
    )
    for copy in loads[1:]:
        copy.wait()
    kt_own[...] = ko_ref[...].astype(F32).T.astype(BF16)
    dqt[...] = jnp.zeros_like(dqt)
    sweep_one(ko_ref[...], vo_ref[...], s_own, p_own, tri, True)

    def assemble():
        grp[x, pl.ds(pl.multiple_of(z * MAIN, TILE), MAIN), :] = mine[0:MAIN, :]
        acc[0:TILE, :] = mine[MAIN:BLOCK, :].astype(F32)
        for d in range(1, NZ):
            other, peer = z_peer(x, z, NZ - d)
            sent = jnp.logical_not(last) | (other < z)
            place = pl.ds(pl.multiple_of(other * MAIN, TILE), MAIN)

            @pl.when(sent)
            def _(d=d, other=other, peer=peer, place=place):
                zcopy(d, peer, other).wait_recv()
                grp[x, place, :] = zrecv[other, 0:MAIN, :]
                acc[0:TILE, :] += zrecv[other, MAIN:BLOCK, :].astype(F32)

            @pl.when(jnp.logical_not(sent))
            def _(place=place):
                grp[x, place, :] = jnp.zeros((MAIN, W2), BF16)

        grp[x, REM0:GROUP, :] = acc[0:TILE, :].astype(BF16)

    def xcopy(d, g):
        other = lax.rem(x + d + NX, NX)
        return pltpu.make_async_remote_copy(
            src_ref=grp.at[g],
            dst_ref=grp.at[g],
            send_sem=xs.at[jnp.abs(d) - 1],
            recv_sem=xr.at[jnp.abs(d) - 1],
            device_id={"seg": other * NZ + z},
            device_id_type=MESH,
        )

    @pl.when(jnp.logical_not(last))
    def _():
        assemble()
        lax.fori_loop(1, NX - x, lambda d, c: (xcopy(d, x).start(), c)[1], 0)

    def full_group(d, carry):
        g = x - d
        xcopy(-d, g).wait_recv()
        sweep_one(grp[g, :, 0:HD], grp[g, :, HD:W2], s_all.at[g], p_all.at[g], None, False)
        return carry

    lax.fori_loop(1, x + 1, full_group, 0)

    @pl.when(last)
    def _():
        assemble()

    @pl.when(z > 0)
    def _():
        r = lax.broadcasted_iota(jnp.int32, (GROUP, TOK), 0)
        mask = (r < MAIN * z) | ((r >= REM0) & (r < REM0 + REM * z))
        sweep_one(grp[x, :, 0:HD], grp[x, :, HD:W2], s_all.at[x], p_all.at[x], mask, False)

    d_ref[...] = d_ref[...] / l_ref[...]
    m_ref[...] = m_ref[...] + jnp.log2(l_ref[...])

    def xback_copy(d, g):
        other = lax.rem(x + d + NX, NX)
        slot = jnp.abs(d) - 1
        return pltpu.make_async_remote_copy(
            src_ref=part.at[g],
            dst_ref=xback.at[slot],
            send_sem=xbs.at[slot],
            recv_sem=xbr.at[slot],
            device_id={"seg": other * NZ + z},
            device_id_type=MESH,
        )

    acc[...] = jnp.zeros_like(acc)

    def back_group(i, carry):
        g = jnp.where(i < x, lax.rem(i + 1, jnp.maximum(x, 1)), x)
        kt[...] = grp[g, :, 0:HD].astype(F32).T.astype(BF16)
        dk, dv = sweep_two(s_all.at[g], p_all.at[g], kt)

        @pl.when(g < x)
        def _():
            part[g, :, 0:HD] = dk.astype(BF16)
            part[g, :, HD:W2] = dv.astype(BF16)
            xback_copy(g - x, g).start()

        @pl.when(g == x)
        def _():
            acc[:, 0:HD] = dk
            acc[:, HD:W2] = dv

        return carry

    lax.fori_loop(0, x + jnp.minimum(z, 1), back_group, 0)

    def add_group(d, carry):
        xback_copy(d, x).wait_recv()
        acc[...] += xback[d - 1].astype(F32)
        return carry

    lax.fori_loop(1, NX - x, add_group, 0)

    for i in range(NZ):
        zsend[i, 0:MAIN, :] = acc[i * MAIN : (i + 1) * MAIN, :].astype(BF16)
        zsend[i, MAIN:BLOCK, :] = acc[REM0:GROUP, :].astype(BF16)

    def zback_copy(d, other, peer):
        return pltpu.make_async_remote_copy(
            src_ref=zsend.at[other],
            dst_ref=zback.at[d - 1],
            send_sem=zbs.at[d - 1],
            recv_sem=zbr.at[d - 1],
            device_id={"seg": peer},
            device_id_type=MESH,
        )

    for d in range(1, NZ):
        other, peer = z_peer(x, z, d)

        @pl.when(jnp.logical_not(last) | (other < z))
        def _(d=d, other=other, peer=peer):
            zback_copy(d, other, peer).start()

    dk, dv = sweep_two(s_own, p_own, kt_own)
    dko_ref[...] = dk.astype(BF16)
    dvo_ref[...] = dv.astype(BF16)
    for h in range(HEADS):
        dq_ref[:, h * HD : (h + 1) * HD] = (dqt[:, lanes(h)] * SCALE).T.astype(BF16)
    stores = [
        pltpu.make_async_copy(src, dst, outsem.at[i])
        for i, (src, dst) in enumerate(((dq_ref, dq_hbm), (dko_ref, dko_hbm), (dvo_ref, dvo_hbm)))
    ]
    for copy in stores:
        copy.start()

    mine_acc = acc.at[0:BLOCK]
    mine_acc[...] = zsend[z].astype(F32)
    for d in range(1, NZ):
        other, peer = z_peer(x, z, NZ - d)

        @pl.when(jnp.logical_not(last) | (other > z))
        def _(d=d, other=other, peer=peer):
            zback_copy(d, other, peer).wait_recv()
            mine_acc[...] += zback[d - 1].astype(F32)

    total = mine_acc[...]
    rem = total[MAIN:BLOCK]
    one = jnp.sum(jnp.where(row == REM * z, rem, 0.0), axis=0, keepdims=True)
    two = jnp.sum(jnp.where(row == REM * z + 1, rem, 0.0), axis=0, keepdims=True)
    em[0:MAIN, :] = total[0:MAIN].astype(BF16)
    em[MAIN:BLOCK, :] = jnp.where(row == 0, one, jnp.where(row == 1, two, 0.0)).astype(BF16)

    def ecopy():
        return pltpu.make_async_remote_copy(
            src_ref=em,
            dst_ref=etwin,
            send_sem=es,
            recv_sem=er,
            device_id={"tp": twin},
            device_id_type=MESH,
        )

    ecopy().start()
    order = (2, 1, 3, 0)
    for d in order:
        target = y_peer(d)[1]
        chunk = pl.ds(pl.multiple_of(target * cols, cols), cols)
        state[d] = dot(em[...], w[chunk, :], LAST)
    for i in range(NY):
        wcopy(i).wait_recv()
    ecopy().wait_recv()

    def tcopy(d, target):
        return pltpu.make_async_remote_copy(
            src_ref=tsend.at[d - 1],
            dst_ref=trecv.at[d - 1],
            send_sem=ts.at[d - 1],
            recv_sem=tr.at[d - 1],
            device_id={"tp": target},
            device_id_type=MESH,
        )

    for d in order:
        other, target = y_peer(d)
        both = (state[d] + dot(etwin[...], wtwin[other], LAST))[0:M]
        if d:
            tsend[d - 1] = both.astype(BF16)
            tcopy(d, target).start()
    out = both + sg_ref[...].astype(F32)
    for d in (1, 3, 2):
        tcopy(d, y_peer(NY - d)[1]).wait_recv()
        out = out + trecv[d - 1].astype(F32)
    out_ref[...] = out.astype(BF16)

    for copy in stores:
        copy.wait()
    for d in range(1, NZ):
        other, peer = z_peer(x, z, d)

        @pl.when(jnp.logical_not(last) | (other > z))
        def _(d=d, peer=peer):
            zcopy(d, peer, z).wait_send()

        @pl.when(jnp.logical_not(last) | (other < z))
        def _(d=d, other=other, peer=peer):
            zback_copy(d, other, peer).wait_send()

    lax.fori_loop(1, NX - x, lambda d, c: (xcopy(d, x).wait_send(), c)[1], 0)
    lax.fori_loop(1, x + 1, lambda d, c: (xback_copy(-d, x - d).wait_send(), c)[1], 0)
    for i in range(NY):
        wcopy(i).wait_send()
    ecopy().wait_send()
    for d in range(1, NY):
        tcopy(d, y_peer(d)[1]).wait_send()


def emit_kernel(*refs):
    count = (len(refs) - 1) // 2
    copies = [
        pltpu.make_async_copy(refs[i], refs[count + i], refs[-1].at[i]) for i in range(count)
    ]
    for copy in copies:
        copy.start()
    for copy in copies:
        copy.wait()


def emit(arrays):
    anywhere = pl.BlockSpec(memory_space=pl.ANY)
    return pl.pallas_call(
        emit_kernel,
        name="emit",
        out_shape=tuple(jax.ShapeDtypeStruct(a.shape, a.dtype) for a in arrays),
        in_specs=[anywhere] * len(arrays),
        out_specs=(anywhere,) * len(arrays),
        scratch_shapes=[pltpu.SemaphoreType.DMA((len(arrays),))],
    )(*arrays)


def per_device(
    queries, keys_own, values_own, out_grad, summary_states, w_key, w_value, summary_grad
):
    anywhere = pl.BlockSpec(memory_space=pl.ANY)
    rows = HEADS * TOK
    cols = D // NTP
    dma = pltpu.SemaphoreType.DMA
    arrays = pl.pallas_call(
        layer_kernel,
        name="layer",
        out_shape=(
            jax.ShapeDtypeStruct((TOK, HEADS * HD), BF16),
            jax.ShapeDtypeStruct((TOK, HD), BF16),
            jax.ShapeDtypeStruct((TOK, HD), BF16),
            jax.ShapeDtypeStruct((M, cols), BF16),
        ),
        in_specs=[anywhere] * 8,
        out_specs=(anywhere,) * 3 + (pl.BlockSpec(memory_space=pltpu.VMEM),),
        scratch_shapes=[
            pltpu.VMEM((TOK, HEADS * HD), BF16),
            pltpu.VMEM((TOK, HEADS * HD), BF16),
            pltpu.VMEM((TOK, HD), BF16),
            pltpu.VMEM((TOK, HD), BF16),
            pltpu.VMEM((M, D), BF16),
            pltpu.VMEM((D, W2), BF16),
            pltpu.VMEM((M, cols), BF16),
            pltpu.VMEM((BLOCK, W2), BF16),
            pltpu.VMEM((NZ, BLOCK, W2), BF16),
            pltpu.VMEM((NX, GROUP, W2), BF16),
            pltpu.VMEM((TOK, rows), F32),
            pltpu.VMEM((TOK, rows), F32),
            pltpu.VMEM((NX, GROUP, rows), F32),
            pltpu.VMEM((NX, GROUP, rows), F32),
            pltpu.VMEM((1, rows), F32),
            pltpu.VMEM((1, rows), F32),
            pltpu.VMEM((1, rows), F32),
            pltpu.VMEM((HD, rows), F32),
            pltpu.VMEM((HD, TOK), BF16),
            pltpu.VMEM((HD, GROUP), BF16),
            pltpu.VMEM((GROUP, HD), F32),
            pltpu.VMEM((GROUP, HD), F32),
            pltpu.VMEM((NX, GROUP, W2), BF16),
            pltpu.VMEM((NX - 1, GROUP, W2), BF16),
            pltpu.VMEM((GROUP, W2), F32),
            pltpu.VMEM((NZ, BLOCK, W2), BF16),
            pltpu.VMEM((NZ - 1, BLOCK, W2), BF16),
            pltpu.VMEM((BLOCK, W2), BF16),
            pltpu.VMEM((BLOCK, W2), BF16),
            pltpu.VMEM((NY, cols, W2), BF16),
            pltpu.VMEM((NY, BLOCK, cols), F32),
            pltpu.VMEM((NY - 1, M, cols), BF16),
            pltpu.VMEM((NY - 1, M, cols), BF16),
            pltpu.VMEM((TOK, HEADS * HD), BF16),
            pltpu.VMEM((TOK, HD), BF16),
            pltpu.VMEM((TOK, HD), BF16),
            dma((WCHUNK, 2)),
            dma((6,)),
            dma((3,)),
            dma((NZ - 1,)),
            dma((NZ - 1,)),
            dma((NX - 1,)),
            dma((NX - 1,)),
            dma((NX - 1,)),
            dma((NX - 1,)),
            dma((NZ - 1,)),
            dma((NZ - 1,)),
            dma((NY - 1,)),
            dma((NY - 1,)),
            dma((NY,)),
            dma((NY,)),
            dma,
            dma,
        ],
        compiler_params=pltpu.CompilerParams(
            collective_id=0, has_side_effects=True, vmem_limit_bytes=58 << 20
        ),
    )(
        queries, out_grad, keys_own, values_own, summary_states, w_key, w_value, summary_grad
    )
    return emit(arrays)


def solution(mesh):
    placed = (
        P("seg", "tp"),
        P("seg", "tp"),
        P("seg", "tp"),
        P("seg", "tp"),
        P("seg", None),
        P(None, "tp"),
        P(None, "tp"),
        P("seg", "tp"),
    )
    return jax.shard_map(
        per_device,
        mesh=mesh,
        in_specs=placed,
        out_specs=(P("seg", "tp"), P("seg", "tp"), P("seg", "tp"), P("seg", "tp")),
        check_vma=False,
    )
```

```python
import functools
import math

import jax
import jax.numpy as jnp
from jax import lax
from jax.experimental import pallas as pl
from jax.experimental.pallas import tpu as pltpu
from jax.sharding import PartitionSpec as P

HD = 128
HEADS = 8
TOK = 256
M = 50
MAIN = 48
REM = M - MAIN
TILE = 16
NX, NZ = 4, 8
NTP = 8
NY = NTP // 2
GROUP = NZ * M
REM0 = NZ * MAIN
BLOCK = MAIN + TILE
D = 8192
W2 = 2 * HD
SCALE = HD ** (-0.5)
SCALE2 = SCALE * math.log2(math.e)
NEG = -1e30
F32 = jnp.float32
BF16 = jnp.bfloat16
MESH = pl.DeviceIdType.MESH
LAST = (((1,), (1,)), ((), ()))
PLAIN = (((1,), (0,)), ((), ()))
WCHUNK = 4


def dot(a, b, dims=PLAIN):
    return lax.dot_general(a, b, dims, preferred_element_type=F32)


def seg_place():
    seg = lax.axis_index("seg")
    return seg // NZ, lax.rem(seg, NZ)


def z_peer(x, z, d):
    other = lax.rem(z + d, NZ)
    return other, x * NZ + other


def x_peer(x, z, d):
    other = lax.rem(x + d, NX)
    return other, other * NZ + z


def greet(peers):
    barrier = pltpu.get_barrier_semaphore()
    for peer in peers:
        pl.semaphore_signal(barrier, inc=1, device_id=peer, device_id_type=MESH)
    return barrier, len(peers)


def load_weights(wk_hbm, wv_hbm, w, sems):
    rows = D // WCHUNK
    copies = []
    for c in range(WCHUNK):
        part = pl.ds(c * rows, rows)
        for i, src in enumerate((wk_hbm, wv_hbm)):
            copy = pltpu.make_async_copy(
                src.at[part], w.at[part, pl.ds(i * HD, HD)], sems.at[c, i]
            )
            copy.start()
            copies.append(copy)
    return copies


def layer_kernel(
    q_hbm, g_hbm, ko_hbm, vo_hbm, st_hbm, wk_hbm, wv_hbm, sg_hbm,
    dq_hbm, dko_hbm, dvo_hbm, out_ref,
    q_ref, g_ref, ko_ref, vo_ref, st, w, sg_ref,
    mine, zrecv, grp, s_own, p_own, s_all, p_all, m_ref, l_ref, d_ref, dqt, kt_own, kt,
    dk_acc, dv_acc, part, xback, acc, zsend, zback, em, etwin, wtwin, state, tsend, trecv, dq_ref, dko_ref, dvo_ref,
    wsem, insem, outsem, zs, zr, xs, xr, xbs, xbr, zbs, zbr, ts, tr, ws, wr, es, er,
):
    x, z = seg_place()
    tp = lax.axis_index("tp")
    peers = [{"seg": z_peer(x, z, d)[1]} for d in range(1, NZ)]
    peers += [{"seg": x_peer(x, z, d)[1]} for d in range(1, NX)]
    core = lax.rem(tp, 2)
    y = tp // 2
    twin = tp + 1 - 2 * core

    def y_peer(d):
        other = lax.rem(y + d, NY)
        return other, 2 * other + core

    peers += [{"tp": twin}] + [{"tp": y_peer(d)[1]} for d in range(1, NY)]
    last = x == NX - 1
    barrier, count = greet(peers)

    loads = []
    for i, (src, dst) in enumerate(
        (
            (st_hbm, st),
            (q_hbm, q_ref),
            (ko_hbm, ko_ref),
            (g_hbm, g_ref),
            (vo_hbm, vo_ref),
            (sg_hbm, sg_ref),
        )
    ):
        loads.append(pltpu.make_async_copy(src, dst, insem.at[i]))
    loads[0].start()
    wcopies = load_weights(wk_hbm, wv_hbm, w, wsem)
    for copy in loads[1:]:
        copy.start()

    loads[0].wait()
    rows = D // WCHUNK
    total = jnp.zeros((M, W2), F32)
    for c in range(WCHUNK):
        wcopies[2 * c].wait()
        wcopies[2 * c + 1].wait()
        chunk = pl.ds(c * rows, rows)
        total = total + dot(st[:, chunk], w[chunk, :])
    mine[0:MAIN, :] = total[0:MAIN].astype(BF16)
    row = lax.broadcasted_iota(jnp.int32, (TILE, W2), 0)
    shared = jnp.where(
        row == REM * z,
        total[MAIN : MAIN + 1],
        jnp.where(row == REM * z + 1, total[MAIN + 1 : MAIN + 2], 0.0),
    )
    mine[MAIN:BLOCK, :] = shared.astype(BF16)
    pl.semaphore_wait(barrier, count)

    def rows_of(i):
        return pl.ds(pl.multiple_of(i * MAIN, TILE), MAIN)

    def zcopies(d, peer, slot):
        own = {"device_id": {"seg": peer}, "device_id_type": MESH}
        return (
            pltpu.make_async_remote_copy(
                src_ref=mine.at[0:MAIN],
                dst_ref=grp.at[x, rows_of(slot)],
                send_sem=zs.at[0, d - 1],
                recv_sem=zr.at[0, d - 1],
                **own,
            ),
            pltpu.make_async_remote_copy(
                src_ref=mine.at[MAIN:BLOCK],
                dst_ref=zrecv.at[slot],
                send_sem=zs.at[1, d - 1],
                recv_sem=zr.at[1, d - 1],
                **own,
            ),
        )

    near = (1, 7, 2, 6, 3, 5, 4)
    for d in near:
        other, peer = z_peer(x, z, d)

        @pl.when(jnp.logical_not(last) | (other > z))
        def _(d=d, peer=peer):
            for copy in zcopies(d, peer, z):
                copy.start()

    def xcopy(d, g, part_rows=None):
        other = lax.rem(x + d + NX, NX)
        ref = grp.at[g] if part_rows is None else grp.at[g, part_rows]
        return pltpu.make_async_remote_copy(
            src_ref=ref,
            dst_ref=ref,
            send_sem=xs.at[jnp.abs(d) - 1],
            recv_sem=xr.at[jnp.abs(d) - 1],
            device_id={"seg": other * NZ + z},
            device_id_type=MESH,
        )

    def pass_on(part_rows):
        for d in (3, 1, 2):
            @pl.when((x + d < NX) & ((x > 0) | (d != 2)))
            def _(d=d):
                xcopy(d, x, part_rows).start()

    grp[x, rows_of(z), :] = mine[0:MAIN, :]
    pass_on(rows_of(z))

    def assemble(sent_on):
        acc[0:TILE, :] = mine[MAIN:BLOCK, :].astype(F32)
        for d in near:
            other, peer = z_peer(x, z, NZ - d)
            if sent_on:
                zcopies(d, peer, other)[0].wait_recv()
                pass_on(rows_of(other))
            else:

                @pl.when(other < z)
                def _(d=d, other=other, peer=peer):
                    zcopies(d, peer, other)[0].wait_recv()

                @pl.when(other > z)
                def _(other=other):
                    grp[x, rows_of(other), :] = jnp.zeros((MAIN, W2), BF16)

        for d in near:
            other, peer = z_peer(x, z, NZ - d)

            @pl.when(jnp.bool_(sent_on) | (other < z))
            def _(d=d, other=other, peer=peer):
                zcopies(d, peer, other)[1].wait_recv()
                acc[0:TILE, :] += zrecv[other].astype(F32)

        grp[x, REM0:GROUP, :] = acc[0:TILE, :].astype(BF16)
        if sent_on:
            pass_on(pl.ds(REM0, TILE))

            @pl.when(x == 0)
            def _():
                xcopy(2, x).start()

    @pl.when(jnp.logical_not(last))
    def _():
        assemble(True)

    cols = D // NTP

    def wcopy(i):
        rows_out = pl.ds(pl.multiple_of((2 * i + 1 - core) * cols, cols), cols)
        return pltpu.make_async_remote_copy(
            src_ref=w.at[rows_out],
            dst_ref=wtwin.at[i],
            send_sem=ws.at[i],
            recv_sem=wr.at[i],
            device_id={"tp": twin},
            device_id_type=MESH,
        )

    for i in range(NY):
        wcopy(i).start()

    def head(ref, h):
        return ref[:, h * HD : (h + 1) * HD]

    def lanes(h):
        return slice(h * TOK, (h + 1) * TOK)

    def sweep_one(keys, vals, s_ref, p_ref, mask, first):
        for h in range(HEADS):
            s = dot(keys, head(q_ref, h), LAST) * SCALE2
            if mask is not None:
                s = jnp.where(mask, s, NEG)
            s_ref[:, lanes(h)] = s
            top = jnp.max(s, axis=0, keepdims=True)
            p = dot(vals, head(g_ref, h), LAST)
            p_ref[:, lanes(h)] = p
            if not first:
                old = m_ref[:, lanes(h)]
                top = jnp.maximum(old, top)
            e = jnp.exp2(s - top)
            total = jnp.sum(e, axis=0, keepdims=True)
            inner = jnp.sum(e * p, axis=0, keepdims=True)
            if not first:
                fade = jnp.exp2(old - top)
                total = total + l_ref[:, lanes(h)] * fade
                inner = inner + d_ref[:, lanes(h)] * fade
            m_ref[:, lanes(h)] = top
            l_ref[:, lanes(h)] = total
            d_ref[:, lanes(h)] = inner

    def sweep_two(s_ref, p_ref, keys_t):
        count = s_ref.shape[0]
        dk = dk_acc.at[0:count]
        dv = dv_acc.at[0:count]
        for h in range(HEADS):
            probs = jnp.exp2(s_ref[:, lanes(h)] - m_ref[:, lanes(h)])
            ds = (probs * (p_ref[:, lanes(h)] - d_ref[:, lanes(h)])).astype(BF16)
            dv_new = dot(probs.astype(BF16), head(g_ref, h))
            dk_new = dot(ds, head(q_ref, h))
            if h:
                dv[...] += dv_new
                dk[...] += dk_new
            else:
                dv[...] = dv_new
                dk[...] = dk_new
            dqt[:, lanes(h)] += dot(keys_t[...], ds)
        return dk[...] * SCALE, dv[...]

    tri = lax.broadcasted_iota(jnp.int32, (TOK, TOK), 0) <= lax.broadcasted_iota(
        jnp.int32, (TOK, TOK), 1
    )
    for copy in loads[1:]:
        copy.wait()
    kt_own[...] = ko_ref[...].astype(F32).T.astype(BF16)
    dqt[...] = jnp.zeros_like(dqt)
    sweep_one(ko_ref[...], vo_ref[...], s_own, p_own, tri, True)

    def full_group(i, carry):
        d = jnp.where(last & (i > 1), 5 - i, i)
        g = x - d
        xcopy(-d, g).wait_recv()
        sweep_one(grp[g, :, 0:HD], grp[g, :, HD:W2], s_all.at[g], p_all.at[g], None, False)
        return carry

    lax.fori_loop(1, x + 1, full_group, 0)

    @pl.when(last)
    def _():
        assemble(False)

    @pl.when(z > 0)
    def _():
        r = lax.broadcasted_iota(jnp.int32, (GROUP, TOK), 0)
        mask = (r < MAIN * z) | ((r >= REM0) & (r < REM0 + REM * z))
        sweep_one(grp[x, :, 0:HD], grp[x, :, HD:W2], s_all.at[x], p_all.at[x], mask, False)

    d_ref[...] = d_ref[...] / l_ref[...]
    m_ref[...] = m_ref[...] + jnp.log2(l_ref[...])

    def hop(g, peer_x, wrap):
        return pltpu.make_async_remote_copy(
            src_ref=part.at[g],
            dst_ref=xback.at[jnp.where(wrap, NX - 1, g)],
            send_sem=xbs.at[g],
            recv_sem=xbr.at[jnp.where(wrap, NX - 1, g)],
            device_id={"seg": peer_x * NZ + z},
            device_id_type=MESH,
        )

    def hop_out(g):
        wrap = last & (g == 0)
        return hop(g, jnp.where(wrap, 0, x - 1), wrap)

    def hop_add(g, peer_x, wrap):
        hop(g, peer_x, wrap).wait_recv()
        acc[...] += xback[jnp.where(wrap, NX - 1, g)].astype(F32)

    def back_group(i, carry):
        g = jnp.where(last & (i < 2), 1 - i, i)
        kt[...] = grp[g, :, 0:HD].astype(F32).T.astype(BF16)
        dk, dv = sweep_two(s_all.at[g], p_all.at[g], kt)
        acc[:, 0:HD] = dk
        acc[:, HD:W2] = dv

        @pl.when(g < x)
        def _():
            @pl.when((x == 1) | ((x == 2) & (g == 1)))
            def _():
                hop_add(g, x + 1, False)

            part[g] = acc[...].astype(BF16)
            hop_out(g).start()

        return carry

    lax.fori_loop(0, x + jnp.minimum(z, 1), back_group, 0)

    @pl.when(z == 0)
    def _():
        acc[...] = jnp.zeros_like(acc)

    @pl.when(jnp.logical_not(last))
    def _():
        hop_add(x, x + 1, False)

    @pl.when(x == 0)
    def _():
        hop_add(x, NX - 1, True)

    for i in range(NZ):
        zsend[i, 0:MAIN, :] = acc[i * MAIN : (i + 1) * MAIN, :].astype(BF16)
        zsend[i, MAIN:BLOCK, :] = acc[REM0:GROUP, :].astype(BF16)

    def zback_copy(d, other, peer):
        return pltpu.make_async_remote_copy(
            src_ref=zsend.at[other],
            dst_ref=zback.at[d - 1],
            send_sem=zbs.at[d - 1],
            recv_sem=zbr.at[d - 1],
            device_id={"seg": peer},
            device_id_type=MESH,
        )

    for d in range(1, NZ):
        other, peer = z_peer(x, z, d)

        @pl.when(jnp.logical_not(last) | (other < z))
        def _(d=d, other=other, peer=peer):
            zback_copy(d, other, peer).start()

    dk, dv = sweep_two(s_own, p_own, kt_own)
    dko_ref[...] = dk.astype(BF16)
    dvo_ref[...] = dv.astype(BF16)
    for h in range(HEADS):
        dq_ref[:, h * HD : (h + 1) * HD] = (dqt[:, lanes(h)] * SCALE).T.astype(BF16)
    stores = [
        pltpu.make_async_copy(src, dst, outsem.at[i])
        for i, (src, dst) in enumerate(((dq_ref, dq_hbm), (dko_ref, dko_hbm), (dvo_ref, dvo_hbm)))
    ]
    for copy in stores:
        copy.start()

    mine_acc = acc.at[0:BLOCK]
    mine_acc[...] = zsend[z].astype(F32)
    for d in range(1, NZ):
        other, peer = z_peer(x, z, NZ - d)

        @pl.when(jnp.logical_not(last) | (other > z))
        def _(d=d, other=other, peer=peer):
            zback_copy(d, other, peer).wait_recv()
            mine_acc[...] += zback[d - 1].astype(F32)

    total = mine_acc[...]
    rem = total[MAIN:BLOCK]
    one = jnp.sum(jnp.where(row == REM * z, rem, 0.0), axis=0, keepdims=True)
    two = jnp.sum(jnp.where(row == REM * z + 1, rem, 0.0), axis=0, keepdims=True)
    em[0:MAIN, :] = total[0:MAIN].astype(BF16)
    em[MAIN:BLOCK, :] = jnp.where(row == 0, one, jnp.where(row == 1, two, 0.0)).astype(BF16)

    def ecopy():
        return pltpu.make_async_remote_copy(
            src_ref=em,
            dst_ref=etwin,
            send_sem=es,
            recv_sem=er,
            device_id={"tp": twin},
            device_id_type=MESH,
        )

    ecopy().start()
    order = (2, 1, 3, 0)
    for d in order:
        target = y_peer(d)[1]
        chunk = pl.ds(pl.multiple_of(target * cols, cols), cols)
        state[d] = dot(em[...], w[chunk, :], LAST)
    for i in range(NY):
        wcopy(i).wait_recv()
    ecopy().wait_recv()

    def tcopy(d, target):
        return pltpu.make_async_remote_copy(
            src_ref=tsend.at[d - 1],
            dst_ref=trecv.at[d - 1],
            send_sem=ts.at[d - 1],
            recv_sem=tr.at[d - 1],
            device_id={"tp": target},
            device_id_type=MESH,
        )

    for d in order:
        other, target = y_peer(d)
        both = (state[d] + dot(etwin[...], wtwin[other], LAST))[0:M]
        if d:
            tsend[d - 1] = both.astype(BF16)
            tcopy(d, target).start()
    out = both + sg_ref[...].astype(F32)
    for d in (1, 3, 2):
        tcopy(d, y_peer(NY - d)[1]).wait_recv()
        out = out + trecv[d - 1].astype(F32)
    out_ref[...] = out.astype(BF16)

    for copy in stores:
        copy.wait()
    for d in range(1, NZ):
        other, peer = z_peer(x, z, d)

        @pl.when(jnp.logical_not(last) | (other > z))
        def _(d=d, peer=peer):
            for copy in zcopies(d, peer, z):
                copy.wait_send()

        @pl.when(jnp.logical_not(last) | (other < z))
        def _(d=d, other=other, peer=peer):
            zback_copy(d, other, peer).wait_send()

    lax.fori_loop(1, NX - x, lambda d, c: (xcopy(d, x).wait_send(), c)[1], 0)
    lax.fori_loop(0, x, lambda g, c: (hop_out(g).wait_send(), c)[1], 0)
    for i in range(NY):
        wcopy(i).wait_send()
    ecopy().wait_send()
    for d in range(1, NY):
        tcopy(d, y_peer(d)[1]).wait_send()


def emit_kernel(count, *refs):
    ins, outs, bufs = refs[:count], refs[count : 2 * count], refs[2 * count : 3 * count]
    sems = refs[3 * count]
    loads = [pltpu.make_async_copy(ins[i], bufs[i], sems.at[0, i]) for i in range(count)]
    stores = [pltpu.make_async_copy(bufs[i], outs[i], sems.at[1, i]) for i in range(count)]
    for copy in loads:
        copy.start()
    for load, store in zip(loads, stores):
        load.wait()
        store.start()
    for copy in stores:
        copy.wait()


def emit(arrays):
    anywhere = pl.BlockSpec(memory_space=pl.ANY)
    count = len(arrays)
    return pl.pallas_call(
        functools.partial(emit_kernel, count),
        name="emit",
        out_shape=tuple(jax.ShapeDtypeStruct(a.shape, a.dtype) for a in arrays),
        in_specs=[anywhere] * count,
        out_specs=(anywhere,) * count,
        scratch_shapes=[pltpu.VMEM(a.shape, a.dtype) for a in arrays]
        + [pltpu.SemaphoreType.DMA((2, count))],
    )(*arrays)


def per_device(
    queries, keys_own, values_own, out_grad, summary_states, w_key, w_value, summary_grad
):
    anywhere = pl.BlockSpec(memory_space=pl.ANY)
    rows = HEADS * TOK
    cols = D // NTP
    dma = pltpu.SemaphoreType.DMA
    arrays = pl.pallas_call(
        layer_kernel,
        name="layer",
        out_shape=(
            jax.ShapeDtypeStruct((TOK, HEADS * HD), BF16),
            jax.ShapeDtypeStruct((TOK, HD), BF16),
            jax.ShapeDtypeStruct((TOK, HD), BF16),
            jax.ShapeDtypeStruct((M, cols), BF16),
        ),
        in_specs=[anywhere] * 8,
        out_specs=(anywhere,) * 3 + (pl.BlockSpec(memory_space=pltpu.VMEM),),
        scratch_shapes=[
            pltpu.VMEM((TOK, HEADS * HD), BF16),
            pltpu.VMEM((TOK, HEADS * HD), BF16),
            pltpu.VMEM((TOK, HD), BF16),
            pltpu.VMEM((TOK, HD), BF16),
            pltpu.VMEM((M, D), BF16),
            pltpu.VMEM((D, W2), BF16),
            pltpu.VMEM((M, cols), BF16),
            pltpu.VMEM((BLOCK, W2), BF16),
            pltpu.VMEM((NZ, TILE, W2), BF16),
            pltpu.VMEM((NX, GROUP, W2), BF16),
            pltpu.VMEM((TOK, rows), F32),
            pltpu.VMEM((TOK, rows), F32),
            pltpu.VMEM((NX, GROUP, rows), F32),
            pltpu.VMEM((NX, GROUP, rows), F32),
            pltpu.VMEM((1, rows), F32),
            pltpu.VMEM((1, rows), F32),
            pltpu.VMEM((1, rows), F32),
            pltpu.VMEM((HD, rows), F32),
            pltpu.VMEM((HD, TOK), BF16),
            pltpu.VMEM((HD, GROUP), BF16),
            pltpu.VMEM((GROUP, HD), F32),
            pltpu.VMEM((GROUP, HD), F32),
            pltpu.VMEM((NX, GROUP, W2), BF16),
            pltpu.VMEM((NX, GROUP, W2), BF16),
            pltpu.VMEM((GROUP, W2), F32),
            pltpu.VMEM((NZ, BLOCK, W2), BF16),
            pltpu.VMEM((NZ - 1, BLOCK, W2), BF16),
            pltpu.VMEM((BLOCK, W2), BF16),
            pltpu.VMEM((BLOCK, W2), BF16),
            pltpu.VMEM((NY, cols, W2), BF16),
            pltpu.VMEM((NY, BLOCK, cols), F32),
            pltpu.VMEM((NY - 1, M, cols), BF16),
            pltpu.VMEM((NY - 1, M, cols), BF16),
            pltpu.VMEM((TOK, HEADS * HD), BF16),
            pltpu.VMEM((TOK, HD), BF16),
            pltpu.VMEM((TOK, HD), BF16),
            dma((WCHUNK, 2)),
            dma((6,)),
            dma((3,)),
            dma((2, NZ - 1)),
            dma((2, NZ - 1)),
            dma((NX - 1,)),
            dma((NX - 1,)),
            dma((NX - 1,)),
            dma((NX,)),
            dma((NZ - 1,)),
            dma((NZ - 1,)),
            dma((NY - 1,)),
            dma((NY - 1,)),
            dma((NY,)),
            dma((NY,)),
            dma,
            dma,
        ],
        compiler_params=pltpu.CompilerParams(
            collective_id=0, has_side_effects=True, vmem_limit_bytes=58 << 20
        ),
    )(
        queries, out_grad, keys_own, values_own, summary_states, w_key, w_value, summary_grad
    )
    return emit(arrays)


def solution(mesh):
    placed = (
        P("seg", "tp"),
        P("seg", "tp"),
        P("seg", "tp"),
        P("seg", "tp"),
        P("seg", None),
        P(None, "tp"),
        P(None, "tp"),
        P("seg", "tp"),
    )
    return jax.shard_map(
        per_device,
        mesh=mesh,
        in_specs=placed,
        out_specs=(P("seg", "tp"), P("seg", "tp"), P("seg", "tp"), P("seg", "tp")),
        check_vma=False,
    )
```

```python
import functools
import math

import jax
import jax.numpy as jnp
from jax import lax
from jax.experimental import pallas as pl
from jax.experimental.pallas import tpu as pltpu
from jax.sharding import PartitionSpec as P

HD = 128
HEADS = 8
TOK = 256
M = 50
MAIN = 48
REM = M - MAIN
TILE = 16
NX, NZ = 4, 8
NTP = 8
NY = NTP // 2
GROUP = NZ * M
REM0 = NZ * MAIN
BLOCK = MAIN + TILE
HALF = REM0 // 2
D = 8192
W2 = 2 * HD
SCALE = HD ** (-0.5)
SCALE2 = SCALE * math.log2(math.e)
NEG = -1e30
F32 = jnp.float32
BF16 = jnp.bfloat16
MESH = pl.DeviceIdType.MESH
LAST = (((1,), (1,)), ((), ()))
PLAIN = (((1,), (0,)), ((), ()))
WCHUNK = 4


def dot(a, b, dims=PLAIN):
    return lax.dot_general(a, b, dims, preferred_element_type=F32)


def seg_place():
    seg = lax.axis_index("seg")
    return seg // NZ, lax.rem(seg, NZ)


def z_peer(x, z, d):
    other = lax.rem(z + d, NZ)
    return other, x * NZ + other


def x_peer(x, z, d):
    other = lax.rem(x + d, NX)
    return other, other * NZ + z


def greet(peers):
    barrier = pltpu.get_barrier_semaphore()
    for peer in peers:
        pl.semaphore_signal(barrier, inc=1, device_id=peer, device_id_type=MESH)
    return barrier, len(peers)


def load_weights(wk_hbm, wv_hbm, w, sems):
    rows = D // WCHUNK
    copies = []
    for c in range(WCHUNK):
        part = pl.ds(c * rows, rows)
        for i, src in enumerate((wk_hbm, wv_hbm)):
            copy = pltpu.make_async_copy(
                src.at[part], w.at[part, pl.ds(i * HD, HD)], sems.at[c, i]
            )
            copy.start()
            copies.append(copy)
    return copies


def layer_kernel(
    q_hbm, g_hbm, ko_hbm, vo_hbm, st_hbm, wk_hbm, wv_hbm, sg_hbm,
    dq_hbm, dko_hbm, dvo_hbm, out_ref,
    q_ref, g_ref, ko_ref, vo_ref, st, w, sg_ref,
    mine, zrecv, grp, s_own, p_own, s_all, p_all, m_ref, l_ref, d_ref, dqt, kt_own, kt,
    dk_acc, dv_acc, part, xback, acc, zmain, zrem, zback, zback_rem, em, etwin, wtwin, state, tsend, trecv, dq_ref, dko_ref, dvo_ref,
    wsem, insem, outsem, zs, zr, xs, xr, xbs, xbr, zbs, zbr, ts, tr, ws, wr, es, er,
):
    x, z = seg_place()
    tp = lax.axis_index("tp")
    peers = [{"seg": z_peer(x, z, d)[1]} for d in range(1, NZ)]
    peers += [{"seg": x_peer(x, z, d)[1]} for d in range(1, NX)]
    core = lax.rem(tp, 2)
    y = tp // 2
    twin = tp + 1 - 2 * core

    def y_peer(d):
        other = lax.rem(y + d, NY)
        return other, 2 * other + core

    peers += [{"tp": twin}] + [{"tp": y_peer(d)[1]} for d in range(1, NY)]
    last = x == NX - 1
    barrier, count = greet(peers)

    loads = []
    for i, (src, dst) in enumerate(
        (
            (st_hbm, st),
            (q_hbm, q_ref),
            (ko_hbm, ko_ref),
            (g_hbm, g_ref),
            (vo_hbm, vo_ref),
            (sg_hbm, sg_ref),
        )
    ):
        loads.append(pltpu.make_async_copy(src, dst, insem.at[i]))
    loads[0].start()
    wcopies = load_weights(wk_hbm, wv_hbm, w, wsem)
    for copy in loads[1:]:
        copy.start()

    loads[0].wait()
    rows = D // WCHUNK
    total = jnp.zeros((M, W2), F32)
    for c in range(WCHUNK):
        wcopies[2 * c].wait()
        wcopies[2 * c + 1].wait()
        chunk = pl.ds(c * rows, rows)
        total = total + dot(st[:, chunk], w[chunk, :])
    mine[0:MAIN, :] = total[0:MAIN].astype(BF16)
    row = lax.broadcasted_iota(jnp.int32, (TILE, W2), 0)
    shared = jnp.where(
        row == REM * z,
        total[MAIN : MAIN + 1],
        jnp.where(row == REM * z + 1, total[MAIN + 1 : MAIN + 2], 0.0),
    )
    mine[MAIN:BLOCK, :] = shared.astype(BF16)
    pl.semaphore_wait(barrier, count)

    def rows_of(i):
        return pl.ds(pl.multiple_of(i * MAIN, TILE), MAIN)

    def zcopies(d, peer, slot):
        own = {"device_id": {"seg": peer}, "device_id_type": MESH}
        return (
            pltpu.make_async_remote_copy(
                src_ref=mine.at[0:MAIN],
                dst_ref=grp.at[x, rows_of(slot)],
                send_sem=zs.at[0, d - 1],
                recv_sem=zr.at[0, d - 1],
                **own,
            ),
            pltpu.make_async_remote_copy(
                src_ref=mine.at[MAIN:BLOCK],
                dst_ref=zrecv.at[slot],
                send_sem=zs.at[1, d - 1],
                recv_sem=zr.at[1, d - 1],
                **own,
            ),
        )

    near = (1, 7, 2, 6, 3, 5, 4)
    for d in near:
        other, peer = z_peer(x, z, d)

        @pl.when(jnp.logical_not(last) | (other > z))
        def _(d=d, peer=peer):
            for copy in zcopies(d, peer, z):
                copy.start()

    def xcopy(d, g, part_rows=None):
        other = lax.rem(x + d + NX, NX)
        ref = grp.at[g] if part_rows is None else grp.at[g, part_rows]
        return pltpu.make_async_remote_copy(
            src_ref=ref,
            dst_ref=ref,
            send_sem=xs.at[jnp.abs(d) - 1],
            recv_sem=xr.at[jnp.abs(d) - 1],
            device_id={"seg": other * NZ + z},
            device_id_type=MESH,
        )

    def pass_on(part_rows):
        for d in (3, 1, 2):
            @pl.when((x + d < NX) & ((x > 0) | (d != 2)))
            def _(d=d):
                xcopy(d, x, part_rows).start()

    grp[x, rows_of(z), :] = mine[0:MAIN, :]
    pass_on(rows_of(z))

    def assemble(sent_on):
        acc[0:TILE, :] = mine[MAIN:BLOCK, :].astype(F32)
        for d in near:
            other, peer = z_peer(x, z, NZ - d)
            if sent_on:
                zcopies(d, peer, other)[0].wait_recv()
                pass_on(rows_of(other))
            else:

                @pl.when(other < z)
                def _(d=d, other=other, peer=peer):
                    zcopies(d, peer, other)[0].wait_recv()

                @pl.when(other > z)
                def _(other=other):
                    grp[x, rows_of(other), :] = jnp.zeros((MAIN, W2), BF16)

        for d in near:
            other, peer = z_peer(x, z, NZ - d)

            @pl.when(jnp.bool_(sent_on) | (other < z))
            def _(d=d, other=other, peer=peer):
                zcopies(d, peer, other)[1].wait_recv()
                acc[0:TILE, :] += zrecv[other].astype(F32)

        grp[x, REM0:GROUP, :] = acc[0:TILE, :].astype(BF16)
        if sent_on:
            pass_on(pl.ds(REM0, TILE))

            @pl.when(x == 0)
            def _():
                xcopy(2, x).start()

    @pl.when(jnp.logical_not(last))
    def _():
        assemble(True)

    cols = D // NTP

    def wcopy(i):
        rows_out = pl.ds(pl.multiple_of((2 * i + 1 - core) * cols, cols), cols)
        return pltpu.make_async_remote_copy(
            src_ref=w.at[rows_out],
            dst_ref=wtwin.at[i],
            send_sem=ws.at[i],
            recv_sem=wr.at[i],
            device_id={"tp": twin},
            device_id_type=MESH,
        )

    for i in range(NY):
        wcopy(i).start()

    def head(ref, h):
        return ref[:, h * HD : (h + 1) * HD]

    def lanes(h):
        return slice(h * TOK, (h + 1) * TOK)

    def sweep_one(keys, vals, s_ref, p_ref, mask, first):
        for h in range(HEADS):
            s = dot(keys, head(q_ref, h), LAST) * SCALE2
            if mask is not None:
                s = jnp.where(mask, s, NEG)
            s_ref[:, lanes(h)] = s
            top = jnp.max(s, axis=0, keepdims=True)
            p = dot(vals, head(g_ref, h), LAST)
            p_ref[:, lanes(h)] = p
            if not first:
                old = m_ref[:, lanes(h)]
                top = jnp.maximum(old, top)
            e = jnp.exp2(s - top)
            total = jnp.sum(e, axis=0, keepdims=True)
            inner = jnp.sum(e * p, axis=0, keepdims=True)
            if not first:
                fade = jnp.exp2(old - top)
                total = total + l_ref[:, lanes(h)] * fade
                inner = inner + d_ref[:, lanes(h)] * fade
            m_ref[:, lanes(h)] = top
            l_ref[:, lanes(h)] = total
            d_ref[:, lanes(h)] = inner

    def sweep_two(s_ref, p_ref, keys_t):
        count = s_ref.shape[0]
        dk = dk_acc.at[0:count]
        dv = dv_acc.at[0:count]
        for h in range(HEADS):
            probs = jnp.exp2(s_ref[:, lanes(h)] - m_ref[:, lanes(h)])
            ds = (probs * (p_ref[:, lanes(h)] - d_ref[:, lanes(h)])).astype(BF16)
            dv_new = dot(probs.astype(BF16), head(g_ref, h))
            dk_new = dot(ds, head(q_ref, h))
            if h:
                dv[...] += dv_new
                dk[...] += dk_new
            else:
                dv[...] = dv_new
                dk[...] = dk_new
            dqt[:, lanes(h)] += dot(keys_t[...], ds)
        return dk[...] * SCALE, dv[...]

    tri = lax.broadcasted_iota(jnp.int32, (TOK, TOK), 0) <= lax.broadcasted_iota(
        jnp.int32, (TOK, TOK), 1
    )
    for copy in loads[1:]:
        copy.wait()
    kt_own[...] = ko_ref[...].astype(F32).T.astype(BF16)
    dqt[...] = jnp.zeros_like(dqt)
    sweep_one(ko_ref[...], vo_ref[...], s_own, p_own, tri, True)

    def full_group(i, carry):
        d = jnp.where(last & (i > 1), 5 - i, i)
        g = x - d
        xcopy(-d, g).wait_recv()
        sweep_one(grp[g, :, 0:HD], grp[g, :, HD:W2], s_all.at[g], p_all.at[g], None, False)
        return carry

    lax.fori_loop(1, x + 1, full_group, 0)

    @pl.when(last)
    def _():
        assemble(False)

    @pl.when(z > 0)
    def _():
        r = lax.broadcasted_iota(jnp.int32, (GROUP, TOK), 0)
        mask = (r < MAIN * z) | ((r >= REM0) & (r < REM0 + REM * z))
        sweep_one(grp[x, :, 0:HD], grp[x, :, HD:W2], s_all.at[x], p_all.at[x], mask, False)

    d_ref[...] = d_ref[...] / l_ref[...]
    m_ref[...] = m_ref[...] + jnp.log2(l_ref[...])

    pieces = (pl.ds(0, HALF), pl.ds(HALF, GROUP - HALF))

    def hop(g, piece, peer_x, wrap):
        slot = jnp.where(wrap, NX - 1, g)
        return pltpu.make_async_remote_copy(
            src_ref=part.at[g, pieces[piece]],
            dst_ref=xback.at[slot, pieces[piece]],
            send_sem=xbs.at[g, piece],
            recv_sem=xbr.at[slot, piece],
            device_id={"seg": peer_x * NZ + z},
            device_id_type=MESH,
        )

    def hop_out(g, piece):
        wrap = last & (g == 0)
        return hop(g, piece, jnp.where(wrap, 0, x - 1), wrap)

    def hop_add(g, piece, peer_x, wrap):
        hop(g, piece, peer_x, wrap).wait_recv()
        rows_in = pieces[piece]
        acc[rows_in, :] += xback[jnp.where(wrap, NX - 1, g), rows_in, :].astype(F32)

    def back_group(i, carry):
        g = jnp.where(last & (i < 2), 1 - i, i)
        kt[...] = grp[g, :, 0:HD].astype(F32).T.astype(BF16)
        dk, dv = sweep_two(s_all.at[g], p_all.at[g], kt)
        acc[:, 0:HD] = dk
        acc[:, HD:W2] = dv

        @pl.when(g < x)
        def _():
            for piece in range(2):

                @pl.when((x == 1) | ((x == 2) & (g == 1)))
                def _(piece=piece):
                    hop_add(g, piece, x + 1, False)

                part[g, pieces[piece], :] = acc[pieces[piece], :].astype(BF16)
                hop_out(g, piece).start()

        return carry

    lax.fori_loop(0, x + jnp.minimum(z, 1), back_group, 0)

    @pl.when(z == 0)
    def _():
        acc[...] = jnp.zeros_like(acc)

    def zmain_copy(source, target):
        return pltpu.make_async_remote_copy(
            src_ref=zmain.at[target],
            dst_ref=zback.at[source],
            send_sem=zbs.at[0, target],
            recv_sem=zbr.at[0, source],
            device_id={"seg": x * NZ + target},
            device_id_type=MESH,
        )

    def zrem_copy(source, target):
        return pltpu.make_async_remote_copy(
            src_ref=zrem,
            dst_ref=zback_rem.at[source],
            send_sem=zbs.at[1, target],
            recv_sem=zbr.at[1, source],
            device_id={"seg": x * NZ + target},
            device_id_type=MESH,
        )

    def sends(source, target):
        return (source != target) & (jnp.logical_not(last) | (target < source))

    for piece in range(2):

        @pl.when(jnp.logical_not(last))
        def _(piece=piece):
            hop_add(x, piece, x + 1, False)

        @pl.when(x == 0)
        def _(piece=piece):
            hop_add(x, piece, NX - 1, True)

        for i in range(piece * NZ // 2, (piece + 1) * NZ // 2):
            zmain[i] = acc[i * MAIN : (i + 1) * MAIN, :].astype(BF16)

            @pl.when(sends(z, i))
            def _(i=i):
                zmain_copy(z, i).start()

    zrem[...] = acc[REM0:GROUP, :].astype(BF16)
    for i in range(NZ):

        @pl.when(sends(z, i))
        def _(i=i):
            zrem_copy(z, i).start()

    dk, dv = sweep_two(s_own, p_own, kt_own)
    dko_ref[...] = dk.astype(BF16)
    dvo_ref[...] = dv.astype(BF16)
    for h in range(HEADS):
        dq_ref[:, h * HD : (h + 1) * HD] = (dqt[:, lanes(h)] * SCALE).T.astype(BF16)
    stores = [
        pltpu.make_async_copy(src, dst, outsem.at[i])
        for i, (src, dst) in enumerate(((dq_ref, dq_hbm), (dko_ref, dko_hbm), (dvo_ref, dvo_hbm)))
    ]
    for copy in stores:
        copy.start()

    acc[0:MAIN, :] = zmain[z].astype(F32)
    acc[MAIN:BLOCK, :] = zrem[...].astype(F32)
    for i in range(NZ):

        @pl.when(sends(i, z))
        def _(i=i):
            zmain_copy(i, z).wait_recv()
            acc[0:MAIN, :] += zback[i].astype(F32)

    for i in range(NZ):

        @pl.when(sends(i, z))
        def _(i=i):
            zrem_copy(i, z).wait_recv()
            acc[MAIN:BLOCK, :] += zback_rem[i].astype(F32)

    total = acc[0:BLOCK, :]
    rem = total[MAIN:BLOCK]
    one = jnp.sum(jnp.where(row == REM * z, rem, 0.0), axis=0, keepdims=True)
    two = jnp.sum(jnp.where(row == REM * z + 1, rem, 0.0), axis=0, keepdims=True)
    em[0:MAIN, :] = total[0:MAIN].astype(BF16)
    em[MAIN:BLOCK, :] = jnp.where(row == 0, one, jnp.where(row == 1, two, 0.0)).astype(BF16)

    def ecopy():
        return pltpu.make_async_remote_copy(
            src_ref=em,
            dst_ref=etwin,
            send_sem=es,
            recv_sem=er,
            device_id={"tp": twin},
            device_id_type=MESH,
        )

    ecopy().start()
    order = (2, 1, 3, 0)
    for d in order:
        target = y_peer(d)[1]
        chunk = pl.ds(pl.multiple_of(target * cols, cols), cols)
        state[d] = dot(em[...], w[chunk, :], LAST)
    for i in range(NY):
        wcopy(i).wait_recv()
    ecopy().wait_recv()

    half = cols // 2
    lo, hi = slice(0, half), slice(half, cols)
    below, above = y_peer(NY - 1)[1], y_peer(1)[1]
    targets = (below, above, below, below, above, above)
    sources = (above, below, above, above, below, below)

    def tcopy(i, target):
        return pltpu.make_async_remote_copy(
            src_ref=tsend.at[i],
            dst_ref=trecv.at[i],
            send_sem=ts.at[i],
            recv_sem=tr.at[i],
            device_id={"tp": target},
            device_id_type=MESH,
        )

    def put(i, value):
        tsend[i] = value.astype(BF16)
        tcopy(i, targets[i]).start()

    def take(i):
        tcopy(i, sources[i]).wait_recv()
        return trecv[i].astype(F32)

    def both(d):
        return (state[d] + dot(etwin[...], wtwin[y_peer(d)[0]], LAST))[0:M]

    value = both(2)
    put(0, value[:, lo])
    put(1, value[:, hi])
    value = both(NY - 1)
    put(3, value[:, hi])
    state[NY - 1, 0:M, :] = value
    value = both(1)
    put(4, value[:, lo])
    state[1, 0:M, :] = value
    state[0, 0:M, :] = both(0) + sg_ref[...].astype(F32)
    put(2, state[NY - 1, 0:M, lo] + take(0))
    put(5, state[1, 0:M, hi] + take(1))
    out_hi = state[0, 0:M, hi] + take(3)
    out_lo = state[0, 0:M, lo] + take(4)
    out_ref[:, lo] = (out_lo + take(2)).astype(BF16)
    out_ref[:, hi] = (out_hi + take(5)).astype(BF16)

    for copy in stores:
        copy.wait()
    for d in range(1, NZ):
        other, peer = z_peer(x, z, d)

        @pl.when(jnp.logical_not(last) | (other > z))
        def _(d=d, peer=peer):
            for copy in zcopies(d, peer, z):
                copy.wait_send()

    for i in range(NZ):

        @pl.when(sends(z, i))
        def _(i=i):
            zmain_copy(z, i).wait_send()
            zrem_copy(z, i).wait_send()

    lax.fori_loop(1, NX - x, lambda d, c: (xcopy(d, x).wait_send(), c)[1], 0)
    for piece in range(2):
        lax.fori_loop(0, x, lambda g, c: (hop_out(g, piece).wait_send(), c)[1], 0)
    for i in range(NY):
        wcopy(i).wait_send()
    ecopy().wait_send()
    for i in range(len(targets)):
        tcopy(i, targets[i]).wait_send()


def emit_kernel(count, *refs):
    ins, outs, bufs = refs[:count], refs[count : 2 * count], refs[2 * count : 3 * count]
    sems = refs[3 * count]
    loads = [pltpu.make_async_copy(ins[i], bufs[i], sems.at[0, i]) for i in range(count)]
    stores = [pltpu.make_async_copy(bufs[i], outs[i], sems.at[1, i]) for i in range(count)]
    for copy in loads:
        copy.start()
    for load, store in zip(loads, stores):
        load.wait()
        store.start()
    for copy in stores:
        copy.wait()


def emit(arrays):
    anywhere = pl.BlockSpec(memory_space=pl.ANY)
    count = len(arrays)
    return pl.pallas_call(
        functools.partial(emit_kernel, count),
        name="emit",
        out_shape=tuple(jax.ShapeDtypeStruct(a.shape, a.dtype) for a in arrays),
        in_specs=[anywhere] * count,
        out_specs=(anywhere,) * count,
        scratch_shapes=[pltpu.VMEM(a.shape, a.dtype) for a in arrays]
        + [pltpu.SemaphoreType.DMA((2, count))],
    )(*arrays)


def per_device(
    queries, keys_own, values_own, out_grad, summary_states, w_key, w_value, summary_grad
):
    anywhere = pl.BlockSpec(memory_space=pl.ANY)
    rows = HEADS * TOK
    cols = D // NTP
    dma = pltpu.SemaphoreType.DMA
    arrays = pl.pallas_call(
        layer_kernel,
        name="layer",
        out_shape=(
            jax.ShapeDtypeStruct((TOK, HEADS * HD), BF16),
            jax.ShapeDtypeStruct((TOK, HD), BF16),
            jax.ShapeDtypeStruct((TOK, HD), BF16),
            jax.ShapeDtypeStruct((M, cols), BF16),
        ),
        in_specs=[anywhere] * 8,
        out_specs=(anywhere,) * 3 + (pl.BlockSpec(memory_space=pltpu.VMEM),),
        scratch_shapes=[
            pltpu.VMEM((TOK, HEADS * HD), BF16),
            pltpu.VMEM((TOK, HEADS * HD), BF16),
            pltpu.VMEM((TOK, HD), BF16),
            pltpu.VMEM((TOK, HD), BF16),
            pltpu.VMEM((M, D), BF16),
            pltpu.VMEM((D, W2), BF16),
            pltpu.VMEM((M, cols), BF16),
            pltpu.VMEM((BLOCK, W2), BF16),
            pltpu.VMEM((NZ, TILE, W2), BF16),
            pltpu.VMEM((NX, GROUP, W2), BF16),
            pltpu.VMEM((TOK, rows), F32),
            pltpu.VMEM((TOK, rows), F32),
            pltpu.VMEM((NX, GROUP, rows), F32),
            pltpu.VMEM((NX, GROUP, rows), F32),
            pltpu.VMEM((1, rows), F32),
            pltpu.VMEM((1, rows), F32),
            pltpu.VMEM((1, rows), F32),
            pltpu.VMEM((HD, rows), F32),
            pltpu.VMEM((HD, TOK), BF16),
            pltpu.VMEM((HD, GROUP), BF16),
            pltpu.VMEM((GROUP, HD), F32),
            pltpu.VMEM((GROUP, HD), F32),
            pltpu.VMEM((NX, GROUP, W2), BF16),
            pltpu.VMEM((NX, GROUP, W2), BF16),
            pltpu.VMEM((GROUP, W2), F32),
            pltpu.VMEM((NZ, MAIN, W2), BF16),
            pltpu.VMEM((TILE, W2), BF16),
            pltpu.VMEM((NZ, MAIN, W2), BF16),
            pltpu.VMEM((NZ, TILE, W2), BF16),
            pltpu.VMEM((BLOCK, W2), BF16),
            pltpu.VMEM((BLOCK, W2), BF16),
            pltpu.VMEM((NY, cols, W2), BF16),
            pltpu.VMEM((NY, BLOCK, cols), F32),
            pltpu.VMEM((6, M, cols // 2), BF16),
            pltpu.VMEM((6, M, cols // 2), BF16),
            pltpu.VMEM((TOK, HEADS * HD), BF16),
            pltpu.VMEM((TOK, HD), BF16),
            pltpu.VMEM((TOK, HD), BF16),
            dma((WCHUNK, 2)),
            dma((6,)),
            dma((3,)),
            dma((2, NZ - 1)),
            dma((2, NZ - 1)),
            dma((NX - 1,)),
            dma((NX - 1,)),
            dma((NX - 1, 2)),
            dma((NX, 2)),
            dma((2, NZ)),
            dma((2, NZ)),
            dma((6,)),
            dma((6,)),
            dma((NY,)),
            dma((NY,)),
            dma,
            dma,
        ],
        compiler_params=pltpu.CompilerParams(
            collective_id=0, has_side_effects=True, vmem_limit_bytes=58 << 20
        ),
    )(
        queries, out_grad, keys_own, values_own, summary_states, w_key, w_value, summary_grad
    )
    return emit(arrays)


def solution(mesh):
    placed = (
        P("seg", "tp"),
        P("seg", "tp"),
        P("seg", "tp"),
        P("seg", "tp"),
        P("seg", None),
        P(None, "tp"),
        P(None, "tp"),
        P("seg", "tp"),
    )
    return jax.shard_map(
        per_device,
        mesh=mesh,
        in_specs=placed,
        out_specs=(P("seg", "tp"), P("seg", "tp"), P("seg", "tp"), P("seg", "tp")),
        check_vma=False,
    )
```

```python
import functools
import math

import jax
import jax.numpy as jnp
from jax import lax
from jax.experimental import pallas as pl
from jax.experimental.pallas import tpu as pltpu
from jax.sharding import PartitionSpec as P

HD = 128
HEADS = 8
TOK = 256
M = 50
MAIN = 48
REM = M - MAIN
TILE = 16
NX, NZ = 4, 8
NTP = 8
NY = NTP // 2
GROUP = NZ * M
REM0 = NZ * MAIN
BLOCK = MAIN + TILE
HALF = REM0 // 2
D = 8192
W2 = 2 * HD
SCALE = HD ** (-0.5)
SCALE2 = SCALE * math.log2(math.e)
NEG = -1e30
F32 = jnp.float32
BF16 = jnp.bfloat16
MESH = pl.DeviceIdType.MESH
LAST = (((1,), (1,)), ((), ()))
PLAIN = (((1,), (0,)), ((), ()))
WCHUNK = 4


def dot(a, b, dims=PLAIN):
    return lax.dot_general(a, b, dims, preferred_element_type=F32)


def seg_place():
    seg = lax.axis_index("seg")
    return seg // NZ, lax.rem(seg, NZ)


def z_peer(x, z, d):
    other = lax.rem(z + d, NZ)
    return other, x * NZ + other


def x_peer(x, z, d):
    other = lax.rem(x + d, NX)
    return other, other * NZ + z


def greet(peers):
    barrier = pltpu.get_barrier_semaphore()
    for peer in peers:
        pl.semaphore_signal(barrier, inc=1, device_id=peer, device_id_type=MESH)
    return barrier, len(peers)


def load_weights(wk_hbm, wv_hbm, w, sems):
    rows = D // WCHUNK
    copies = []
    for c in range(WCHUNK):
        part = pl.ds(c * rows, rows)
        for i, src in enumerate((wk_hbm, wv_hbm)):
            copy = pltpu.make_async_copy(
                src.at[part], w.at[part, pl.ds(i * HD, HD)], sems.at[c, i]
            )
            copy.start()
            copies.append(copy)
    return copies


def layer_kernel(
    q_hbm, g_hbm, ko_hbm, vo_hbm, st_hbm, wk_hbm, wv_hbm, sg_hbm,
    dq_hbm, dko_hbm, dvo_hbm, out_ref,
    q_ref, g_ref, ko_ref, vo_ref, st, w, sg_ref,
    mine, mine_rem, zrecv, grp, s_own, p_own, s_all, p_all, m_ref, l_ref, d_ref, dqt, kt_own, kt,
    dk_acc, dv_acc, part, xback, acc, zmain, zrem, zback, zback_rem, em, etwin, wtwin, state, tsend, trecv, dq_ref, dko_ref, dvo_ref,
    wsem, insem, outsem, zs, zr, xs, xr, xbs, xbr, zbs, zbr, ts, tr, ws, wr, es, er,
):
    x, z = seg_place()
    tp = lax.axis_index("tp")
    peers = [{"seg": z_peer(x, z, d)[1]} for d in range(1, NZ)]
    peers += [{"seg": x_peer(x, z, d)[1]} for d in range(1, NX)]
    core = lax.rem(tp, 2)
    y = tp // 2
    twin = tp + 1 - 2 * core

    def y_peer(d):
        other = lax.rem(y + d, NY)
        return other, 2 * other + core

    peers += [{"tp": twin}] + [{"tp": y_peer(d)[1]} for d in range(1, NY)]
    last = x == NX - 1
    barrier, count = greet(peers)

    loads = []
    for i, (src, dst) in enumerate(
        (
            (st_hbm, st),
            (q_hbm, q_ref),
            (ko_hbm, ko_ref),
            (g_hbm, g_ref),
            (vo_hbm, vo_ref),
            (sg_hbm, sg_ref),
        )
    ):
        loads.append(pltpu.make_async_copy(src, dst, insem.at[i]))
    loads[0].start()
    wcopies = load_weights(wk_hbm, wv_hbm, w, wsem)
    for copy in loads[1:]:
        copy.start()

    loads[0].wait()
    rows = D // WCHUNK
    total = jnp.zeros((M, W2), F32)
    for c in range(WCHUNK):
        wcopies[2 * c].wait()
        wcopies[2 * c + 1].wait()
        chunk = pl.ds(c * rows, rows)
        total = total + dot(st[:, chunk], w[chunk, :])
    mine[...] = total[0:MAIN].astype(BF16)
    mine_rem[...] = total[MAIN:M].astype(BF16)
    row = lax.broadcasted_iota(jnp.int32, (TILE, W2), 0)
    pl.semaphore_wait(barrier, count)

    def rows_of(i):
        return pl.ds(pl.multiple_of(i * MAIN, TILE), MAIN)

    def zcopies(d, peer, slot):
        own = {"device_id": {"seg": peer}, "device_id_type": MESH}
        return (
            pltpu.make_async_remote_copy(
                src_ref=mine,
                dst_ref=grp.at[x, rows_of(slot)],
                send_sem=zs.at[0, d - 1],
                recv_sem=zr.at[0, d - 1],
                **own,
            ),
            pltpu.make_async_remote_copy(
                src_ref=mine_rem,
                dst_ref=zrecv.at[slot],
                send_sem=zs.at[1, d - 1],
                recv_sem=zr.at[1, d - 1],
                **own,
            ),
        )

    near = (1, 7, 2, 6, 3, 5, 4)
    for d in near:
        other, peer = z_peer(x, z, d)

        @pl.when(jnp.logical_not(last) | (other > z))
        def _(d=d, peer=peer):
            for copy in zcopies(d, peer, z):
                copy.start()

    def xcopy(d, g, part_rows=None):
        other = lax.rem(x + d + NX, NX)
        ref = grp.at[g] if part_rows is None else grp.at[g, part_rows]
        return pltpu.make_async_remote_copy(
            src_ref=ref,
            dst_ref=ref,
            send_sem=xs.at[jnp.abs(d) - 1],
            recv_sem=xr.at[jnp.abs(d) - 1],
            device_id={"seg": other * NZ + z},
            device_id_type=MESH,
        )

    def pass_on(part_rows):
        for d in (3, 1, 2):
            @pl.when((x + d < NX) & ((x > 0) | (d != 2)))
            def _(d=d):
                xcopy(d, x, part_rows).start()

    grp[x, rows_of(z), :] = mine[...]
    pass_on(rows_of(z))

    def assemble(sent_on):
        def place_rem(ref, i):
            two = ref.astype(F32)
            acc[0:TILE, :] = jnp.where(
                row == REM * i,
                two[0:1],
                jnp.where(row == REM * i + 1, two[1:2], acc[0:TILE, :]),
            )

        acc[0:TILE, :] = jnp.zeros((TILE, W2), F32)
        place_rem(mine_rem[...], z)
        for d in near:
            other, peer = z_peer(x, z, NZ - d)
            if sent_on:
                zcopies(d, peer, other)[0].wait_recv()
                pass_on(rows_of(other))
            else:

                @pl.when(other < z)
                def _(d=d, other=other, peer=peer):
                    zcopies(d, peer, other)[0].wait_recv()

                @pl.when(other > z)
                def _(other=other):
                    grp[x, rows_of(other), :] = jnp.zeros((MAIN, W2), BF16)

        for d in near:
            other, peer = z_peer(x, z, NZ - d)

            @pl.when(jnp.bool_(sent_on) | (other < z))
            def _(d=d, other=other, peer=peer):
                zcopies(d, peer, other)[1].wait_recv()
                place_rem(zrecv[other], other)

        grp[x, REM0:GROUP, :] = acc[0:TILE, :].astype(BF16)
        if sent_on:
            pass_on(pl.ds(REM0, TILE))

            @pl.when(x == 0)
            def _():
                xcopy(2, x).start()

    @pl.when(jnp.logical_not(last))
    def _():
        assemble(True)

    cols = D // NTP

    def wcopy(i):
        rows_out = pl.ds(pl.multiple_of((2 * i + 1 - core) * cols, cols), cols)
        return pltpu.make_async_remote_copy(
            src_ref=w.at[rows_out],
            dst_ref=wtwin.at[i],
            send_sem=ws.at[i],
            recv_sem=wr.at[i],
            device_id={"tp": twin},
            device_id_type=MESH,
        )

    for i in range(NY):
        wcopy(i).start()

    def head(ref, h):
        return ref[:, h * HD : (h + 1) * HD]

    def lanes(h):
        return slice(h * TOK, (h + 1) * TOK)

    def sweep_one(keys, vals, s_ref, p_ref, mask, first):
        for h in range(HEADS):
            s = dot(keys, head(q_ref, h), LAST) * SCALE2
            if mask is not None:
                s = jnp.where(mask, s, NEG)
            s_ref[:, lanes(h)] = s
            top = jnp.max(s, axis=0, keepdims=True)
            p = dot(vals, head(g_ref, h), LAST)
            p_ref[:, lanes(h)] = p
            if not first:
                old = m_ref[:, lanes(h)]
                top = jnp.maximum(old, top)
            e = jnp.exp2(s - top)
            total = jnp.sum(e, axis=0, keepdims=True)
            inner = jnp.sum(e * p, axis=0, keepdims=True)
            if not first:
                fade = jnp.exp2(old - top)
                total = total + l_ref[:, lanes(h)] * fade
                inner = inner + d_ref[:, lanes(h)] * fade
            m_ref[:, lanes(h)] = top
            l_ref[:, lanes(h)] = total
            d_ref[:, lanes(h)] = inner

    def sweep_two(s_ref, p_ref, keys_t):
        count = s_ref.shape[0]
        dk = dk_acc.at[0:count]
        dv = dv_acc.at[0:count]
        for h in range(HEADS):
            probs = jnp.exp2(s_ref[:, lanes(h)] - m_ref[:, lanes(h)])
            ds = (probs * (p_ref[:, lanes(h)] - d_ref[:, lanes(h)])).astype(BF16)
            dv_new = dot(probs.astype(BF16), head(g_ref, h))
            dk_new = dot(ds, head(q_ref, h))
            if h:
                dv[...] += dv_new
                dk[...] += dk_new
            else:
                dv[...] = dv_new
                dk[...] = dk_new
            dqt[:, lanes(h)] += dot(keys_t[...], ds)
        return dk[...] * SCALE, dv[...]

    tri = lax.broadcasted_iota(jnp.int32, (TOK, TOK), 0) <= lax.broadcasted_iota(
        jnp.int32, (TOK, TOK), 1
    )
    for copy in loads[1:]:
        copy.wait()
    kt_own[...] = ko_ref[...].astype(F32).T.astype(BF16)
    dqt[...] = jnp.zeros_like(dqt)
    sweep_one(ko_ref[...], vo_ref[...], s_own, p_own, tri, True)

    def full_group(i, carry):
        d = jnp.where(last & (i > 1), 5 - i, i)
        g = x - d
        xcopy(-d, g).wait_recv()
        sweep_one(grp[g, :, 0:HD], grp[g, :, HD:W2], s_all.at[g], p_all.at[g], None, False)
        return carry

    lax.fori_loop(1, x + 1, full_group, 0)

    @pl.when(last)
    def _():
        assemble(False)

    @pl.when(z > 0)
    def _():
        r = lax.broadcasted_iota(jnp.int32, (GROUP, TOK), 0)
        mask = (r < MAIN * z) | ((r >= REM0) & (r < REM0 + REM * z))
        sweep_one(grp[x, :, 0:HD], grp[x, :, HD:W2], s_all.at[x], p_all.at[x], mask, False)

    d_ref[...] = d_ref[...] / l_ref[...]
    m_ref[...] = m_ref[...] + jnp.log2(l_ref[...])

    pieces = (pl.ds(0, HALF), pl.ds(HALF, GROUP - HALF))

    def hop(g, piece, slot, peer_x):
        return pltpu.make_async_remote_copy(
            src_ref=part.at[g, pieces[piece]],
            dst_ref=xback.at[slot, pieces[piece]],
            send_sem=xbs.at[g, piece],
            recv_sem=xbr.at[slot, piece],
            device_id={"seg": peer_x * NZ + z},
            device_id_type=MESH,
        )

    def hop_out(g, piece):
        around = last & ((g == 0) | ((g == 1) & (piece == 1)))
        slot = jnp.where(around, NX - 1 + g, g)
        up = (x == 2) & (g == 0)
        return hop(g, piece, slot, jnp.where(around, 0, jnp.where(up, NX - 1, x - 1)))

    def hop_add(piece, slot, peer_x):
        hop(0, piece, slot, peer_x).wait_recv()
        rows_in = pieces[piece]
        acc[rows_in, :] += xback[slot, rows_in, :].astype(F32)

    def back_group(i, carry):
        g = jnp.where(last & (i < x), lax.rem(i + 1, x + (x == 0)), i)
        kt[...] = grp[g, :, 0:HD].astype(F32).T.astype(BF16)
        dk, dv = sweep_two(s_all.at[g], p_all.at[g], kt)
        acc[:, 0:HD] = dk
        acc[:, HD:W2] = dv

        @pl.when(g < x)
        def _():
            for piece in range(2):

                @pl.when(last & (g == 0))
                def _(piece=piece):
                    hop_add(piece, 0, 2)

                if piece == 0:

                    @pl.when((x == 2) & (g == 1))
                    def _():
                        hop_add(0, 1, NX - 1)

                part[g, pieces[piece], :] = acc[pieces[piece], :].astype(BF16)
                hop_out(g, piece).start()

        return carry

    lax.fori_loop(0, x + jnp.minimum(z, 1), back_group, 0)

    @pl.when(z == 0)
    def _():
        acc[...] = jnp.zeros_like(acc)

    def zmain_copy(source, target):
        return pltpu.make_async_remote_copy(
            src_ref=zmain.at[target],
            dst_ref=zback.at[source],
            send_sem=zbs.at[0, target],
            recv_sem=zbr.at[0, source],
            device_id={"seg": x * NZ + target},
            device_id_type=MESH,
        )

    def zrem_copy(source, target):
        return pltpu.make_async_remote_copy(
            src_ref=zrem.at[target],
            dst_ref=zback_rem.at[source],
            send_sem=zbs.at[1, target],
            recv_sem=zbr.at[1, source],
            device_id={"seg": x * NZ + target},
            device_id_type=MESH,
        )

    def sends(source, target):
        return (source != target) & (jnp.logical_not(last) | (target < source))

    def relay():
        return pltpu.make_async_remote_copy(
            src_ref=xback.at[NX, pieces[1]],
            dst_ref=xback.at[NX, pieces[1]],
            send_sem=xbs.at[1, 1],
            recv_sem=xbr.at[NX, 1],
            device_id={"seg": NZ + z},
            device_id_type=MESH,
        )

    @pl.when(x == 0)
    def _():
        hop(1, 1, NX, NX - 1).wait_recv()
        relay().start()

    for piece in range(2):

        @pl.when(x == 0)
        def _(piece=piece):
            hop_add(piece, 0, 1)
            hop_add(piece, NX - 1, NX - 1)

        @pl.when(x == 1)
        def _(piece=piece):
            hop_add(piece, 1, 2)
            if piece == 1:
                hop_add(1, NX, 0)

        @pl.when(x == 2)
        def _(piece=piece):
            hop_add(piece, 2, NX - 1)

        for i in range(piece * NZ // 2, (piece + 1) * NZ // 2):
            zmain[i] = acc[i * MAIN : (i + 1) * MAIN, :].astype(BF16)

            @pl.when(sends(z, i))
            def _(i=i):
                zmain_copy(z, i).start()

    for i in range(NZ):
        zrem[i] = acc[REM0 + REM * i : REM0 + REM * (i + 1), :].astype(BF16)

        @pl.when(sends(z, i))
        def _(i=i):
            zrem_copy(z, i).start()

    dk, dv = sweep_two(s_own, p_own, kt_own)
    dko_ref[...] = dk.astype(BF16)
    dvo_ref[...] = dv.astype(BF16)
    for h in range(HEADS):
        dq_ref[:, h * HD : (h + 1) * HD] = (dqt[:, lanes(h)] * SCALE).T.astype(BF16)
    stores = [
        pltpu.make_async_copy(src, dst, outsem.at[i])
        for i, (src, dst) in enumerate(((dq_ref, dq_hbm), (dko_ref, dko_hbm), (dvo_ref, dvo_hbm)))
    ]
    for copy in stores:
        copy.start()

    acc[0:MAIN, :] = zmain[z].astype(F32)
    acc[MAIN:M, :] = zrem[z].astype(F32)
    for i in range(NZ):

        @pl.when(sends(i, z))
        def _(i=i):
            zmain_copy(i, z).wait_recv()
            acc[0:MAIN, :] += zback[i].astype(F32)

    for i in range(NZ):

        @pl.when(sends(i, z))
        def _(i=i):
            zrem_copy(i, z).wait_recv()
            acc[MAIN:M, :] += zback_rem[i].astype(F32)

    em[0:MAIN, :] = acc[0:MAIN, :].astype(BF16)
    em[MAIN:BLOCK, :] = jnp.where(
        row == 0, acc[MAIN : MAIN + 1, :], jnp.where(row == 1, acc[MAIN + 1 : M, :], 0.0)
    ).astype(BF16)

    def ecopy():
        return pltpu.make_async_remote_copy(
            src_ref=em,
            dst_ref=etwin,
            send_sem=es,
            recv_sem=er,
            device_id={"tp": twin},
            device_id_type=MESH,
        )

    ecopy().start()
    order = (2, 1, 3, 0)
    for d in order:
        target = y_peer(d)[1]
        chunk = pl.ds(pl.multiple_of(target * cols, cols), cols)
        state[d] = dot(em[...], w[chunk, :], LAST)
    for i in range(NY):
        wcopy(i).wait_recv()
    ecopy().wait_recv()

    half = cols // 2
    lo, hi = slice(0, half), slice(half, cols)
    below, above = y_peer(NY - 1)[1], y_peer(1)[1]
    targets = (below, above, below, below, above, above)
    sources = (above, below, above, above, below, below)

    def tcopy(i, target):
        return pltpu.make_async_remote_copy(
            src_ref=tsend.at[i],
            dst_ref=trecv.at[i],
            send_sem=ts.at[i],
            recv_sem=tr.at[i],
            device_id={"tp": target},
            device_id_type=MESH,
        )

    def put(i, value):
        tsend[i] = value.astype(BF16)
        tcopy(i, targets[i]).start()

    def take(i):
        tcopy(i, sources[i]).wait_recv()
        return trecv[i].astype(F32)

    def both(d):
        return (state[d] + dot(etwin[...], wtwin[y_peer(d)[0]], LAST))[0:M]

    value = both(2)
    put(0, value[:, lo])
    put(1, value[:, hi])
    value = both(NY - 1)
    put(3, value[:, hi])
    state[NY - 1, 0:M, :] = value
    value = both(1)
    put(4, value[:, lo])
    state[1, 0:M, :] = value
    state[0, 0:M, :] = both(0) + sg_ref[...].astype(F32)
    put(2, state[NY - 1, 0:M, lo] + take(0))
    put(5, state[1, 0:M, hi] + take(1))
    out_hi = state[0, 0:M, hi] + take(3)
    out_lo = state[0, 0:M, lo] + take(4)
    out_ref[:, lo] = (out_lo + take(2)).astype(BF16)
    out_ref[:, hi] = (out_hi + take(5)).astype(BF16)

    for copy in stores:
        copy.wait()
    for d in range(1, NZ):
        other, peer = z_peer(x, z, d)

        @pl.when(jnp.logical_not(last) | (other > z))
        def _(d=d, peer=peer):
            for copy in zcopies(d, peer, z):
                copy.wait_send()

    for i in range(NZ):

        @pl.when(sends(z, i))
        def _(i=i):
            zmain_copy(z, i).wait_send()
            zrem_copy(z, i).wait_send()

    lax.fori_loop(1, NX - x, lambda d, c: (xcopy(d, x).wait_send(), c)[1], 0)
    for piece in range(2):
        lax.fori_loop(0, x, lambda g, c: (hop_out(g, piece).wait_send(), c)[1], 0)
    for i in range(NY):
        wcopy(i).wait_send()
    ecopy().wait_send()
    @pl.when(x == 0)
    def _():
        relay().wait_send()

    for i in range(len(targets)):
        tcopy(i, targets[i]).wait_send()


def emit_kernel(count, *refs):
    ins, outs, bufs = refs[:count], refs[count : 2 * count], refs[2 * count : 3 * count]
    sems = refs[3 * count]
    loads = [pltpu.make_async_copy(ins[i], bufs[i], sems.at[0, i]) for i in range(count)]
    stores = [pltpu.make_async_copy(bufs[i], outs[i], sems.at[1, i]) for i in range(count)]
    for copy in loads:
        copy.start()
    for load, store in zip(loads, stores):
        load.wait()
        store.start()
    for copy in stores:
        copy.wait()


def emit(arrays):
    anywhere = pl.BlockSpec(memory_space=pl.ANY)
    count = len(arrays)
    return pl.pallas_call(
        functools.partial(emit_kernel, count),
        name="emit",
        out_shape=tuple(jax.ShapeDtypeStruct(a.shape, a.dtype) for a in arrays),
        in_specs=[anywhere] * count,
        out_specs=(anywhere,) * count,
        scratch_shapes=[pltpu.VMEM(a.shape, a.dtype) for a in arrays]
        + [pltpu.SemaphoreType.DMA((2, count))],
    )(*arrays)


def per_device(
    queries, keys_own, values_own, out_grad, summary_states, w_key, w_value, summary_grad
):
    anywhere = pl.BlockSpec(memory_space=pl.ANY)
    rows = HEADS * TOK
    cols = D // NTP
    dma = pltpu.SemaphoreType.DMA
    arrays = pl.pallas_call(
        layer_kernel,
        name="layer",
        out_shape=(
            jax.ShapeDtypeStruct((TOK, HEADS * HD), BF16),
            jax.ShapeDtypeStruct((TOK, HD), BF16),
            jax.ShapeDtypeStruct((TOK, HD), BF16),
            jax.ShapeDtypeStruct((M, cols), BF16),
        ),
        in_specs=[anywhere] * 8,
        out_specs=(anywhere,) * 3 + (pl.BlockSpec(memory_space=pltpu.VMEM),),
        scratch_shapes=[
            pltpu.VMEM((TOK, HEADS * HD), BF16),
            pltpu.VMEM((TOK, HEADS * HD), BF16),
            pltpu.VMEM((TOK, HD), BF16),
            pltpu.VMEM((TOK, HD), BF16),
            pltpu.VMEM((M, D), BF16),
            pltpu.VMEM((D, W2), BF16),
            pltpu.VMEM((M, cols), BF16),
            pltpu.VMEM((MAIN, W2), BF16),
            pltpu.VMEM((REM, W2), BF16),
            pltpu.VMEM((NZ, REM, W2), BF16),
            pltpu.VMEM((NX, GROUP, W2), BF16),
            pltpu.VMEM((TOK, rows), F32),
            pltpu.VMEM((TOK, rows), F32),
            pltpu.VMEM((NX, GROUP, rows), F32),
            pltpu.VMEM((NX, GROUP, rows), F32),
            pltpu.VMEM((1, rows), F32),
            pltpu.VMEM((1, rows), F32),
            pltpu.VMEM((1, rows), F32),
            pltpu.VMEM((HD, rows), F32),
            pltpu.VMEM((HD, TOK), BF16),
            pltpu.VMEM((HD, GROUP), BF16),
            pltpu.VMEM((GROUP, HD), F32),
            pltpu.VMEM((GROUP, HD), F32),
            pltpu.VMEM((NX, GROUP, W2), BF16),
            pltpu.VMEM((NX + 1, GROUP, W2), BF16),
            pltpu.VMEM((GROUP, W2), F32),
            pltpu.VMEM((NZ, MAIN, W2), BF16),
            pltpu.VMEM((NZ, REM, W2), BF16),
            pltpu.VMEM((NZ, MAIN, W2), BF16),
            pltpu.VMEM((NZ, REM, W2), BF16),
            pltpu.VMEM((BLOCK, W2), BF16),
            pltpu.VMEM((BLOCK, W2), BF16),
            pltpu.VMEM((NY, cols, W2), BF16),
            pltpu.VMEM((NY, BLOCK, cols), F32),
            pltpu.VMEM((6, M, cols // 2), BF16),
            pltpu.VMEM((6, M, cols // 2), BF16),
            pltpu.VMEM((TOK, HEADS * HD), BF16),
            pltpu.VMEM((TOK, HD), BF16),
            pltpu.VMEM((TOK, HD), BF16),
            dma((WCHUNK, 2)),
            dma((6,)),
            dma((3,)),
            dma((2, NZ - 1)),
            dma((2, NZ - 1)),
            dma((NX - 1,)),
            dma((NX - 1,)),
            dma((NX - 1, 2)),
            dma((NX + 1, 2)),
            dma((2, NZ)),
            dma((2, NZ)),
            dma((6,)),
            dma((6,)),
            dma((NY,)),
            dma((NY,)),
            dma,
            dma,
        ],
        compiler_params=pltpu.CompilerParams(
            collective_id=0, has_side_effects=True, vmem_limit_bytes=58 << 20
        ),
    )(
        queries, out_grad, keys_own, values_own, summary_states, w_key, w_value, summary_grad
    )
    return emit(arrays)


def solution(mesh):
    placed = (
        P("seg", "tp"),
        P("seg", "tp"),
        P("seg", "tp"),
        P("seg", "tp"),
        P("seg", None),
        P(None, "tp"),
        P(None, "tp"),
        P("seg", "tp"),
    )
    return jax.shard_map(
        per_device,
        mesh=mesh,
        in_specs=placed,
        out_specs=(P("seg", "tp"), P("seg", "tp"), P("seg", "tp"), P("seg", "tp")),
        check_vma=False,
    )
```

```python
import functools
import math

import jax
import jax.numpy as jnp
from jax import lax
from jax.experimental import pallas as pl
from jax.experimental.pallas import tpu as pltpu
from jax.sharding import PartitionSpec as P

HD = 128
HEADS = 8
TOK = 256
M = 50
MAIN = 48
REM = M - MAIN
TILE = 16
NX, NZ = 4, 8
NTP = 8
NY = NTP // 2
GROUP = NZ * M
REM0 = NZ * MAIN
BLOCK = MAIN + TILE
HALF = REM0 // 2
D = 8192
W2 = 2 * HD
SCALE = HD ** (-0.5)
SCALE2 = SCALE * math.log2(math.e)
NEG = -1e30
F32 = jnp.float32
BF16 = jnp.bfloat16
MESH = pl.DeviceIdType.MESH
LAST = (((1,), (1,)), ((), ()))
PLAIN = (((1,), (0,)), ((), ()))
WCHUNK = 4


def dot(a, b, dims=PLAIN):
    return lax.dot_general(a, b, dims, preferred_element_type=F32)


def seg_place():
    seg = lax.axis_index("seg")
    return seg // NZ, lax.rem(seg, NZ)


def z_peer(x, z, d):
    other = lax.rem(z + d, NZ)
    return other, x * NZ + other


def x_peer(x, z, d):
    other = lax.rem(x + d, NX)
    return other, other * NZ + z


def greet(peers):
    barrier = pltpu.get_barrier_semaphore()
    for peer in peers:
        pl.semaphore_signal(barrier, inc=1, device_id=peer, device_id_type=MESH)
    return barrier, len(peers)


def load_weights(wk_hbm, wv_hbm, w, sems):
    rows = D // WCHUNK
    copies = []
    for c in range(WCHUNK):
        part = pl.ds(c * rows, rows)
        for i, src in enumerate((wk_hbm, wv_hbm)):
            copy = pltpu.make_async_copy(
                src.at[part], w.at[part, pl.ds(i * HD, HD)], sems.at[c, i]
            )
            copy.start()
            copies.append(copy)
    return copies


def layer_kernel(
    q_hbm, g_hbm, ko_hbm, vo_hbm, st_hbm, wk_hbm, wv_hbm, sg_hbm,
    dq_hbm, dko_hbm, dvo_hbm, out_ref,
    q_ref, g_ref, ko_ref, vo_ref, st, w, sg_ref,
    mine, mine_rem, zrecv, grp, s_own, p_own, s_all, p_all, m_ref, l_ref, d_ref, dqt, kt_own, kt,
    dk_acc, dv_acc, part, xback, acc, zmain, zrem, zback, zback_rem, em, etwin, wtwin, state, tsend, trecv, dq_ref, dko_ref, dvo_ref,
    wsem, insem, outsem, zs, zr, xs, xr, xbs, xbr, zbs, zbr, ts, tr, ws, wr, es, er,
):
    x, z = seg_place()
    tp = lax.axis_index("tp")
    peers = [{"seg": z_peer(x, z, d)[1]} for d in range(1, NZ)]
    peers += [{"seg": x_peer(x, z, d)[1]} for d in range(1, NX)]
    core = lax.rem(tp, 2)
    y = tp // 2
    twin = tp + 1 - 2 * core

    def y_peer(d):
        other = lax.rem(y + d, NY)
        return other, 2 * other + core

    peers += [{"tp": twin}] + [{"tp": y_peer(d)[1]} for d in range(1, NY)]
    last = x == NX - 1
    barrier, count = greet(peers)

    loads = []
    for i, (src, dst) in enumerate(
        (
            (st_hbm, st),
            (q_hbm, q_ref),
            (ko_hbm, ko_ref),
            (g_hbm, g_ref),
            (vo_hbm, vo_ref),
            (sg_hbm, sg_ref),
        )
    ):
        loads.append(pltpu.make_async_copy(src, dst, insem.at[i]))
    loads[0].start()
    wcopies = load_weights(wk_hbm, wv_hbm, w, wsem)
    for copy in loads[1:]:
        copy.start()

    loads[0].wait()
    rows = D // WCHUNK
    total = jnp.zeros((M, W2), F32)
    for c in range(WCHUNK):
        wcopies[2 * c].wait()
        wcopies[2 * c + 1].wait()
        chunk = pl.ds(c * rows, rows)
        total = total + dot(st[:, chunk], w[chunk, :])
    mine[...] = total[0:MAIN].astype(BF16)
    mine_rem[...] = total[MAIN:M].astype(BF16)
    row = lax.broadcasted_iota(jnp.int32, (TILE, W2), 0)
    pl.semaphore_wait(barrier, count)

    def rows_of(i):
        return pl.ds(pl.multiple_of(i * MAIN, TILE), MAIN)

    def zcopies(d, peer, slot):
        own = {"device_id": {"seg": peer}, "device_id_type": MESH}
        return (
            pltpu.make_async_remote_copy(
                src_ref=mine,
                dst_ref=grp.at[x, rows_of(slot)],
                send_sem=zs.at[0, d - 1],
                recv_sem=zr.at[0, d - 1],
                **own,
            ),
            pltpu.make_async_remote_copy(
                src_ref=mine_rem,
                dst_ref=zrecv.at[slot],
                send_sem=zs.at[1, d - 1],
                recv_sem=zr.at[1, d - 1],
                **own,
            ),
        )

    near = (1, 7, 2, 6, 3, 5, 4)
    for d in near:
        other, peer = z_peer(x, z, d)

        @pl.when(jnp.logical_not(last) | (other > z))
        def _(d=d, peer=peer):
            for copy in zcopies(d, peer, z):
                copy.start()

    def xcopy(d, g, part_rows=None):
        other = lax.rem(x + d + NX, NX)
        ref = grp.at[g] if part_rows is None else grp.at[g, part_rows]
        return pltpu.make_async_remote_copy(
            src_ref=ref,
            dst_ref=ref,
            send_sem=xs.at[jnp.abs(d) - 1],
            recv_sem=xr.at[jnp.abs(d) - 1],
            device_id={"seg": other * NZ + z},
            device_id_type=MESH,
        )

    def pass_on(part_rows):
        for d in (3, 1, 2):
            @pl.when((x + d < NX) & ((x > 0) | (d != 2)))
            def _(d=d):
                xcopy(d, x, part_rows).start()

    grp[x, rows_of(z), :] = mine[...]
    pass_on(rows_of(z))

    def assemble(sent_on):
        def place_rem(ref, i):
            two = ref.astype(F32)
            acc[0:TILE, :] = jnp.where(
                row == REM * i,
                two[0:1],
                jnp.where(row == REM * i + 1, two[1:2], acc[0:TILE, :]),
            )

        acc[0:TILE, :] = jnp.zeros((TILE, W2), F32)
        place_rem(mine_rem[...], z)
        for d in near:
            other, peer = z_peer(x, z, NZ - d)
            if sent_on:
                zcopies(d, peer, other)[0].wait_recv()
                pass_on(rows_of(other))
            else:

                @pl.when(other < z)
                def _(d=d, other=other, peer=peer):
                    zcopies(d, peer, other)[0].wait_recv()

                @pl.when(other > z)
                def _(other=other):
                    grp[x, rows_of(other), :] = jnp.zeros((MAIN, W2), BF16)

        for d in near:
            other, peer = z_peer(x, z, NZ - d)

            @pl.when(jnp.bool_(sent_on) | (other < z))
            def _(d=d, other=other, peer=peer):
                zcopies(d, peer, other)[1].wait_recv()
                place_rem(zrecv[other], other)

        grp[x, REM0:GROUP, :] = acc[0:TILE, :].astype(BF16)
        if sent_on:
            pass_on(pl.ds(REM0, TILE))

            @pl.when(x == 0)
            def _():
                xcopy(2, x).start()

    @pl.when(jnp.logical_not(last))
    def _():
        assemble(True)

    cols = D // NTP

    def wcopy(i):
        rows_out = pl.ds(pl.multiple_of((2 * i + 1 - core) * cols, cols), cols)
        return pltpu.make_async_remote_copy(
            src_ref=w.at[rows_out],
            dst_ref=wtwin.at[i],
            send_sem=ws.at[i],
            recv_sem=wr.at[i],
            device_id={"tp": twin},
            device_id_type=MESH,
        )

    for i in range(NY):
        wcopy(i).start()

    def head(ref, h):
        return ref[:, h * HD : (h + 1) * HD]

    def lanes(h):
        return slice(h * TOK, (h + 1) * TOK)

    def sweep_one(keys, vals, s_ref, p_ref, mask, first):
        for h in range(HEADS):
            s = dot(keys, head(q_ref, h), LAST) * SCALE2
            if mask is not None:
                s = jnp.where(mask, s, NEG)
            s_ref[:, lanes(h)] = s
            top = jnp.max(s, axis=0, keepdims=True)
            p = dot(vals, head(g_ref, h), LAST)
            p_ref[:, lanes(h)] = p
            if not first:
                old = m_ref[:, lanes(h)]
                top = jnp.maximum(old, top)
            e = jnp.exp2(s - top)
            total = jnp.sum(e, axis=0, keepdims=True)
            inner = jnp.sum(e * p, axis=0, keepdims=True)
            if not first:
                fade = jnp.exp2(old - top)
                total = total + l_ref[:, lanes(h)] * fade
                inner = inner + d_ref[:, lanes(h)] * fade
            m_ref[:, lanes(h)] = top
            l_ref[:, lanes(h)] = total
            d_ref[:, lanes(h)] = inner

    def sweep_two(s_ref, p_ref, keys_t):
        count = s_ref.shape[0]
        dk = dk_acc.at[0:count]
        dv = dv_acc.at[0:count]
        for h in range(HEADS):
            probs = jnp.exp2(s_ref[:, lanes(h)] - m_ref[:, lanes(h)])
            ds = (probs * (p_ref[:, lanes(h)] - d_ref[:, lanes(h)])).astype(BF16)
            dv_new = dot(probs.astype(BF16), head(g_ref, h))
            dk_new = dot(ds, head(q_ref, h))
            if h:
                dv[...] += dv_new
                dk[...] += dk_new
            else:
                dv[...] = dv_new
                dk[...] = dk_new
            dqt[:, lanes(h)] += dot(keys_t[...], ds)
        return dk[...] * SCALE, dv[...]

    tri = lax.broadcasted_iota(jnp.int32, (TOK, TOK), 0) <= lax.broadcasted_iota(
        jnp.int32, (TOK, TOK), 1
    )
    for copy in loads[1:]:
        copy.wait()
    kt_own[...] = ko_ref[...].astype(F32).T.astype(BF16)
    dqt[...] = jnp.zeros_like(dqt)
    sweep_one(ko_ref[...], vo_ref[...], s_own, p_own, tri, True)

    @pl.when(last)
    def _():
        assemble(False)

    @pl.when(z > 0)
    def _():
        r = lax.broadcasted_iota(jnp.int32, (GROUP, TOK), 0)
        mask = (r < MAIN * z) | ((r >= REM0) & (r < REM0 + REM * z))
        sweep_one(grp[x, :, 0:HD], grp[x, :, HD:W2], s_all.at[x], p_all.at[x], mask, False)

    def full_group(i, carry):
        d = jnp.where(last & (i > 1), 5 - i, i)
        g = x - d
        xcopy(-d, g).wait_recv()
        sweep_one(grp[g, :, 0:HD], grp[g, :, HD:W2], s_all.at[g], p_all.at[g], None, False)
        return carry

    lax.fori_loop(1, x + 1, full_group, 0)

    d_ref[...] = d_ref[...] / l_ref[...]
    m_ref[...] = m_ref[...] + jnp.log2(l_ref[...])

    pieces = (pl.ds(0, HALF), pl.ds(HALF, GROUP - HALF))

    def hop(g, piece, slot, peer_x):
        return pltpu.make_async_remote_copy(
            src_ref=part.at[g, pieces[piece]],
            dst_ref=xback.at[slot, pieces[piece]],
            send_sem=xbs.at[g, piece],
            recv_sem=xbr.at[slot, piece],
            device_id={"seg": peer_x * NZ + z},
            device_id_type=MESH,
        )

    def hop_out(g, piece):
        around = last & ((g == 0) | ((g == 1) & (piece == 1)))
        slot = jnp.where(around, NX - 1 + g, g)
        up = (x == 2) & (g == 0)
        return hop(g, piece, slot, jnp.where(around, 0, jnp.where(up, NX - 1, x - 1)))

    def hop_add(piece, slot, peer_x):
        hop(0, piece, slot, peer_x).wait_recv()
        rows_in = pieces[piece]
        acc[rows_in, :] += xback[slot, rows_in, :].astype(F32)

    def back_group(i, carry):
        g = jnp.where(last & (i < x), lax.rem(i + 1, x + (x == 0)), i)
        kt[...] = grp[g, :, 0:HD].astype(F32).T.astype(BF16)
        dk, dv = sweep_two(s_all.at[g], p_all.at[g], kt)
        acc[:, 0:HD] = dk
        acc[:, HD:W2] = dv

        @pl.when(g < x)
        def _():
            for piece in range(2):

                @pl.when(last & (g == 0))
                def _(piece=piece):
                    hop_add(piece, 0, 2)

                if piece == 0:

                    @pl.when((x == 2) & (g == 1))
                    def _():
                        hop_add(0, 1, NX - 1)

                part[g, pieces[piece], :] = acc[pieces[piece], :].astype(BF16)
                hop_out(g, piece).start()

        return carry

    lax.fori_loop(0, x + jnp.minimum(z, 1), back_group, 0)

    @pl.when(z == 0)
    def _():
        acc[...] = jnp.zeros_like(acc)

    def zmain_copy(source, target):
        return pltpu.make_async_remote_copy(
            src_ref=zmain.at[target],
            dst_ref=zback.at[source],
            send_sem=zbs.at[0, target],
            recv_sem=zbr.at[0, source],
            device_id={"seg": x * NZ + target},
            device_id_type=MESH,
        )

    def zrem_copy(source, target):
        return pltpu.make_async_remote_copy(
            src_ref=zrem.at[target],
            dst_ref=zback_rem.at[source],
            send_sem=zbs.at[1, target],
            recv_sem=zbr.at[1, source],
            device_id={"seg": x * NZ + target},
            device_id_type=MESH,
        )

    def sends(source, target):
        return (source != target) & (jnp.logical_not(last) | (target < source))

    def relay():
        return pltpu.make_async_remote_copy(
            src_ref=xback.at[NX, pieces[1]],
            dst_ref=xback.at[NX, pieces[1]],
            send_sem=xbs.at[1, 1],
            recv_sem=xbr.at[NX, 1],
            device_id={"seg": NZ + z},
            device_id_type=MESH,
        )

    @pl.when(x == 0)
    def _():
        hop(1, 1, NX, NX - 1).wait_recv()
        relay().start()

    for piece in range(2):

        @pl.when(x == 0)
        def _(piece=piece):
            hop_add(piece, 0, 1)
            hop_add(piece, NX - 1, NX - 1)

        @pl.when(x == 1)
        def _(piece=piece):
            hop_add(piece, 1, 2)
            if piece == 1:
                hop_add(1, NX, 0)

        @pl.when(x == 2)
        def _(piece=piece):
            hop_add(piece, 2, NX - 1)

        for i in range(piece * NZ // 2, (piece + 1) * NZ // 2):
            zmain[i] = acc[i * MAIN : (i + 1) * MAIN, :].astype(BF16)

            @pl.when(sends(z, i))
            def _(i=i):
                zmain_copy(z, i).start()

    for i in range(NZ):
        zrem[i] = acc[REM0 + REM * i : REM0 + REM * (i + 1), :].astype(BF16)

        @pl.when(sends(z, i))
        def _(i=i):
            zrem_copy(z, i).start()

    dk, dv = sweep_two(s_own, p_own, kt_own)
    dko_ref[...] = dk.astype(BF16)
    dvo_ref[...] = dv.astype(BF16)
    for h in range(HEADS):
        dq_ref[:, h * HD : (h + 1) * HD] = (dqt[:, lanes(h)] * SCALE).T.astype(BF16)
    stores = [
        pltpu.make_async_copy(src, dst, outsem.at[i])
        for i, (src, dst) in enumerate(((dq_ref, dq_hbm), (dko_ref, dko_hbm), (dvo_ref, dvo_hbm)))
    ]
    for copy in stores:
        copy.start()

    acc[0:MAIN, :] = zmain[z].astype(F32)
    acc[MAIN:M, :] = zrem[z].astype(F32)
    for i in range(NZ):

        @pl.when(sends(i, z))
        def _(i=i):
            zmain_copy(i, z).wait_recv()
            acc[0:MAIN, :] += zback[i].astype(F32)

    for i in range(NZ):

        @pl.when(sends(i, z))
        def _(i=i):
            zrem_copy(i, z).wait_recv()
            acc[MAIN:M, :] += zback_rem[i].astype(F32)

    em[0:MAIN, :] = acc[0:MAIN, :].astype(BF16)
    em[MAIN:BLOCK, :] = jnp.where(
        row == 0, acc[MAIN : MAIN + 1, :], jnp.where(row == 1, acc[MAIN + 1 : M, :], 0.0)
    ).astype(BF16)

    def ecopy():
        return pltpu.make_async_remote_copy(
            src_ref=em,
            dst_ref=etwin,
            send_sem=es,
            recv_sem=er,
            device_id={"tp": twin},
            device_id_type=MESH,
        )

    ecopy().start()
    order = (2, 1, 3, 0)
    for d in order:
        target = y_peer(d)[1]
        chunk = pl.ds(pl.multiple_of(target * cols, cols), cols)
        state[d] = dot(em[...], w[chunk, :], LAST)
    for i in range(NY):
        wcopy(i).wait_recv()
    ecopy().wait_recv()

    half = cols // 2
    lo, hi = slice(0, half), slice(half, cols)
    below, above = y_peer(NY - 1)[1], y_peer(1)[1]
    targets = (below, above, below, below, above, above)
    sources = (above, below, above, above, below, below)

    def tcopy(i, target):
        return pltpu.make_async_remote_copy(
            src_ref=tsend.at[i],
            dst_ref=trecv.at[i],
            send_sem=ts.at[i],
            recv_sem=tr.at[i],
            device_id={"tp": target},
            device_id_type=MESH,
        )

    def put(i, value):
        tsend[i] = value.astype(BF16)
        tcopy(i, targets[i]).start()

    def take(i):
        tcopy(i, sources[i]).wait_recv()
        return trecv[i].astype(F32)

    def both(d):
        return (state[d] + dot(etwin[...], wtwin[y_peer(d)[0]], LAST))[0:M]

    value = both(2)
    put(0, value[:, lo])
    put(1, value[:, hi])
    value = both(NY - 1)
    put(3, value[:, hi])
    state[NY - 1, 0:M, :] = value
    value = both(1)
    put(4, value[:, lo])
    state[1, 0:M, :] = value
    state[0, 0:M, :] = both(0) + sg_ref[...].astype(F32)
    put(2, state[NY - 1, 0:M, lo] + take(0))
    put(5, state[1, 0:M, hi] + take(1))
    out_hi = state[0, 0:M, hi] + take(3)
    out_lo = state[0, 0:M, lo] + take(4)
    out_ref[:, lo] = (out_lo + take(2)).astype(BF16)
    out_ref[:, hi] = (out_hi + take(5)).astype(BF16)

    for copy in stores:
        copy.wait()
    for d in range(1, NZ):
        other, peer = z_peer(x, z, d)

        @pl.when(jnp.logical_not(last) | (other > z))
        def _(d=d, peer=peer):
            for copy in zcopies(d, peer, z):
                copy.wait_send()

    for i in range(NZ):

        @pl.when(sends(z, i))
        def _(i=i):
            zmain_copy(z, i).wait_send()
            zrem_copy(z, i).wait_send()

    lax.fori_loop(1, NX - x, lambda d, c: (xcopy(d, x).wait_send(), c)[1], 0)
    for piece in range(2):
        lax.fori_loop(0, x, lambda g, c: (hop_out(g, piece).wait_send(), c)[1], 0)
    for i in range(NY):
        wcopy(i).wait_send()
    ecopy().wait_send()
    @pl.when(x == 0)
    def _():
        relay().wait_send()

    for i in range(len(targets)):
        tcopy(i, targets[i]).wait_send()


def emit_kernel(count, *refs):
    ins, outs, bufs = refs[:count], refs[count : 2 * count], refs[2 * count : 3 * count]
    sems = refs[3 * count]
    loads = [pltpu.make_async_copy(ins[i], bufs[i], sems.at[0, i]) for i in range(count)]
    stores = [pltpu.make_async_copy(bufs[i], outs[i], sems.at[1, i]) for i in range(count)]
    for copy in loads:
        copy.start()
    for load, store in zip(loads, stores):
        load.wait()
        store.start()
    for copy in stores:
        copy.wait()


def emit(arrays):
    anywhere = pl.BlockSpec(memory_space=pl.ANY)
    count = len(arrays)
    return pl.pallas_call(
        functools.partial(emit_kernel, count),
        name="emit",
        out_shape=tuple(jax.ShapeDtypeStruct(a.shape, a.dtype) for a in arrays),
        in_specs=[anywhere] * count,
        out_specs=(anywhere,) * count,
        scratch_shapes=[pltpu.VMEM(a.shape, a.dtype) for a in arrays]
        + [pltpu.SemaphoreType.DMA((2, count))],
    )(*arrays)


def per_device(
    queries, keys_own, values_own, out_grad, summary_states, w_key, w_value, summary_grad
):
    anywhere = pl.BlockSpec(memory_space=pl.ANY)
    rows = HEADS * TOK
    cols = D // NTP
    dma = pltpu.SemaphoreType.DMA
    arrays = pl.pallas_call(
        layer_kernel,
        name="layer",
        out_shape=(
            jax.ShapeDtypeStruct((TOK, HEADS * HD), BF16),
            jax.ShapeDtypeStruct((TOK, HD), BF16),
            jax.ShapeDtypeStruct((TOK, HD), BF16),
            jax.ShapeDtypeStruct((M, cols), BF16),
        ),
        in_specs=[anywhere] * 8,
        out_specs=(anywhere,) * 3 + (pl.BlockSpec(memory_space=pltpu.VMEM),),
        scratch_shapes=[
            pltpu.VMEM((TOK, HEADS * HD), BF16),
            pltpu.VMEM((TOK, HEADS * HD), BF16),
            pltpu.VMEM((TOK, HD), BF16),
            pltpu.VMEM((TOK, HD), BF16),
            pltpu.VMEM((M, D), BF16),
            pltpu.VMEM((D, W2), BF16),
            pltpu.VMEM((M, cols), BF16),
            pltpu.VMEM((MAIN, W2), BF16),
            pltpu.VMEM((REM, W2), BF16),
            pltpu.VMEM((NZ, REM, W2), BF16),
            pltpu.VMEM((NX, GROUP, W2), BF16),
            pltpu.VMEM((TOK, rows), F32),
            pltpu.VMEM((TOK, rows), F32),
            pltpu.VMEM((NX, GROUP, rows), F32),
            pltpu.VMEM((NX, GROUP, rows), F32),
            pltpu.VMEM((1, rows), F32),
            pltpu.VMEM((1, rows), F32),
            pltpu.VMEM((1, rows), F32),
            pltpu.VMEM((HD, rows), F32),
            pltpu.VMEM((HD, TOK), BF16),
            pltpu.VMEM((HD, GROUP), BF16),
            pltpu.VMEM((GROUP, HD), F32),
            pltpu.VMEM((GROUP, HD), F32),
            pltpu.VMEM((NX, GROUP, W2), BF16),
            pltpu.VMEM((NX + 1, GROUP, W2), BF16),
            pltpu.VMEM((GROUP, W2), F32),
            pltpu.VMEM((NZ, MAIN, W2), BF16),
            pltpu.VMEM((NZ, REM, W2), BF16),
            pltpu.VMEM((NZ, MAIN, W2), BF16),
            pltpu.VMEM((NZ, REM, W2), BF16),
            pltpu.VMEM((BLOCK, W2), BF16),
            pltpu.VMEM((BLOCK, W2), BF16),
            pltpu.VMEM((NY, cols, W2), BF16),
            pltpu.VMEM((NY, BLOCK, cols), F32),
            pltpu.VMEM((6, M, cols // 2), BF16),
            pltpu.VMEM((6, M, cols // 2), BF16),
            pltpu.VMEM((TOK, HEADS * HD), BF16),
            pltpu.VMEM((TOK, HD), BF16),
            pltpu.VMEM((TOK, HD), BF16),
            dma((WCHUNK, 2)),
            dma((6,)),
            dma((3,)),
            dma((2, NZ - 1)),
            dma((2, NZ - 1)),
            dma((NX - 1,)),
            dma((NX - 1,)),
            dma((NX - 1, 2)),
            dma((NX + 1, 2)),
            dma((2, NZ)),
            dma((2, NZ)),
            dma((6,)),
            dma((6,)),
            dma((NY,)),
            dma((NY,)),
            dma,
            dma,
        ],
        compiler_params=pltpu.CompilerParams(
            collective_id=0, has_side_effects=True, vmem_limit_bytes=58 << 20
        ),
    )(
        queries, out_grad, keys_own, values_own, summary_states, w_key, w_value, summary_grad
    )
    return emit(arrays)


def solution(mesh):
    placed = (
        P("seg", "tp"),
        P("seg", "tp"),
        P("seg", "tp"),
        P("seg", "tp"),
        P("seg", None),
        P(None, "tp"),
        P(None, "tp"),
        P("seg", "tp"),
    )
    return jax.shard_map(
        per_device,
        mesh=mesh,
        in_specs=placed,
        out_specs=(P("seg", "tp"), P("seg", "tp"), P("seg", "tp"), P("seg", "tp")),
        check_vma=False,
    )
```

```python
import functools
import math

import jax
import jax.numpy as jnp
from jax import lax
from jax.experimental import pallas as pl
from jax.experimental.pallas import tpu as pltpu
from jax.sharding import PartitionSpec as P

HD = 128
HEADS = 8
TOK = 256
M = 50
MAIN = 48
REM = M - MAIN
TILE = 16
NX, NZ = 4, 8
NTP = 8
NY = NTP // 2
GROUP = NZ * M
REM0 = NZ * MAIN
BLOCK = MAIN + TILE
PIECES = 4
PAIR = NZ // PIECES
D = 8192
W2 = 2 * HD
SCALE = HD ** (-0.5)
SCALE2 = SCALE * math.log2(math.e)
NEG = -1e30
F32 = jnp.float32
BF16 = jnp.bfloat16
MESH = pl.DeviceIdType.MESH
LAST = (((1,), (1,)), ((), ()))
PLAIN = (((1,), (0,)), ((), ()))
WCHUNK = 4


def dot(a, b, dims=PLAIN):
    return lax.dot_general(a, b, dims, preferred_element_type=F32)


def seg_place():
    seg = lax.axis_index("seg")
    return seg // NZ, lax.rem(seg, NZ)


def z_peer(x, z, d):
    other = lax.rem(z + d, NZ)
    return other, x * NZ + other


def x_peer(x, z, d):
    other = lax.rem(x + d, NX)
    return other, other * NZ + z


def greet(peers):
    barrier = pltpu.get_barrier_semaphore()
    for peer in peers:
        pl.semaphore_signal(barrier, inc=1, device_id=peer, device_id_type=MESH)
    return barrier, len(peers)


def load_weights(wk_hbm, wv_hbm, w, sems):
    rows = D // WCHUNK
    copies = []
    for c in range(WCHUNK):
        part = pl.ds(c * rows, rows)
        for i, src in enumerate((wk_hbm, wv_hbm)):
            copy = pltpu.make_async_copy(
                src.at[part], w.at[part, pl.ds(i * HD, HD)], sems.at[c, i]
            )
            copy.start()
            copies.append(copy)
    return copies


def layer_kernel(
    q_hbm, g_hbm, ko_hbm, vo_hbm, st_hbm, wk_hbm, wv_hbm, sg_hbm,
    dq_hbm, dko_hbm, dvo_hbm, out_ref,
    q_ref, g_ref, ko_ref, vo_ref, st, w, sg_ref,
    mine, mine_rem, zrecv, grp, s_own, p_own, s_all, p_all, m_ref, l_ref, d_ref, dqt, kt_own, kt,
    dk_acc, dv_acc, part, xback, acc, zmain, zrem, zback, zback_rem, em, etwin, wtwin, state, tsend, trecv, dq_ref, dko_ref, dvo_ref,
    wsem, insem, outsem, zs, zr, xs, xr, xbs, xbr, zbs, zbr, ts, tr, ws, wr, es, er,
):
    x, z = seg_place()
    tp = lax.axis_index("tp")
    peers = [{"seg": z_peer(x, z, d)[1]} for d in range(1, NZ)]
    peers += [{"seg": x_peer(x, z, d)[1]} for d in range(1, NX)]
    core = lax.rem(tp, 2)
    y = tp // 2
    twin = tp + 1 - 2 * core

    def y_peer(d):
        other = lax.rem(y + d, NY)
        return other, 2 * other + core

    peers += [{"tp": twin}] + [{"tp": y_peer(d)[1]} for d in range(1, NY)]
    last = x == NX - 1
    barrier, count = greet(peers)

    loads = []
    for i, (src, dst) in enumerate(
        (
            (st_hbm, st),
            (q_hbm, q_ref),
            (ko_hbm, ko_ref),
            (g_hbm, g_ref),
            (vo_hbm, vo_ref),
            (sg_hbm, sg_ref),
        )
    ):
        loads.append(pltpu.make_async_copy(src, dst, insem.at[i]))
    loads[0].start()
    wcopies = load_weights(wk_hbm, wv_hbm, w, wsem)
    for copy in loads[1:]:
        copy.start()

    loads[0].wait()
    rows = D // WCHUNK
    total = jnp.zeros((M, W2), F32)
    for c in range(WCHUNK):
        wcopies[2 * c].wait()
        wcopies[2 * c + 1].wait()
        chunk = pl.ds(c * rows, rows)
        total = total + dot(st[:, chunk], w[chunk, :])
    mine[...] = total[0:MAIN].astype(BF16)
    mine_rem[...] = total[MAIN:M].astype(BF16)
    row = lax.broadcasted_iota(jnp.int32, (TILE, W2), 0)
    pl.semaphore_wait(barrier, count)

    def rows_of(i):
        return pl.ds(pl.multiple_of(i * MAIN, TILE), MAIN)

    def zcopies(d, peer, slot):
        own = {"device_id": {"seg": peer}, "device_id_type": MESH}
        return (
            pltpu.make_async_remote_copy(
                src_ref=mine,
                dst_ref=grp.at[x, rows_of(slot)],
                send_sem=zs.at[0, d - 1],
                recv_sem=zr.at[0, d - 1],
                **own,
            ),
            pltpu.make_async_remote_copy(
                src_ref=mine_rem,
                dst_ref=zrecv.at[slot],
                send_sem=zs.at[1, d - 1],
                recv_sem=zr.at[1, d - 1],
                **own,
            ),
        )

    near = (1, 7, 2, 6, 3, 5, 4)
    for d in near:
        other, peer = z_peer(x, z, d)

        @pl.when(jnp.logical_not(last) | (other > z))
        def _(d=d, peer=peer):
            for copy in zcopies(d, peer, z):
                copy.start()

    def xcopy(d, g, part_rows=None):
        other = lax.rem(x + d + NX, NX)
        ref = grp.at[g] if part_rows is None else grp.at[g, part_rows]
        return pltpu.make_async_remote_copy(
            src_ref=ref,
            dst_ref=ref,
            send_sem=xs.at[jnp.abs(d) - 1],
            recv_sem=xr.at[jnp.abs(d) - 1],
            device_id={"seg": other * NZ + z},
            device_id_type=MESH,
        )

    def pass_on(part_rows):
        for d in (3, 1, 2):
            @pl.when((x + d < NX) & ((x > 0) | (d != 2)))
            def _(d=d):
                xcopy(d, x, part_rows).start()

    grp[x, rows_of(z), :] = mine[...]
    pass_on(rows_of(z))

    def assemble(sent_on):
        def place_rem(ref, i):
            two = ref.astype(F32)
            acc[0:TILE, :] = jnp.where(
                row == REM * i,
                two[0:1],
                jnp.where(row == REM * i + 1, two[1:2], acc[0:TILE, :]),
            )

        acc[0:TILE, :] = jnp.zeros((TILE, W2), F32)
        place_rem(mine_rem[...], z)
        for d in near:
            other, peer = z_peer(x, z, NZ - d)
            if sent_on:
                zcopies(d, peer, other)[0].wait_recv()
                pass_on(rows_of(other))
            else:

                @pl.when(other < z)
                def _(d=d, other=other, peer=peer):
                    zcopies(d, peer, other)[0].wait_recv()

                @pl.when(other > z)
                def _(other=other):
                    grp[x, rows_of(other), :] = jnp.zeros((MAIN, W2), BF16)

        for d in near:
            other, peer = z_peer(x, z, NZ - d)

            @pl.when(jnp.bool_(sent_on) | (other < z))
            def _(d=d, other=other, peer=peer):
                zcopies(d, peer, other)[1].wait_recv()
                place_rem(zrecv[other], other)

        grp[x, REM0:GROUP, :] = acc[0:TILE, :].astype(BF16)
        if sent_on:
            pass_on(pl.ds(REM0, TILE))

            @pl.when(x == 0)
            def _():
                xcopy(2, x).start()

    @pl.when(jnp.logical_not(last))
    def _():
        assemble(True)

    cols = D // NTP

    def wcopy(i):
        rows_out = pl.ds(pl.multiple_of((2 * i + 1 - core) * cols, cols), cols)
        return pltpu.make_async_remote_copy(
            src_ref=w.at[rows_out],
            dst_ref=wtwin.at[i],
            send_sem=ws.at[i],
            recv_sem=wr.at[i],
            device_id={"tp": twin},
            device_id_type=MESH,
        )

    for i in range(NY):
        wcopy(i).start()

    def head(ref, h):
        return ref[:, h * HD : (h + 1) * HD]

    def lanes(h):
        return slice(h * TOK, (h + 1) * TOK)

    def sweep_one(keys, vals, s_ref, p_ref, mask, first):
        for h in range(HEADS):
            s = dot(keys, head(q_ref, h), LAST) * SCALE2
            if mask is not None:
                s = jnp.where(mask, s, NEG)
            s_ref[:, lanes(h)] = s
            top = jnp.max(s, axis=0, keepdims=True)
            p = dot(vals, head(g_ref, h), LAST)
            p_ref[:, lanes(h)] = p
            if not first:
                old = m_ref[:, lanes(h)]
                top = jnp.maximum(old, top)
            e = jnp.exp2(s - top)
            total = jnp.sum(e, axis=0, keepdims=True)
            inner = jnp.sum(e * p, axis=0, keepdims=True)
            if not first:
                fade = jnp.exp2(old - top)
                total = total + l_ref[:, lanes(h)] * fade
                inner = inner + d_ref[:, lanes(h)] * fade
            m_ref[:, lanes(h)] = top
            l_ref[:, lanes(h)] = total
            d_ref[:, lanes(h)] = inner

    def sweep_two(s_ref, p_ref, keys_t):
        count = s_ref.shape[0]
        dk = dk_acc.at[0:count]
        dv = dv_acc.at[0:count]
        for h in range(HEADS):
            probs = jnp.exp2(s_ref[:, lanes(h)] - m_ref[:, lanes(h)])
            ds = (probs * (p_ref[:, lanes(h)] - d_ref[:, lanes(h)])).astype(BF16)
            dv_new = dot(probs.astype(BF16), head(g_ref, h))
            dk_new = dot(ds, head(q_ref, h))
            if h:
                dv[...] += dv_new
                dk[...] += dk_new
            else:
                dv[...] = dv_new
                dk[...] = dk_new
            dqt[:, lanes(h)] += dot(keys_t[...], ds)
        return dk[...] * SCALE, dv[...]

    tri = lax.broadcasted_iota(jnp.int32, (TOK, TOK), 0) <= lax.broadcasted_iota(
        jnp.int32, (TOK, TOK), 1
    )
    for copy in loads[1:]:
        copy.wait()
    kt_own[...] = ko_ref[...].astype(F32).T.astype(BF16)
    dqt[...] = jnp.zeros_like(dqt)
    sweep_one(ko_ref[...], vo_ref[...], s_own, p_own, tri, True)

    @pl.when(last)
    def _():
        assemble(False)

    @pl.when(z > 0)
    def _():
        r = lax.broadcasted_iota(jnp.int32, (GROUP, TOK), 0)
        mask = (r < MAIN * z) | ((r >= REM0) & (r < REM0 + REM * z))
        sweep_one(grp[x, :, 0:HD], grp[x, :, HD:W2], s_all.at[x], p_all.at[x], mask, False)

    def full_group(i, carry):
        d = jnp.where(last & (i > 1), 5 - i, i)
        g = x - d
        xcopy(-d, g).wait_recv()
        sweep_one(grp[g, :, 0:HD], grp[g, :, HD:W2], s_all.at[g], p_all.at[g], None, False)
        return carry

    lax.fori_loop(1, x + 1, full_group, 0)

    d_ref[...] = d_ref[...] / l_ref[...]
    m_ref[...] = m_ref[...] + jnp.log2(l_ref[...])

    step = PAIR * MAIN
    pieces = [pl.ds(p * step, step) for p in range(PIECES - 1)]
    pieces.append(pl.ds((PIECES - 1) * step, GROUP - (PIECES - 1) * step))
    split = PIECES // 2

    def hop(g, piece, slot, peer_x):
        return pltpu.make_async_remote_copy(
            src_ref=part.at[g, pieces[piece]],
            dst_ref=xback.at[slot, pieces[piece]],
            send_sem=xbs.at[g, piece],
            recv_sem=xbr.at[slot, piece],
            device_id={"seg": peer_x * NZ + z},
            device_id_type=MESH,
        )

    def hop_out(g, piece):
        around = last & ((g == 0) | ((g == 1) & (piece >= split)))
        slot = jnp.where(around, NX - 1 + g, g)
        up = (x == 2) & (g == 0)
        return hop(g, piece, slot, jnp.where(around, 0, jnp.where(up, NX - 1, x - 1)))

    def hop_add(piece, slot, peer_x):
        hop(0, piece, slot, peer_x).wait_recv()
        rows_in = pieces[piece]
        acc[rows_in, :] += xback[slot, rows_in, :].astype(F32)

    def back_group(i, carry):
        g = jnp.where(last & (i < x), lax.rem(i + 1, x + (x == 0)), i)
        kt[...] = grp[g, :, 0:HD].astype(F32).T.astype(BF16)
        dk, dv = sweep_two(s_all.at[g], p_all.at[g], kt)
        acc[:, 0:HD] = dk
        acc[:, HD:W2] = dv

        @pl.when(g < x)
        def _():
            def put(piece):
                part[g, pieces[piece], :] = acc[pieces[piece], :].astype(BF16)
                hop_out(g, piece).start()

            joined = (x == 2) & (g == 1)
            for piece in range(split, PIECES):

                @pl.when(joined)
                def _(piece=piece):
                    put(piece)

            for piece in range(PIECES):

                @pl.when(last & (g == 0))
                def _(piece=piece):
                    hop_add(piece, 0, 2)

                if piece < split:

                    @pl.when(joined)
                    def _(piece=piece):
                        hop_add(piece, 1, NX - 1)

                @pl.when(jnp.logical_not(joined) | (piece < split))
                def _(piece=piece):
                    put(piece)

        return carry

    lax.fori_loop(0, x + jnp.minimum(z, 1), back_group, 0)

    @pl.when(z == 0)
    def _():
        acc[...] = jnp.zeros_like(acc)

    def zmain_copy(source, target):
        return pltpu.make_async_remote_copy(
            src_ref=zmain.at[target],
            dst_ref=zback.at[source],
            send_sem=zbs.at[0, target],
            recv_sem=zbr.at[0, source],
            device_id={"seg": x * NZ + target},
            device_id_type=MESH,
        )

    def zrem_copy(source, target):
        return pltpu.make_async_remote_copy(
            src_ref=zrem.at[target],
            dst_ref=zback_rem.at[source],
            send_sem=zbs.at[1, target],
            recv_sem=zbr.at[1, source],
            device_id={"seg": x * NZ + target},
            device_id_type=MESH,
        )

    def sends(source, target):
        return (source != target) & (jnp.logical_not(last) | (target < source))

    def relay(piece):
        return pltpu.make_async_remote_copy(
            src_ref=xback.at[NX, pieces[piece]],
            dst_ref=xback.at[NX, pieces[piece]],
            send_sem=xbs.at[1, piece],
            recv_sem=xbr.at[NX, piece],
            device_id={"seg": NZ + z},
            device_id_type=MESH,
        )

    @pl.when(x == 0)
    def _():
        for piece in range(split, PIECES):
            hop(1, piece, NX, NX - 1).wait_recv()
            relay(piece).start()

    for piece in range(PIECES):

        @pl.when(x == 0)
        def _(piece=piece):
            hop_add(piece, 0, 1)
            hop_add(piece, NX - 1, NX - 1)

        @pl.when(x == 1)
        def _(piece=piece):
            hop_add(piece, 1, 2)
            if piece >= split:
                hop_add(piece, NX, 0)

        @pl.when(x == 2)
        def _(piece=piece):
            hop_add(piece, 2, NX - 1)

        for i in range(piece * PAIR, (piece + 1) * PAIR):
            zmain[i] = acc[i * MAIN : (i + 1) * MAIN, :].astype(BF16)

            @pl.when(sends(z, i))
            def _(i=i):
                zmain_copy(z, i).start()

    for i in range(NZ):
        zrem[i] = acc[REM0 + REM * i : REM0 + REM * (i + 1), :].astype(BF16)

        @pl.when(sends(z, i))
        def _(i=i):
            zrem_copy(z, i).start()

    dk, dv = sweep_two(s_own, p_own, kt_own)
    dko_ref[...] = dk.astype(BF16)
    dvo_ref[...] = dv.astype(BF16)
    for h in range(HEADS):
        dq_ref[:, h * HD : (h + 1) * HD] = (dqt[:, lanes(h)] * SCALE).T.astype(BF16)
    stores = [
        pltpu.make_async_copy(src, dst, outsem.at[i])
        for i, (src, dst) in enumerate(((dq_ref, dq_hbm), (dko_ref, dko_hbm), (dvo_ref, dvo_hbm)))
    ]
    for copy in stores:
        copy.start()

    acc[0:MAIN, :] = zmain[z].astype(F32)
    acc[MAIN:M, :] = zrem[z].astype(F32)
    for i in range(NZ):

        @pl.when(sends(i, z))
        def _(i=i):
            zmain_copy(i, z).wait_recv()
            acc[0:MAIN, :] += zback[i].astype(F32)

    for i in range(NZ):

        @pl.when(sends(i, z))
        def _(i=i):
            zrem_copy(i, z).wait_recv()
            acc[MAIN:M, :] += zback_rem[i].astype(F32)

    em[0:MAIN, :] = acc[0:MAIN, :].astype(BF16)
    em[MAIN:BLOCK, :] = jnp.where(
        row == 0, acc[MAIN : MAIN + 1, :], jnp.where(row == 1, acc[MAIN + 1 : M, :], 0.0)
    ).astype(BF16)

    def ecopy():
        return pltpu.make_async_remote_copy(
            src_ref=em,
            dst_ref=etwin,
            send_sem=es,
            recv_sem=er,
            device_id={"tp": twin},
            device_id_type=MESH,
        )

    ecopy().start()
    order = (2, 1, 3, 0)
    for d in order:
        target = y_peer(d)[1]
        chunk = pl.ds(pl.multiple_of(target * cols, cols), cols)
        state[d] = dot(em[...], w[chunk, :], LAST)
    for i in range(NY):
        wcopy(i).wait_recv()
    ecopy().wait_recv()

    half = cols // 2
    lo, hi = slice(0, half), slice(half, cols)
    below, above = y_peer(NY - 1)[1], y_peer(1)[1]
    targets = (below, above, below, below, above, above)
    sources = (above, below, above, above, below, below)

    def tcopy(i, target):
        return pltpu.make_async_remote_copy(
            src_ref=tsend.at[i],
            dst_ref=trecv.at[i],
            send_sem=ts.at[i],
            recv_sem=tr.at[i],
            device_id={"tp": target},
            device_id_type=MESH,
        )

    def put(i, value):
        tsend[i] = value.astype(BF16)
        tcopy(i, targets[i]).start()

    def take(i):
        tcopy(i, sources[i]).wait_recv()
        return trecv[i].astype(F32)

    def both(d):
        return (state[d] + dot(etwin[...], wtwin[y_peer(d)[0]], LAST))[0:M]

    value = both(2)
    put(0, value[:, lo])
    put(1, value[:, hi])
    value = both(NY - 1)
    put(3, value[:, hi])
    state[NY - 1, 0:M, :] = value
    value = both(1)
    put(4, value[:, lo])
    state[1, 0:M, :] = value
    state[0, 0:M, :] = both(0) + sg_ref[...].astype(F32)
    put(2, state[NY - 1, 0:M, lo] + take(0))
    put(5, state[1, 0:M, hi] + take(1))
    out_hi = state[0, 0:M, hi] + take(3)
    out_lo = state[0, 0:M, lo] + take(4)
    out_ref[:, lo] = (out_lo + take(2)).astype(BF16)
    out_ref[:, hi] = (out_hi + take(5)).astype(BF16)

    for copy in stores:
        copy.wait()
    for d in range(1, NZ):
        other, peer = z_peer(x, z, d)

        @pl.when(jnp.logical_not(last) | (other > z))
        def _(d=d, peer=peer):
            for copy in zcopies(d, peer, z):
                copy.wait_send()

    for i in range(NZ):

        @pl.when(sends(z, i))
        def _(i=i):
            zmain_copy(z, i).wait_send()
            zrem_copy(z, i).wait_send()

    lax.fori_loop(1, NX - x, lambda d, c: (xcopy(d, x).wait_send(), c)[1], 0)
    for piece in range(PIECES):
        lax.fori_loop(0, x, lambda g, c: (hop_out(g, piece).wait_send(), c)[1], 0)
    for i in range(NY):
        wcopy(i).wait_send()
    ecopy().wait_send()
    @pl.when(x == 0)
    def _():
        for piece in range(split, PIECES):
            relay(piece).wait_send()

    for i in range(len(targets)):
        tcopy(i, targets[i]).wait_send()


def emit_kernel(count, *refs):
    ins, outs, bufs = refs[:count], refs[count : 2 * count], refs[2 * count : 3 * count]
    sems = refs[3 * count]
    loads = [pltpu.make_async_copy(ins[i], bufs[i], sems.at[0, i]) for i in range(count)]
    stores = [pltpu.make_async_copy(bufs[i], outs[i], sems.at[1, i]) for i in range(count)]
    for copy in loads:
        copy.start()
    for load, store in zip(loads, stores):
        load.wait()
        store.start()
    for copy in stores:
        copy.wait()


def emit(arrays):
    anywhere = pl.BlockSpec(memory_space=pl.ANY)
    count = len(arrays)
    return pl.pallas_call(
        functools.partial(emit_kernel, count),
        name="emit",
        out_shape=tuple(jax.ShapeDtypeStruct(a.shape, a.dtype) for a in arrays),
        in_specs=[anywhere] * count,
        out_specs=(anywhere,) * count,
        scratch_shapes=[pltpu.VMEM(a.shape, a.dtype) for a in arrays]
        + [pltpu.SemaphoreType.DMA((2, count))],
    )(*arrays)


def per_device(
    queries, keys_own, values_own, out_grad, summary_states, w_key, w_value, summary_grad
):
    anywhere = pl.BlockSpec(memory_space=pl.ANY)
    rows = HEADS * TOK
    cols = D // NTP
    dma = pltpu.SemaphoreType.DMA
    arrays = pl.pallas_call(
        layer_kernel,
        name="layer",
        out_shape=(
            jax.ShapeDtypeStruct((TOK, HEADS * HD), BF16),
            jax.ShapeDtypeStruct((TOK, HD), BF16),
            jax.ShapeDtypeStruct((TOK, HD), BF16),
            jax.ShapeDtypeStruct((M, cols), BF16),
        ),
        in_specs=[anywhere] * 8,
        out_specs=(anywhere,) * 3 + (pl.BlockSpec(memory_space=pltpu.VMEM),),
        scratch_shapes=[
            pltpu.VMEM((TOK, HEADS * HD), BF16),
            pltpu.VMEM((TOK, HEADS * HD), BF16),
            pltpu.VMEM((TOK, HD), BF16),
            pltpu.VMEM((TOK, HD), BF16),
            pltpu.VMEM((M, D), BF16),
            pltpu.VMEM((D, W2), BF16),
            pltpu.VMEM((M, cols), BF16),
            pltpu.VMEM((MAIN, W2), BF16),
            pltpu.VMEM((REM, W2), BF16),
            pltpu.VMEM((NZ, REM, W2), BF16),
            pltpu.VMEM((NX, GROUP, W2), BF16),
            pltpu.VMEM((TOK, rows), F32),
            pltpu.VMEM((TOK, rows), F32),
            pltpu.VMEM((NX, GROUP, rows), F32),
            pltpu.VMEM((NX, GROUP, rows), F32),
            pltpu.VMEM((1, rows), F32),
            pltpu.VMEM((1, rows), F32),
            pltpu.VMEM((1, rows), F32),
            pltpu.VMEM((HD, rows), F32),
            pltpu.VMEM((HD, TOK), BF16),
            pltpu.VMEM((HD, GROUP), BF16),
            pltpu.VMEM((GROUP, HD), F32),
            pltpu.VMEM((GROUP, HD), F32),
            pltpu.VMEM((NX, GROUP, W2), BF16),
            pltpu.VMEM((NX + 1, GROUP, W2), BF16),
            pltpu.VMEM((GROUP, W2), F32),
            pltpu.VMEM((NZ, MAIN, W2), BF16),
            pltpu.VMEM((NZ, REM, W2), BF16),
            pltpu.VMEM((NZ, MAIN, W2), BF16),
            pltpu.VMEM((NZ, REM, W2), BF16),
            pltpu.VMEM((BLOCK, W2), BF16),
            pltpu.VMEM((BLOCK, W2), BF16),
            pltpu.VMEM((NY, cols, W2), BF16),
            pltpu.VMEM((NY, BLOCK, cols), F32),
            pltpu.VMEM((6, M, cols // 2), BF16),
            pltpu.VMEM((6, M, cols // 2), BF16),
            pltpu.VMEM((TOK, HEADS * HD), BF16),
            pltpu.VMEM((TOK, HD), BF16),
            pltpu.VMEM((TOK, HD), BF16),
            dma((WCHUNK, 2)),
            dma((6,)),
            dma((3,)),
            dma((2, NZ - 1)),
            dma((2, NZ - 1)),
            dma((NX - 1,)),
            dma((NX - 1,)),
            dma((NX - 1, PIECES)),
            dma((NX + 1, PIECES)),
            dma((2, NZ)),
            dma((2, NZ)),
            dma((6,)),
            dma((6,)),
            dma((NY,)),
            dma((NY,)),
            dma,
            dma,
        ],
        compiler_params=pltpu.CompilerParams(
            collective_id=0, has_side_effects=True, vmem_limit_bytes=58 << 20
        ),
    )(
        queries, out_grad, keys_own, values_own, summary_states, w_key, w_value, summary_grad
    )
    return emit(arrays)


def solution(mesh):
    placed = (
        P("seg", "tp"),
        P("seg", "tp"),
        P("seg", "tp"),
        P("seg", "tp"),
        P("seg", None),
        P(None, "tp"),
        P(None, "tp"),
        P("seg", "tp"),
    )
    return jax.shard_map(
        per_device,
        mesh=mesh,
        in_specs=placed,
        out_specs=(P("seg", "tp"), P("seg", "tp"), P("seg", "tp"), P("seg", "tp")),
        check_vma=False,
    )
```

```python
import functools
import math

import jax
import jax.numpy as jnp
from jax import lax
from jax.experimental import pallas as pl
from jax.experimental.pallas import tpu as pltpu
from jax.sharding import PartitionSpec as P

HD = 128
HEADS = 8
TOK = 256
M = 50
MAIN = 48
REM = M - MAIN
TILE = 16
NX, NZ = 4, 8
NTP = 8
NY = NTP // 2
GROUP = NZ * M
REM0 = NZ * MAIN
BLOCK = MAIN + TILE
PIECES = 4
PAIR = NZ // PIECES
D = 8192
W2 = 2 * HD
SCALE = HD ** (-0.5)
SCALE2 = SCALE * math.log2(math.e)
NEG = -1e30
F32 = jnp.float32
BF16 = jnp.bfloat16
MESH = pl.DeviceIdType.MESH
LAST = (((1,), (1,)), ((), ()))
PLAIN = (((1,), (0,)), ((), ()))
WCHUNK = 4


def dot(a, b, dims=PLAIN):
    return lax.dot_general(a, b, dims, preferred_element_type=F32)


def seg_place():
    seg = lax.axis_index("seg")
    return seg // NZ, lax.rem(seg, NZ)


def z_peer(x, z, d):
    other = lax.rem(z + d, NZ)
    return other, x * NZ + other


def x_peer(x, z, d):
    other = lax.rem(x + d, NX)
    return other, other * NZ + z


def greet(peers):
    barrier = pltpu.get_barrier_semaphore()
    for peer in peers:
        pl.semaphore_signal(barrier, inc=1, device_id=peer, device_id_type=MESH)
    return barrier, len(peers)


def load_weights(wk_hbm, wv_hbm, w, sems):
    rows = D // WCHUNK
    copies = []
    for c in range(WCHUNK):
        part = pl.ds(c * rows, rows)
        for i, src in enumerate((wk_hbm, wv_hbm)):
            copy = pltpu.make_async_copy(
                src.at[part], w.at[part, pl.ds(i * HD, HD)], sems.at[c, i]
            )
            copy.start()
            copies.append(copy)
    return copies


def layer_kernel(
    q_hbm, g_hbm, ko_hbm, vo_hbm, st_hbm, wk_hbm, wv_hbm, sg_hbm,
    dq_hbm, dko_hbm, dvo_hbm, out_ref,
    q_ref, g_ref, ko_ref, vo_ref, st, w, sg_ref,
    mine, mine_rem, zrecv, grp, s_own, p_own, s_all, p_all, m_ref, l_ref, d_ref, dqt, kt_own, kt,
    dk_acc, dv_acc, part, xback, acc, zmain, zrem, zback, zback_rem, em, etwin, wtwin, state, tsend, trecv, dq_ref, dko_ref, dvo_ref,
    wsem, insem, outsem, zs, zr, xs, xr, xbs, xbr, zbs, zbr, ts, tr, ws, wr, es, er, gs, gin,
):
    x, z = seg_place()
    tp = lax.axis_index("tp")
    peers = [{"seg": z_peer(x, z, d)[1]} for d in range(1, NZ)]
    peers += [{"seg": x_peer(x, z, d)[1]} for d in range(1, NX)]
    core = lax.rem(tp, 2)
    y = tp // 2
    twin = tp + 1 - 2 * core

    def y_peer(d):
        other = lax.rem(y + d, NY)
        return other, 2 * other + core

    peers += [{"tp": twin}] + [{"tp": y_peer(d)[1]} for d in range(1, NY)]
    last = x == NX - 1
    barrier, count = greet(peers)

    loads = []
    for i, (src, dst) in enumerate(
        (
            (st_hbm, st),
            (q_hbm, q_ref),
            (ko_hbm, ko_ref),
            (g_hbm, g_ref),
            (vo_hbm, vo_ref),
            (sg_hbm, sg_ref),
        )
    ):
        loads.append(pltpu.make_async_copy(src, dst, insem.at[i]))
    loads[0].start()
    wcopies = load_weights(wk_hbm, wv_hbm, w, wsem)
    for copy in loads[1:]:
        copy.start()

    loads[0].wait()
    rows = D // WCHUNK
    total = jnp.zeros((M, W2), F32)
    for c in range(WCHUNK):
        wcopies[2 * c].wait()
        wcopies[2 * c + 1].wait()
        chunk = pl.ds(c * rows, rows)
        total = total + dot(st[:, chunk], w[chunk, :])
    mine[...] = total[0:MAIN].astype(BF16)
    mine_rem[...] = total[MAIN:M].astype(BF16)
    row = lax.broadcasted_iota(jnp.int32, (TILE, W2), 0)
    pl.semaphore_wait(barrier, count)

    def rows_of(i):
        return pl.ds(pl.multiple_of(i * MAIN, TILE), MAIN)

    def zcopies(d, peer, slot):
        own = {"device_id": {"seg": peer}, "device_id_type": MESH}
        return (
            pltpu.make_async_remote_copy(
                src_ref=mine,
                dst_ref=grp.at[x, rows_of(slot)],
                send_sem=zs.at[0, d - 1],
                recv_sem=zr.at[0, d - 1],
                **own,
            ),
            pltpu.make_async_remote_copy(
                src_ref=mine_rem,
                dst_ref=zrecv.at[slot],
                send_sem=zs.at[1, d - 1],
                recv_sem=zr.at[1, d - 1],
                **own,
            ),
        )

    near = (1, 7, 2, 6, 3, 5, 4)
    for d in near:
        other, peer = z_peer(x, z, d)

        @pl.when(jnp.logical_not(last) | (other > z))
        def _(d=d, peer=peer):
            for copy in zcopies(d, peer, z):
                copy.start()

    def xcopy(d, g, part_rows=None):
        other = lax.rem(x + d + NX, NX)
        ref = grp.at[g] if part_rows is None else grp.at[g, part_rows]
        return pltpu.make_async_remote_copy(
            src_ref=ref,
            dst_ref=ref,
            send_sem=xs.at[jnp.abs(d) - 1],
            recv_sem=xr.at[jnp.abs(d) - 1],
            device_id={"seg": other * NZ + z},
            device_id_type=MESH,
        )

    near_rows, far_rows = pl.ds(0, REM0 // 2), pl.ds(REM0 // 2, GROUP - REM0 // 2)

    def detour(part_rows, to, send_sem, recv_sem):
        return pltpu.make_async_remote_copy(
            src_ref=grp.at[1, part_rows],
            dst_ref=grp.at[1, part_rows],
            send_sem=send_sem,
            recv_sem=recv_sem,
            device_id={"seg": to * NZ + z},
            device_id_type=MESH,
        )

    def pass_on(part_rows, i=NZ):
        for d in (3, 1, 2):
            direct = (x + d < NX) & ((x > 0) | (d != 2))
            if d == 2:
                direct = direct & (i >= NZ // 2)

            @pl.when(direct)
            def _(d=d):
                xcopy(d, x, part_rows).start()

        @pl.when((x == 1) & (i < NZ // 2))
        def _():
            detour(part_rows, 0, gs.at[0], gin.at[lax.rem(i, NZ)]).start()

    def turn(i):
        @pl.when((x == 0) & (i < NZ // 2))
        def _():
            detour(rows_of(i), 0, gs.at[0], gin.at[i]).wait_recv()
            detour(rows_of(i), NX - 1, gs.at[1], gin.at[NZ]).start()

    grp[x, rows_of(z), :] = mine[...]
    pass_on(rows_of(z), z)

    def assemble(sent_on):
        def place_rem(ref, i):
            two = ref.astype(F32)
            acc[0:TILE, :] = jnp.where(
                row == REM * i,
                two[0:1],
                jnp.where(row == REM * i + 1, two[1:2], acc[0:TILE, :]),
            )

        acc[0:TILE, :] = jnp.zeros((TILE, W2), F32)
        place_rem(mine_rem[...], z)
        passed = [z]
        for d in near:
            other, peer = z_peer(x, z, NZ - d)
            if sent_on:
                zcopies(d, peer, other)[0].wait_recv()
                pass_on(rows_of(other), other)
                passed.append(other)
                if len(passed) > 2:
                    turn(passed[-3])
            else:

                @pl.when(other < z)
                def _(d=d, other=other, peer=peer):
                    zcopies(d, peer, other)[0].wait_recv()

                @pl.when(other > z)
                def _(other=other):
                    grp[x, rows_of(other), :] = jnp.zeros((MAIN, W2), BF16)

        for d in near:
            other, peer = z_peer(x, z, NZ - d)

            @pl.when(jnp.bool_(sent_on) | (other < z))
            def _(d=d, other=other, peer=peer):
                zcopies(d, peer, other)[1].wait_recv()
                place_rem(zrecv[other], other)

        grp[x, REM0:GROUP, :] = acc[0:TILE, :].astype(BF16)
        if sent_on:
            pass_on(pl.ds(REM0, TILE))
            turn(passed[-2])
            turn(passed[-1])

            @pl.when(x == 0)
            def _():
                xcopy(2, x).start()

    @pl.when(jnp.logical_not(last))
    def _():
        assemble(True)

    cols = D // NTP

    def wcopy(i):
        rows_out = pl.ds(pl.multiple_of((2 * i + 1 - core) * cols, cols), cols)
        return pltpu.make_async_remote_copy(
            src_ref=w.at[rows_out],
            dst_ref=wtwin.at[i],
            send_sem=ws.at[i],
            recv_sem=wr.at[i],
            device_id={"tp": twin},
            device_id_type=MESH,
        )

    for i in range(NY):
        wcopy(i).start()

    def head(ref, h):
        return ref[:, h * HD : (h + 1) * HD]

    def lanes(h):
        return slice(h * TOK, (h + 1) * TOK)

    def sweep_one(keys, vals, s_ref, p_ref, mask, first):
        for h in range(HEADS):
            s = dot(keys, head(q_ref, h), LAST) * SCALE2
            if mask is not None:
                s = jnp.where(mask, s, NEG)
            s_ref[:, lanes(h)] = s
            top = jnp.max(s, axis=0, keepdims=True)
            p = dot(vals, head(g_ref, h), LAST)
            p_ref[:, lanes(h)] = p
            if not first:
                old = m_ref[:, lanes(h)]
                top = jnp.maximum(old, top)
            e = jnp.exp2(s - top)
            total = jnp.sum(e, axis=0, keepdims=True)
            inner = jnp.sum(e * p, axis=0, keepdims=True)
            if not first:
                fade = jnp.exp2(old - top)
                total = total + l_ref[:, lanes(h)] * fade
                inner = inner + d_ref[:, lanes(h)] * fade
            m_ref[:, lanes(h)] = top
            l_ref[:, lanes(h)] = total
            d_ref[:, lanes(h)] = inner

    def sweep_two(s_ref, p_ref, keys_t):
        count = s_ref.shape[0]
        dk = dk_acc.at[0:count]
        dv = dv_acc.at[0:count]
        for h in range(HEADS):
            probs = jnp.exp2(s_ref[:, lanes(h)] - m_ref[:, lanes(h)])
            ds = (probs * (p_ref[:, lanes(h)] - d_ref[:, lanes(h)])).astype(BF16)
            dv_new = dot(probs.astype(BF16), head(g_ref, h))
            dk_new = dot(ds, head(q_ref, h))
            if h:
                dv[...] += dv_new
                dk[...] += dk_new
            else:
                dv[...] = dv_new
                dk[...] = dk_new
            dqt[:, lanes(h)] += dot(keys_t[...], ds)
        return dk[...] * SCALE, dv[...]

    tri = lax.broadcasted_iota(jnp.int32, (TOK, TOK), 0) <= lax.broadcasted_iota(
        jnp.int32, (TOK, TOK), 1
    )
    for copy in loads[1:]:
        copy.wait()
    kt_own[...] = ko_ref[...].astype(F32).T.astype(BF16)
    dqt[...] = jnp.zeros_like(dqt)
    sweep_one(ko_ref[...], vo_ref[...], s_own, p_own, tri, True)

    @pl.when(last)
    def _():
        assemble(False)

    @pl.when(z > 0)
    def _():
        r = lax.broadcasted_iota(jnp.int32, (GROUP, TOK), 0)
        mask = (r < MAIN * z) | ((r >= REM0) & (r < REM0 + REM * z))
        sweep_one(grp[x, :, 0:HD], grp[x, :, HD:W2], s_all.at[x], p_all.at[x], mask, False)

    def full_group(i, carry):
        d = jnp.where(last & (i > 1), 5 - i, i)
        g = x - d
        parted = last & (g == 1)

        @pl.when(parted)
        def _():
            xcopy(-2, g, far_rows).wait_recv()
            detour(near_rows, 0, gs.at[0], gin.at[NZ]).wait_recv()

        @pl.when(jnp.logical_not(parted))
        def _():
            xcopy(-d, g).wait_recv()

        sweep_one(grp[g, :, 0:HD], grp[g, :, HD:W2], s_all.at[g], p_all.at[g], None, False)
        return carry

    lax.fori_loop(1, x + 1, full_group, 0)

    d_ref[...] = d_ref[...] / l_ref[...]
    m_ref[...] = m_ref[...] + jnp.log2(l_ref[...])

    step = PAIR * MAIN
    pieces = [pl.ds(p * step, step) for p in range(PIECES - 1)]
    pieces.append(pl.ds((PIECES - 1) * step, GROUP - (PIECES - 1) * step))
    split = PIECES // 2

    def hop(g, piece, slot, peer_x):
        return pltpu.make_async_remote_copy(
            src_ref=part.at[g, pieces[piece]],
            dst_ref=xback.at[slot, pieces[piece]],
            send_sem=xbs.at[g, piece],
            recv_sem=xbr.at[slot, piece],
            device_id={"seg": peer_x * NZ + z},
            device_id_type=MESH,
        )

    def hop_out(g, piece):
        around = last & ((g == 0) | ((g == 1) & (piece >= split)))
        slot = jnp.where(around, NX - 1 + g, g)
        up = (x == 2) & (g == 0)
        return hop(g, piece, slot, jnp.where(around, 0, jnp.where(up, NX - 1, x - 1)))

    def hop_add(piece, slot, peer_x):
        hop(0, piece, slot, peer_x).wait_recv()
        rows_in = pieces[piece]
        acc[rows_in, :] += xback[slot, rows_in, :].astype(F32)

    def back_group(i, carry):
        g = jnp.where(last & (i < x), lax.rem(i + 1, x + (x == 0)), i)
        kt[...] = grp[g, :, 0:HD].astype(F32).T.astype(BF16)
        dk, dv = sweep_two(s_all.at[g], p_all.at[g], kt)
        acc[:, 0:HD] = dk
        acc[:, HD:W2] = dv

        @pl.when(g < x)
        def _():
            def put(piece):
                part[g, pieces[piece], :] = acc[pieces[piece], :].astype(BF16)
                hop_out(g, piece).start()

            joined = (x == 2) & (g == 1)
            for piece in range(split, PIECES):

                @pl.when(joined)
                def _(piece=piece):
                    put(piece)

            for piece in range(PIECES):

                @pl.when(last & (g == 0))
                def _(piece=piece):
                    hop_add(piece, 0, 2)

                if piece < split:

                    @pl.when(joined)
                    def _(piece=piece):
                        hop_add(piece, 1, NX - 1)

                @pl.when(jnp.logical_not(joined) | (piece < split))
                def _(piece=piece):
                    put(piece)

        return carry

    lax.fori_loop(0, x + jnp.minimum(z, 1), back_group, 0)

    @pl.when(z == 0)
    def _():
        acc[...] = jnp.zeros_like(acc)

    def zmain_copy(source, target):
        return pltpu.make_async_remote_copy(
            src_ref=zmain.at[target],
            dst_ref=zback.at[source],
            send_sem=zbs.at[0, target],
            recv_sem=zbr.at[0, source],
            device_id={"seg": x * NZ + target},
            device_id_type=MESH,
        )

    def zrem_copy(source, target):
        return pltpu.make_async_remote_copy(
            src_ref=zrem.at[target],
            dst_ref=zback_rem.at[source],
            send_sem=zbs.at[1, target],
            recv_sem=zbr.at[1, source],
            device_id={"seg": x * NZ + target},
            device_id_type=MESH,
        )

    def sends(source, target):
        return (source != target) & (jnp.logical_not(last) | (target < source))

    def relay(piece):
        return pltpu.make_async_remote_copy(
            src_ref=xback.at[NX, pieces[piece]],
            dst_ref=xback.at[NX, pieces[piece]],
            send_sem=xbs.at[1, piece],
            recv_sem=xbr.at[NX, piece],
            device_id={"seg": NZ + z},
            device_id_type=MESH,
        )

    @pl.when(x == 0)
    def _():
        for piece in range(split, PIECES):
            hop(1, piece, NX, NX - 1).wait_recv()
            relay(piece).start()

    for piece in range(PIECES):

        @pl.when(x == 0)
        def _(piece=piece):
            hop_add(piece, 0, 1)
            hop_add(piece, NX - 1, NX - 1)

        @pl.when(x == 1)
        def _(piece=piece):
            hop_add(piece, 1, 2)
            if piece >= split:
                hop_add(piece, NX, 0)

        @pl.when(x == 2)
        def _(piece=piece):
            hop_add(piece, 2, NX - 1)

        for i in range(piece * PAIR, (piece + 1) * PAIR):
            zmain[i] = acc[i * MAIN : (i + 1) * MAIN, :].astype(BF16)

            @pl.when(sends(z, i))
            def _(i=i):
                zmain_copy(z, i).start()

    for i in range(NZ):
        zrem[i] = acc[REM0 + REM * i : REM0 + REM * (i + 1), :].astype(BF16)

        @pl.when(sends(z, i))
        def _(i=i):
            zrem_copy(z, i).start()

    dk, dv = sweep_two(s_own, p_own, kt_own)
    dko_ref[...] = dk.astype(BF16)
    dvo_ref[...] = dv.astype(BF16)
    for h in range(HEADS):
        dq_ref[:, h * HD : (h + 1) * HD] = (dqt[:, lanes(h)] * SCALE).T.astype(BF16)
    stores = [
        pltpu.make_async_copy(src, dst, outsem.at[i])
        for i, (src, dst) in enumerate(((dq_ref, dq_hbm), (dko_ref, dko_hbm), (dvo_ref, dvo_hbm)))
    ]
    for copy in stores:
        copy.start()

    acc[0:MAIN, :] = zmain[z].astype(F32)
    acc[MAIN:M, :] = zrem[z].astype(F32)
    for i in range(NZ):

        @pl.when(sends(i, z))
        def _(i=i):
            zmain_copy(i, z).wait_recv()
            acc[0:MAIN, :] += zback[i].astype(F32)

    for i in range(NZ):

        @pl.when(sends(i, z))
        def _(i=i):
            zrem_copy(i, z).wait_recv()
            acc[MAIN:M, :] += zback_rem[i].astype(F32)

    em[0:MAIN, :] = acc[0:MAIN, :].astype(BF16)
    em[MAIN:BLOCK, :] = jnp.where(
        row == 0, acc[MAIN : MAIN + 1, :], jnp.where(row == 1, acc[MAIN + 1 : M, :], 0.0)
    ).astype(BF16)

    def ecopy():
        return pltpu.make_async_remote_copy(
            src_ref=em,
            dst_ref=etwin,
            send_sem=es,
            recv_sem=er,
            device_id={"tp": twin},
            device_id_type=MESH,
        )

    ecopy().start()
    order = (2, 1, 3, 0)
    for d in order:
        target = y_peer(d)[1]
        chunk = pl.ds(pl.multiple_of(target * cols, cols), cols)
        state[d] = dot(em[...], w[chunk, :], LAST)
    for i in range(NY):
        wcopy(i).wait_recv()
    ecopy().wait_recv()

    half = cols // 2
    lo, hi = slice(0, half), slice(half, cols)
    below, above = y_peer(NY - 1)[1], y_peer(1)[1]
    targets = (below, above, below, below, above, above)
    sources = (above, below, above, above, below, below)

    def tcopy(i, target):
        return pltpu.make_async_remote_copy(
            src_ref=tsend.at[i],
            dst_ref=trecv.at[i],
            send_sem=ts.at[i],
            recv_sem=tr.at[i],
            device_id={"tp": target},
            device_id_type=MESH,
        )

    def put(i, value):
        tsend[i] = value.astype(BF16)
        tcopy(i, targets[i]).start()

    def take(i):
        tcopy(i, sources[i]).wait_recv()
        return trecv[i].astype(F32)

    def both(d):
        return (state[d] + dot(etwin[...], wtwin[y_peer(d)[0]], LAST))[0:M]

    value = both(2)
    put(0, value[:, lo])
    put(1, value[:, hi])
    value = both(NY - 1)
    put(3, value[:, hi])
    state[NY - 1, 0:M, :] = value
    value = both(1)
    put(4, value[:, lo])
    state[1, 0:M, :] = value
    state[0, 0:M, :] = both(0) + sg_ref[...].astype(F32)
    put(2, state[NY - 1, 0:M, lo] + take(0))
    put(5, state[1, 0:M, hi] + take(1))
    out_hi = state[0, 0:M, hi] + take(3)
    out_lo = state[0, 0:M, lo] + take(4)
    out_ref[:, lo] = (out_lo + take(2)).astype(BF16)
    out_ref[:, hi] = (out_hi + take(5)).astype(BF16)

    for copy in stores:
        copy.wait()
    for d in range(1, NZ):
        other, peer = z_peer(x, z, d)

        @pl.when(jnp.logical_not(last) | (other > z))
        def _(d=d, peer=peer):
            for copy in zcopies(d, peer, z):
                copy.wait_send()

    for i in range(NZ):

        @pl.when(sends(z, i))
        def _(i=i):
            zmain_copy(z, i).wait_send()
            zrem_copy(z, i).wait_send()

    for d in range(1, NX):

        @pl.when((x + d < NX) & ((x != 1) | (d != 2)))
        def _(d=d):
            xcopy(d, x).wait_send()

    @pl.when(x == 1)
    def _():
        xcopy(2, x, far_rows).wait_send()
        detour(near_rows, 0, gs.at[0], gin.at[NZ]).wait_send()

    @pl.when(x == 0)
    def _():
        detour(near_rows, NX - 1, gs.at[1], gin.at[NZ]).wait_send()

    for piece in range(PIECES):
        lax.fori_loop(0, x, lambda g, c: (hop_out(g, piece).wait_send(), c)[1], 0)
    for i in range(NY):
        wcopy(i).wait_send()
    ecopy().wait_send()
    @pl.when(x == 0)
    def _():
        for piece in range(split, PIECES):
            relay(piece).wait_send()

    for i in range(len(targets)):
        tcopy(i, targets[i]).wait_send()


def emit_kernel(count, *refs):
    ins, outs, bufs = refs[:count], refs[count : 2 * count], refs[2 * count : 3 * count]
    sems = refs[3 * count]
    loads = [pltpu.make_async_copy(ins[i], bufs[i], sems.at[0, i]) for i in range(count)]
    stores = [pltpu.make_async_copy(bufs[i], outs[i], sems.at[1, i]) for i in range(count)]
    for copy in loads:
        copy.start()
    for load, store in zip(loads, stores):
        load.wait()
        store.start()
    for copy in stores:
        copy.wait()


def emit(arrays):
    anywhere = pl.BlockSpec(memory_space=pl.ANY)
    count = len(arrays)
    return pl.pallas_call(
        functools.partial(emit_kernel, count),
        name="emit",
        out_shape=tuple(jax.ShapeDtypeStruct(a.shape, a.dtype) for a in arrays),
        in_specs=[anywhere] * count,
        out_specs=(anywhere,) * count,
        scratch_shapes=[pltpu.VMEM(a.shape, a.dtype) for a in arrays]
        + [pltpu.SemaphoreType.DMA((2, count))],
    )(*arrays)


def per_device(
    queries, keys_own, values_own, out_grad, summary_states, w_key, w_value, summary_grad
):
    anywhere = pl.BlockSpec(memory_space=pl.ANY)
    rows = HEADS * TOK
    cols = D // NTP
    dma = pltpu.SemaphoreType.DMA
    arrays = pl.pallas_call(
        layer_kernel,
        name="layer",
        out_shape=(
            jax.ShapeDtypeStruct((TOK, HEADS * HD), BF16),
            jax.ShapeDtypeStruct((TOK, HD), BF16),
            jax.ShapeDtypeStruct((TOK, HD), BF16),
            jax.ShapeDtypeStruct((M, cols), BF16),
        ),
        in_specs=[anywhere] * 8,
        out_specs=(anywhere,) * 3 + (pl.BlockSpec(memory_space=pltpu.VMEM),),
        scratch_shapes=[
            pltpu.VMEM((TOK, HEADS * HD), BF16),
            pltpu.VMEM((TOK, HEADS * HD), BF16),
            pltpu.VMEM((TOK, HD), BF16),
            pltpu.VMEM((TOK, HD), BF16),
            pltpu.VMEM((M, D), BF16),
            pltpu.VMEM((D, W2), BF16),
            pltpu.VMEM((M, cols), BF16),
            pltpu.VMEM((MAIN, W2), BF16),
            pltpu.VMEM((REM, W2), BF16),
            pltpu.VMEM((NZ, REM, W2), BF16),
            pltpu.VMEM((NX, GROUP, W2), BF16),
            pltpu.VMEM((TOK, rows), F32),
            pltpu.VMEM((TOK, rows), F32),
            pltpu.VMEM((NX, GROUP, rows), F32),
            pltpu.VMEM((NX, GROUP, rows), F32),
            pltpu.VMEM((1, rows), F32),
            pltpu.VMEM((1, rows), F32),
            pltpu.VMEM((1, rows), F32),
            pltpu.VMEM((HD, rows), F32),
            pltpu.VMEM((HD, TOK), BF16),
            pltpu.VMEM((HD, GROUP), BF16),
            pltpu.VMEM((GROUP, HD), F32),
            pltpu.VMEM((GROUP, HD), F32),
            pltpu.VMEM((NX, GROUP, W2), BF16),
            pltpu.VMEM((NX + 1, GROUP, W2), BF16),
            pltpu.VMEM((GROUP, W2), F32),
            pltpu.VMEM((NZ, MAIN, W2), BF16),
            pltpu.VMEM((NZ, REM, W2), BF16),
            pltpu.VMEM((NZ, MAIN, W2), BF16),
            pltpu.VMEM((NZ, REM, W2), BF16),
            pltpu.VMEM((BLOCK, W2), BF16),
            pltpu.VMEM((BLOCK, W2), BF16),
            pltpu.VMEM((NY, cols, W2), BF16),
            pltpu.VMEM((NY, BLOCK, cols), F32),
            pltpu.VMEM((6, M, cols // 2), BF16),
            pltpu.VMEM((6, M, cols // 2), BF16),
            pltpu.VMEM((TOK, HEADS * HD), BF16),
            pltpu.VMEM((TOK, HD), BF16),
            pltpu.VMEM((TOK, HD), BF16),
            dma((WCHUNK, 2)),
            dma((6,)),
            dma((3,)),
            dma((2, NZ - 1)),
            dma((2, NZ - 1)),
            dma((NX - 1,)),
            dma((NX - 1,)),
            dma((NX - 1, PIECES)),
            dma((NX + 1, PIECES)),
            dma((2, NZ)),
            dma((2, NZ)),
            dma((6,)),
            dma((6,)),
            dma((NY,)),
            dma((NY,)),
            dma,
            dma,
            dma((2,)),
            dma((NZ + 1,)),
        ],
        compiler_params=pltpu.CompilerParams(
            collective_id=0, has_side_effects=True, vmem_limit_bytes=58 << 20
        ),
    )(
        queries, out_grad, keys_own, values_own, summary_states, w_key, w_value, summary_grad
    )
    return emit(arrays)


def solution(mesh):
    placed = (
        P("seg", "tp"),
        P("seg", "tp"),
        P("seg", "tp"),
        P("seg", "tp"),
        P("seg", None),
        P(None, "tp"),
        P(None, "tp"),
        P("seg", "tp"),
    )
    return jax.shard_map(
        per_device,
        mesh=mesh,
        in_specs=placed,
        out_specs=(P("seg", "tp"), P("seg", "tp"), P("seg", "tp"), P("seg", "tp")),
        check_vma=False,
    )
```

```python
import functools
import math

import jax
import jax.numpy as jnp
from jax import lax
from jax.experimental import pallas as pl
from jax.experimental.pallas import tpu as pltpu
from jax.sharding import PartitionSpec as P

HD = 128
HEADS = 8
TOK = 256
M = 50
MAIN = 48
REM = M - MAIN
TILE = 16
NX, NZ = 4, 8
NTP = 8
NY = NTP // 2
GROUP = NZ * M
REM0 = NZ * MAIN
BLOCK = MAIN + TILE
PIECES = 4
PAIR = NZ // PIECES
D = 8192
W2 = 2 * HD
SCALE = HD ** (-0.5)
SCALE2 = SCALE * math.log2(math.e)
NEG = -1e30
F32 = jnp.float32
BF16 = jnp.bfloat16
MESH = pl.DeviceIdType.MESH
LAST = (((1,), (1,)), ((), ()))
PLAIN = (((1,), (0,)), ((), ()))
WCHUNK = 4


def dot(a, b, dims=PLAIN):
    return lax.dot_general(a, b, dims, preferred_element_type=F32)


def seg_place():
    seg = lax.axis_index("seg")
    return seg // NZ, lax.rem(seg, NZ)


def z_peer(x, z, d):
    other = lax.rem(z + d, NZ)
    return other, x * NZ + other


def x_peer(x, z, d):
    other = lax.rem(x + d, NX)
    return other, other * NZ + z


def greet(peers):
    barrier = pltpu.get_barrier_semaphore()
    for peer in peers:
        pl.semaphore_signal(barrier, inc=1, device_id=peer, device_id_type=MESH)
    return barrier, len(peers)


def load_weights(wk_hbm, wv_hbm, w, sems):
    rows = D // WCHUNK
    copies = []
    for c in range(WCHUNK):
        part = pl.ds(c * rows, rows)
        for i, src in enumerate((wk_hbm, wv_hbm)):
            copy = pltpu.make_async_copy(
                src.at[part], w.at[part, pl.ds(i * HD, HD)], sems.at[c, i]
            )
            copy.start()
            copies.append(copy)
    return copies


def layer_kernel(
    q_hbm, g_hbm, ko_hbm, vo_hbm, st_hbm, wk_hbm, wv_hbm, sg_hbm,
    dq_hbm, dko_hbm, dvo_hbm, out_ref,
    q_ref, g_ref, ko_ref, vo_ref, st, w, sg_ref,
    mine, mine_rem, zrecv, grp, s_own, p_own, s_all, p_all, m_ref, l_ref, d_ref, dqt, kt_own, kt,
    dk_acc, dv_acc, part, xback, acc, zmain, zrem, zback, zback_rem, em, etwin, wtwin, state, tsend, trecv, dq_ref, dko_ref, dvo_ref,
    wsem, insem, outsem, zs, zr, xs, xr, xbs, xbr, zbs, zbr, ts, tr, ws, wr, es, er,
):
    x, z = seg_place()
    tp = lax.axis_index("tp")
    peers = [{"seg": z_peer(x, z, d)[1]} for d in range(1, NZ)]
    peers += [{"seg": x_peer(x, z, d)[1]} for d in range(1, NX)]
    core = lax.rem(tp, 2)
    y = tp // 2
    twin = tp + 1 - 2 * core

    def y_peer(d):
        other = lax.rem(y + d, NY)
        return other, 2 * other + core

    peers += [{"tp": twin}] + [{"tp": y_peer(d)[1]} for d in range(1, NY)]
    last = x == NX - 1
    barrier, count = greet(peers)

    loads = []
    for i, (src, dst) in enumerate(
        (
            (st_hbm, st),
            (q_hbm, q_ref),
            (ko_hbm, ko_ref),
            (g_hbm, g_ref),
            (vo_hbm, vo_ref),
            (sg_hbm, sg_ref),
        )
    ):
        loads.append(pltpu.make_async_copy(src, dst, insem.at[i]))
    loads[0].start()
    wcopies = load_weights(wk_hbm, wv_hbm, w, wsem)
    for copy in loads[1:]:
        copy.start()

    loads[0].wait()
    rows = D // WCHUNK
    total = jnp.zeros((M, W2), F32)
    for c in range(WCHUNK):
        wcopies[2 * c].wait()
        wcopies[2 * c + 1].wait()
        chunk = pl.ds(c * rows, rows)
        total = total + dot(st[:, chunk], w[chunk, :])
    mine[...] = total[0:MAIN].astype(BF16)
    mine_rem[...] = total[MAIN:M].astype(BF16)
    row = lax.broadcasted_iota(jnp.int32, (TILE, W2), 0)
    pl.semaphore_wait(barrier, count)

    def rows_of(i):
        return pl.ds(pl.multiple_of(i * MAIN, TILE), MAIN)

    def zcopies(d, peer, slot):
        own = {"device_id": {"seg": peer}, "device_id_type": MESH}
        return (
            pltpu.make_async_remote_copy(
                src_ref=mine,
                dst_ref=grp.at[x, rows_of(slot)],
                send_sem=zs.at[0, d - 1],
                recv_sem=zr.at[0, d - 1],
                **own,
            ),
            pltpu.make_async_remote_copy(
                src_ref=mine_rem,
                dst_ref=zrecv.at[slot],
                send_sem=zs.at[1, d - 1],
                recv_sem=zr.at[1, d - 1],
                **own,
            ),
        )

    near = (1, 7, 2, 6, 3, 5, 4)
    for d in near:
        other, peer = z_peer(x, z, d)

        @pl.when(jnp.logical_not(last) | (other > z))
        def _(d=d, peer=peer):
            for copy in zcopies(d, peer, z):
                copy.start()

    def xcopy(d, g, part_rows=None):
        other = lax.rem(x + d + NX, NX)
        ref = grp.at[g] if part_rows is None else grp.at[g, part_rows]
        return pltpu.make_async_remote_copy(
            src_ref=ref,
            dst_ref=ref,
            send_sem=xs.at[jnp.abs(d) - 1],
            recv_sem=xr.at[jnp.abs(d) - 1],
            device_id={"seg": other * NZ + z},
            device_id_type=MESH,
        )

    def pass_on(part_rows):
        for d in (3, 2, 1):
            @pl.when((x + d < NX) & ((x > 0) | (d != 2)))
            def _(d=d):
                xcopy(d, x, part_rows).start()

    grp[x, rows_of(z), :] = mine[...]
    pass_on(rows_of(z))

    def assemble(sent_on):
        def place_rem(ref, i):
            two = ref.astype(F32)
            acc[0:TILE, :] = jnp.where(
                row == REM * i,
                two[0:1],
                jnp.where(row == REM * i + 1, two[1:2], acc[0:TILE, :]),
            )

        acc[0:TILE, :] = jnp.zeros((TILE, W2), F32)
        place_rem(mine_rem[...], z)
        for d in near:
            other, peer = z_peer(x, z, NZ - d)
            if sent_on:
                zcopies(d, peer, other)[0].wait_recv()
                pass_on(rows_of(other))
            else:

                @pl.when(other < z)
                def _(d=d, other=other, peer=peer):
                    zcopies(d, peer, other)[0].wait_recv()

                @pl.when(other > z)
                def _(other=other):
                    grp[x, rows_of(other), :] = jnp.zeros((MAIN, W2), BF16)

        for d in near:
            other, peer = z_peer(x, z, NZ - d)

            @pl.when(jnp.bool_(sent_on) | (other < z))
            def _(d=d, other=other, peer=peer):
                zcopies(d, peer, other)[1].wait_recv()
                place_rem(zrecv[other], other)

        grp[x, REM0:GROUP, :] = acc[0:TILE, :].astype(BF16)
        if sent_on:
            pass_on(pl.ds(REM0, TILE))

            @pl.when(x == 0)
            def _():
                xcopy(2, x).start()

    @pl.when(jnp.logical_not(last))
    def _():
        assemble(True)

    cols = D // NTP

    def wcopy(i):
        rows_out = pl.ds(pl.multiple_of((2 * i + 1 - core) * cols, cols), cols)
        return pltpu.make_async_remote_copy(
            src_ref=w.at[rows_out],
            dst_ref=wtwin.at[i],
            send_sem=ws.at[i],
            recv_sem=wr.at[i],
            device_id={"tp": twin},
            device_id_type=MESH,
        )

    for i in range(NY):
        wcopy(i).start()

    def head(ref, h):
        return ref[:, h * HD : (h + 1) * HD]

    def lanes(h):
        return slice(h * TOK, (h + 1) * TOK)

    def sweep_one(keys, vals, s_ref, p_ref, mask, first):
        for h in range(HEADS):
            s = dot(keys, head(q_ref, h), LAST) * SCALE2
            if mask is not None:
                s = jnp.where(mask, s, NEG)
            s_ref[:, lanes(h)] = s
            top = jnp.max(s, axis=0, keepdims=True)
            p = dot(vals, head(g_ref, h), LAST)
            p_ref[:, lanes(h)] = p
            if not first:
                old = m_ref[:, lanes(h)]
                top = jnp.maximum(old, top)
            e = jnp.exp2(s - top)
            total = jnp.sum(e, axis=0, keepdims=True)
            inner = jnp.sum(e * p, axis=0, keepdims=True)
            if not first:
                fade = jnp.exp2(old - top)
                total = total + l_ref[:, lanes(h)] * fade
                inner = inner + d_ref[:, lanes(h)] * fade
            m_ref[:, lanes(h)] = top
            l_ref[:, lanes(h)] = total
            d_ref[:, lanes(h)] = inner

    def sweep_two(s_ref, p_ref, keys_t):
        count = s_ref.shape[0]
        dk = dk_acc.at[0:count]
        dv = dv_acc.at[0:count]
        for h in range(HEADS):
            probs = jnp.exp2(s_ref[:, lanes(h)] - m_ref[:, lanes(h)])
            ds = (probs * (p_ref[:, lanes(h)] - d_ref[:, lanes(h)])).astype(BF16)
            dv_new = dot(probs.astype(BF16), head(g_ref, h))
            dk_new = dot(ds, head(q_ref, h))
            if h:
                dv[...] += dv_new
                dk[...] += dk_new
            else:
                dv[...] = dv_new
                dk[...] = dk_new
            dqt[:, lanes(h)] += dot(keys_t[...], ds)
        return dk[...] * SCALE, dv[...]

    tri = lax.broadcasted_iota(jnp.int32, (TOK, TOK), 0) <= lax.broadcasted_iota(
        jnp.int32, (TOK, TOK), 1
    )
    for copy in loads[1:]:
        copy.wait()
    kt_own[...] = ko_ref[...].astype(F32).T.astype(BF16)
    dqt[...] = jnp.zeros_like(dqt)
    sweep_one(ko_ref[...], vo_ref[...], s_own, p_own, tri, True)

    @pl.when(last)
    def _():
        assemble(False)

    @pl.when(z > 0)
    def _():
        r = lax.broadcasted_iota(jnp.int32, (GROUP, TOK), 0)
        mask = (r < MAIN * z) | ((r >= REM0) & (r < REM0 + REM * z))
        sweep_one(grp[x, :, 0:HD], grp[x, :, HD:W2], s_all.at[x], p_all.at[x], mask, False)

    def full_group(i, carry):
        d = jnp.where(last, lax.rem(i + 1, NX - 1) + 1, i)
        g = x - d
        xcopy(-d, g).wait_recv()
        sweep_one(grp[g, :, 0:HD], grp[g, :, HD:W2], s_all.at[g], p_all.at[g], None, False)
        return carry

    lax.fori_loop(1, x + 1, full_group, 0)

    d_ref[...] = d_ref[...] / l_ref[...]
    m_ref[...] = m_ref[...] + jnp.log2(l_ref[...])

    step = PAIR * MAIN
    pieces = [pl.ds(p * step, step) for p in range(PIECES - 1)]
    pieces.append(pl.ds((PIECES - 1) * step, GROUP - (PIECES - 1) * step))
    split = PIECES // 2

    def hop(g, piece, slot, peer_x):
        return pltpu.make_async_remote_copy(
            src_ref=part.at[g, pieces[piece]],
            dst_ref=xback.at[slot, pieces[piece]],
            send_sem=xbs.at[g, piece],
            recv_sem=xbr.at[slot, piece],
            device_id={"seg": peer_x * NZ + z},
            device_id_type=MESH,
        )

    def hop_out(g, piece):
        around = last & ((g == 0) | ((g == 1) & (piece >= split)))
        slot = jnp.where(around, NX - 1 + g, g)
        up = (x == 2) & (g == 0)
        return hop(g, piece, slot, jnp.where(around, 0, jnp.where(up, NX - 1, x - 1)))

    def hop_add(piece, slot, peer_x):
        hop(0, piece, slot, peer_x).wait_recv()
        rows_in = pieces[piece]
        acc[rows_in, :] += xback[slot, rows_in, :].astype(F32)

    def back_group(i, carry):
        g = jnp.where(last & (i < x), lax.rem(i + 1, x + (x == 0)), i)
        kt[...] = grp[g, :, 0:HD].astype(F32).T.astype(BF16)
        dk, dv = sweep_two(s_all.at[g], p_all.at[g], kt)
        acc[:, 0:HD] = dk
        acc[:, HD:W2] = dv

        @pl.when(g < x)
        def _():
            def put(piece):
                part[g, pieces[piece], :] = acc[pieces[piece], :].astype(BF16)
                hop_out(g, piece).start()

            joined = (x == 2) & (g == 1)
            for piece in range(split, PIECES):

                @pl.when(joined)
                def _(piece=piece):
                    put(piece)

            for piece in range(PIECES):

                @pl.when(last & (g == 0))
                def _(piece=piece):
                    hop_add(piece, 0, 2)

                if piece < split:

                    @pl.when(joined)
                    def _(piece=piece):
                        hop_add(piece, 1, NX - 1)

                @pl.when(jnp.logical_not(joined) | (piece < split))
                def _(piece=piece):
                    put(piece)

        return carry

    lax.fori_loop(0, x + jnp.minimum(z, 1), back_group, 0)

    @pl.when(z == 0)
    def _():
        acc[...] = jnp.zeros_like(acc)

    def zmain_copy(source, target):
        return pltpu.make_async_remote_copy(
            src_ref=zmain.at[target],
            dst_ref=zback.at[source],
            send_sem=zbs.at[0, target],
            recv_sem=zbr.at[0, source],
            device_id={"seg": x * NZ + target},
            device_id_type=MESH,
        )

    def zrem_copy(source, target):
        return pltpu.make_async_remote_copy(
            src_ref=zrem.at[target],
            dst_ref=zback_rem.at[source],
            send_sem=zbs.at[1, target],
            recv_sem=zbr.at[1, source],
            device_id={"seg": x * NZ + target},
            device_id_type=MESH,
        )

    def sends(source, target):
        return (source != target) & (jnp.logical_not(last) | (target < source))

    def relay(piece):
        return pltpu.make_async_remote_copy(
            src_ref=xback.at[NX, pieces[piece]],
            dst_ref=xback.at[NX, pieces[piece]],
            send_sem=xbs.at[1, piece],
            recv_sem=xbr.at[NX, piece],
            device_id={"seg": NZ + z},
            device_id_type=MESH,
        )

    @pl.when(x == 0)
    def _():
        for piece in range(split, PIECES):
            hop(1, piece, NX, NX - 1).wait_recv()
            relay(piece).start()

    for piece in range(PIECES):

        @pl.when(x == 0)
        def _(piece=piece):
            hop_add(piece, 0, 1)
            hop_add(piece, NX - 1, NX - 1)

        @pl.when(x == 1)
        def _(piece=piece):
            hop_add(piece, 1, 2)
            if piece >= split:
                hop_add(piece, NX, 0)

        @pl.when(x == 2)
        def _(piece=piece):
            hop_add(piece, 2, NX - 1)

        for i in range(piece * PAIR, (piece + 1) * PAIR):
            zmain[i] = acc[i * MAIN : (i + 1) * MAIN, :].astype(BF16)

            @pl.when(sends(z, i))
            def _(i=i):
                zmain_copy(z, i).start()

    for i in range(NZ):
        zrem[i] = acc[REM0 + REM * i : REM0 + REM * (i + 1), :].astype(BF16)

        @pl.when(sends(z, i))
        def _(i=i):
            zrem_copy(z, i).start()

    dk, dv = sweep_two(s_own, p_own, kt_own)
    dko_ref[...] = dk.astype(BF16)
    dvo_ref[...] = dv.astype(BF16)
    for h in range(HEADS):
        dq_ref[:, h * HD : (h + 1) * HD] = (dqt[:, lanes(h)] * SCALE).T.astype(BF16)
    stores = [
        pltpu.make_async_copy(src, dst, outsem.at[i])
        for i, (src, dst) in enumerate(((dq_ref, dq_hbm), (dko_ref, dko_hbm), (dvo_ref, dvo_hbm)))
    ]
    for copy in stores:
        copy.start()

    acc[0:MAIN, :] = zmain[z].astype(F32)
    acc[MAIN:M, :] = zrem[z].astype(F32)
    for i in range(NZ):

        @pl.when(sends(i, z))
        def _(i=i):
            zmain_copy(i, z).wait_recv()
            acc[0:MAIN, :] += zback[i].astype(F32)

    for i in range(NZ):

        @pl.when(sends(i, z))
        def _(i=i):
            zrem_copy(i, z).wait_recv()
            acc[MAIN:M, :] += zback_rem[i].astype(F32)

    em[0:MAIN, :] = acc[0:MAIN, :].astype(BF16)
    em[MAIN:BLOCK, :] = jnp.where(
        row == 0, acc[MAIN : MAIN + 1, :], jnp.where(row == 1, acc[MAIN + 1 : M, :], 0.0)
    ).astype(BF16)

    def ecopy():
        return pltpu.make_async_remote_copy(
            src_ref=em,
            dst_ref=etwin,
            send_sem=es,
            recv_sem=er,
            device_id={"tp": twin},
            device_id_type=MESH,
        )

    ecopy().start()
    order = (2, 1, 3, 0)
    for d in order:
        target = y_peer(d)[1]
        chunk = pl.ds(pl.multiple_of(target * cols, cols), cols)
        state[d] = dot(em[...], w[chunk, :], LAST)
    for i in range(NY):
        wcopy(i).wait_recv()
    ecopy().wait_recv()

    half = cols // 2
    lo, hi = slice(0, half), slice(half, cols)
    below, above = y_peer(NY - 1)[1], y_peer(1)[1]
    targets = (below, above, below, below, above, above)
    sources = (above, below, above, above, below, below)

    def tcopy(i, target):
        return pltpu.make_async_remote_copy(
            src_ref=tsend.at[i],
            dst_ref=trecv.at[i],
            send_sem=ts.at[i],
            recv_sem=tr.at[i],
            device_id={"tp": target},
            device_id_type=MESH,
        )

    def put(i, value):
        tsend[i] = value.astype(BF16)
        tcopy(i, targets[i]).start()

    def take(i):
        tcopy(i, sources[i]).wait_recv()
        return trecv[i].astype(F32)

    def both(d):
        return (state[d] + dot(etwin[...], wtwin[y_peer(d)[0]], LAST))[0:M]

    value = both(2)
    put(0, value[:, lo])
    put(1, value[:, hi])
    value = both(NY - 1)
    put(3, value[:, hi])
    state[NY - 1, 0:M, :] = value
    value = both(1)
    put(4, value[:, lo])
    state[1, 0:M, :] = value
    state[0, 0:M, :] = both(0) + sg_ref[...].astype(F32)
    put(2, state[NY - 1, 0:M, lo] + take(0))
    put(5, state[1, 0:M, hi] + take(1))
    out_hi = state[0, 0:M, hi] + take(3)
    out_lo = state[0, 0:M, lo] + take(4)
    out_ref[:, lo] = (out_lo + take(2)).astype(BF16)
    out_ref[:, hi] = (out_hi + take(5)).astype(BF16)

    for copy in stores:
        copy.wait()
    for d in range(1, NZ):
        other, peer = z_peer(x, z, d)

        @pl.when(jnp.logical_not(last) | (other > z))
        def _(d=d, peer=peer):
            for copy in zcopies(d, peer, z):
                copy.wait_send()

    for i in range(NZ):

        @pl.when(sends(z, i))
        def _(i=i):
            zmain_copy(z, i).wait_send()
            zrem_copy(z, i).wait_send()

    lax.fori_loop(1, NX - x, lambda d, c: (xcopy(d, x).wait_send(), c)[1], 0)
    for piece in range(PIECES):
        lax.fori_loop(0, x, lambda g, c: (hop_out(g, piece).wait_send(), c)[1], 0)
    for i in range(NY):
        wcopy(i).wait_send()
    ecopy().wait_send()
    @pl.when(x == 0)
    def _():
        for piece in range(split, PIECES):
            relay(piece).wait_send()

    for i in range(len(targets)):
        tcopy(i, targets[i]).wait_send()


def emit_kernel(count, *refs):
    ins, outs, bufs = refs[:count], refs[count : 2 * count], refs[2 * count : 3 * count]
    sems = refs[3 * count]
    loads = [pltpu.make_async_copy(ins[i], bufs[i], sems.at[0, i]) for i in range(count)]
    stores = [pltpu.make_async_copy(bufs[i], outs[i], sems.at[1, i]) for i in range(count)]
    for copy in loads:
        copy.start()
    for load, store in zip(loads, stores):
        load.wait()
        store.start()
    for copy in stores:
        copy.wait()


def emit(arrays):
    anywhere = pl.BlockSpec(memory_space=pl.ANY)
    count = len(arrays)
    return pl.pallas_call(
        functools.partial(emit_kernel, count),
        name="emit",
        out_shape=tuple(jax.ShapeDtypeStruct(a.shape, a.dtype) for a in arrays),
        in_specs=[anywhere] * count,
        out_specs=(anywhere,) * count,
        scratch_shapes=[pltpu.VMEM(a.shape, a.dtype) for a in arrays]
        + [pltpu.SemaphoreType.DMA((2, count))],
    )(*arrays)


def per_device(
    queries, keys_own, values_own, out_grad, summary_states, w_key, w_value, summary_grad
):
    anywhere = pl.BlockSpec(memory_space=pl.ANY)
    rows = HEADS * TOK
    cols = D // NTP
    dma = pltpu.SemaphoreType.DMA
    arrays = pl.pallas_call(
        layer_kernel,
        name="layer",
        out_shape=(
            jax.ShapeDtypeStruct((TOK, HEADS * HD), BF16),
            jax.ShapeDtypeStruct((TOK, HD), BF16),
            jax.ShapeDtypeStruct((TOK, HD), BF16),
            jax.ShapeDtypeStruct((M, cols), BF16),
        ),
        in_specs=[anywhere] * 8,
        out_specs=(anywhere,) * 3 + (pl.BlockSpec(memory_space=pltpu.VMEM),),
        scratch_shapes=[
            pltpu.VMEM((TOK, HEADS * HD), BF16),
            pltpu.VMEM((TOK, HEADS * HD), BF16),
            pltpu.VMEM((TOK, HD), BF16),
            pltpu.VMEM((TOK, HD), BF16),
            pltpu.VMEM((M, D), BF16),
            pltpu.VMEM((D, W2), BF16),
            pltpu.VMEM((M, cols), BF16),
            pltpu.VMEM((MAIN, W2), BF16),
            pltpu.VMEM((REM, W2), BF16),
            pltpu.VMEM((NZ, REM, W2), BF16),
            pltpu.VMEM((NX, GROUP, W2), BF16),
            pltpu.VMEM((TOK, rows), F32),
            pltpu.VMEM((TOK, rows), F32),
            pltpu.VMEM((NX, GROUP, rows), F32),
            pltpu.VMEM((NX, GROUP, rows), F32),
            pltpu.VMEM((1, rows), F32),
            pltpu.VMEM((1, rows), F32),
            pltpu.VMEM((1, rows), F32),
            pltpu.VMEM((HD, rows), F32),
            pltpu.VMEM((HD, TOK), BF16),
            pltpu.VMEM((HD, GROUP), BF16),
            pltpu.VMEM((GROUP, HD), F32),
            pltpu.VMEM((GROUP, HD), F32),
            pltpu.VMEM((NX, GROUP, W2), BF16),
            pltpu.VMEM((NX + 1, GROUP, W2), BF16),
            pltpu.VMEM((GROUP, W2), F32),
            pltpu.VMEM((NZ, MAIN, W2), BF16),
            pltpu.VMEM((NZ, REM, W2), BF16),
            pltpu.VMEM((NZ, MAIN, W2), BF16),
            pltpu.VMEM((NZ, REM, W2), BF16),
            pltpu.VMEM((BLOCK, W2), BF16),
            pltpu.VMEM((BLOCK, W2), BF16),
            pltpu.VMEM((NY, cols, W2), BF16),
            pltpu.VMEM((NY, BLOCK, cols), F32),
            pltpu.VMEM((6, M, cols // 2), BF16),
            pltpu.VMEM((6, M, cols // 2), BF16),
            pltpu.VMEM((TOK, HEADS * HD), BF16),
            pltpu.VMEM((TOK, HD), BF16),
            pltpu.VMEM((TOK, HD), BF16),
            dma((WCHUNK, 2)),
            dma((6,)),
            dma((3,)),
            dma((2, NZ - 1)),
            dma((2, NZ - 1)),
            dma((NX - 1,)),
            dma((NX - 1,)),
            dma((NX - 1, PIECES)),
            dma((NX + 1, PIECES)),
            dma((2, NZ)),
            dma((2, NZ)),
            dma((6,)),
            dma((6,)),
            dma((NY,)),
            dma((NY,)),
            dma,
            dma,
        ],
        compiler_params=pltpu.CompilerParams(
            collective_id=0, has_side_effects=True, vmem_limit_bytes=58 << 20
        ),
    )(
        queries, out_grad, keys_own, values_own, summary_states, w_key, w_value, summary_grad
    )
    return emit(arrays)


def solution(mesh):
    placed = (
        P("seg", "tp"),
        P("seg", "tp"),
        P("seg", "tp"),
        P("seg", "tp"),
        P("seg", None),
        P(None, "tp"),
        P(None, "tp"),
        P("seg", "tp"),
    )
    return jax.shard_map(
        per_device,
        mesh=mesh,
        in_specs=placed,
        out_specs=(P("seg", "tp"), P("seg", "tp"), P("seg", "tp"), P("seg", "tp")),
        check_vma=False,
    )
```

```python
import functools
import math

import jax
import jax.numpy as jnp
from jax import lax
from jax.experimental import pallas as pl
from jax.experimental.pallas import tpu as pltpu
from jax.sharding import PartitionSpec as P

HD = 128
HEADS = 8
TOK = 256
M = 50
MAIN = 48
REM = M - MAIN
TILE = 16
NX, NZ = 4, 8
NTP = 8
NY = NTP // 2
GROUP = NZ * M
REM0 = NZ * MAIN
BLOCK = MAIN + TILE
PIECES = 4
PAIR = NZ // PIECES
D = 8192
W2 = 2 * HD
SCALE = HD ** (-0.5)
SCALE2 = SCALE * math.log2(math.e)
NEG = -1e30
F32 = jnp.float32
BF16 = jnp.bfloat16
MESH = pl.DeviceIdType.MESH
LAST = (((1,), (1,)), ((), ()))
PLAIN = (((1,), (0,)), ((), ()))
WCHUNK = 4


def dot(a, b, dims=PLAIN):
    return lax.dot_general(a, b, dims, preferred_element_type=F32)


def seg_place():
    seg = lax.axis_index("seg")
    return seg // NZ, lax.rem(seg, NZ)


def z_peer(x, z, d):
    other = lax.rem(z + d, NZ)
    return other, x * NZ + other


def x_peer(x, z, d):
    other = lax.rem(x + d, NX)
    return other, other * NZ + z


def greet(peers):
    barrier = pltpu.get_barrier_semaphore()
    for peer in peers:
        pl.semaphore_signal(barrier, inc=1, device_id=peer, device_id_type=MESH)
    return barrier, len(peers)


def load_weights(wk_hbm, wv_hbm, w, sems):
    rows = D // WCHUNK
    copies = []
    for c in range(WCHUNK):
        part = pl.ds(c * rows, rows)
        for i, src in enumerate((wk_hbm, wv_hbm)):
            copy = pltpu.make_async_copy(
                src.at[part], w.at[part, pl.ds(i * HD, HD)], sems.at[c, i]
            )
            copy.start()
            copies.append(copy)
    return copies


def layer_kernel(
    q_hbm, g_hbm, ko_hbm, vo_hbm, st_hbm, wk_hbm, wv_hbm, sg_hbm,
    dq_hbm, dko_hbm, dvo_hbm, out_ref,
    q_ref, g_ref, ko_ref, vo_ref, st, w, sg_ref,
    mine, mine_rem, zrecv, grp, s_own, p_own, s_all, p_all, m_ref, l_ref, d_ref, dqt, kt_own, kt,
    dk_acc, dv_acc, part, xback, acc, zmain, zrem, zback, zback_rem, em, etwin, wtwin, state, tsend, trecv, dq_ref, dko_ref, dvo_ref,
    wsem, insem, outsem, zs, zr, xs, xr, xbs, xbr, zbs, zbr, ts, tr, ws, wr, es, er,
):
    x, z = seg_place()
    tp = lax.axis_index("tp")
    peers = [{"seg": z_peer(x, z, d)[1]} for d in range(1, NZ)]
    peers += [{"seg": x_peer(x, z, d)[1]} for d in range(1, NX)]
    core = lax.rem(tp, 2)
    y = tp // 2
    twin = tp + 1 - 2 * core

    def y_peer(d):
        other = lax.rem(y + d, NY)
        return other, 2 * other + core

    peers += [{"tp": twin}] + [{"tp": y_peer(d)[1]} for d in range(1, NY)]
    last = x == NX - 1
    barrier, count = greet(peers)

    loads = []
    for i, (src, dst) in enumerate(
        (
            (st_hbm, st),
            (q_hbm, q_ref),
            (ko_hbm, ko_ref),
            (g_hbm, g_ref),
            (vo_hbm, vo_ref),
            (sg_hbm, sg_ref),
        )
    ):
        loads.append(pltpu.make_async_copy(src, dst, insem.at[i]))
    loads[0].start()
    wcopies = load_weights(wk_hbm, wv_hbm, w, wsem)
    for copy in loads[1:]:
        copy.start()

    loads[0].wait()
    rows = D // WCHUNK
    total = jnp.zeros((M, W2), F32)
    for c in range(WCHUNK):
        wcopies[2 * c].wait()
        wcopies[2 * c + 1].wait()
        chunk = pl.ds(c * rows, rows)
        total = total + dot(st[:, chunk], w[chunk, :])
    mine[...] = total[0:MAIN].astype(BF16)
    mine_rem[...] = total[MAIN:M].astype(BF16)
    row = lax.broadcasted_iota(jnp.int32, (TILE, W2), 0)
    pl.semaphore_wait(barrier, count)

    def rows_of(i):
        return pl.ds(pl.multiple_of(i * MAIN, TILE), MAIN)

    def zcopies(d, peer, slot):
        own = {"device_id": {"seg": peer}, "device_id_type": MESH}
        return (
            pltpu.make_async_remote_copy(
                src_ref=mine,
                dst_ref=grp.at[x, rows_of(slot)],
                send_sem=zs.at[0, d - 1],
                recv_sem=zr.at[0, d - 1],
                **own,
            ),
            pltpu.make_async_remote_copy(
                src_ref=mine_rem,
                dst_ref=zrecv.at[slot],
                send_sem=zs.at[1, d - 1],
                recv_sem=zr.at[1, d - 1],
                **own,
            ),
        )

    near = (1, 7, 2, 6, 3, 5, 4)
    for d in near:
        other, peer = z_peer(x, z, d)

        @pl.when(jnp.logical_not(last) | (other > z))
        def _(d=d, peer=peer):
            for copy in zcopies(d, peer, z):
                copy.start()

    def xcopy(d, g, part_rows=None):
        other = lax.rem(x + d + NX, NX)
        ref = grp.at[g] if part_rows is None else grp.at[g, part_rows]
        return pltpu.make_async_remote_copy(
            src_ref=ref,
            dst_ref=ref,
            send_sem=xs.at[jnp.abs(d) - 1],
            recv_sem=xr.at[jnp.abs(d) - 1],
            device_id={"seg": other * NZ + z},
            device_id_type=MESH,
        )

    def pass_on(part_rows):
        for d in (3, 1, 2):
            @pl.when((x + d < NX) & ((x > 0) | (d != 2)))
            def _(d=d):
                xcopy(d, x, part_rows).start()

    grp[x, rows_of(z), :] = mine[...]
    pass_on(rows_of(z))

    def assemble(sent_on):
        def place_rem(ref, i):
            two = ref.astype(F32)
            acc[0:TILE, :] = jnp.where(
                row == REM * i,
                two[0:1],
                jnp.where(row == REM * i + 1, two[1:2], acc[0:TILE, :]),
            )

        acc[0:TILE, :] = jnp.zeros((TILE, W2), F32)
        place_rem(mine_rem[...], z)
        for d in near:
            other, peer = z_peer(x, z, NZ - d)
            if sent_on:
                zcopies(d, peer, other)[0].wait_recv()
                pass_on(rows_of(other))
            else:

                @pl.when(other < z)
                def _(d=d, other=other, peer=peer):
                    zcopies(d, peer, other)[0].wait_recv()

                @pl.when(other > z)
                def _(other=other):
                    grp[x, rows_of(other), :] = jnp.zeros((MAIN, W2), BF16)

        for d in near:
            other, peer = z_peer(x, z, NZ - d)

            @pl.when(jnp.bool_(sent_on) | (other < z))
            def _(d=d, other=other, peer=peer):
                zcopies(d, peer, other)[1].wait_recv()
                place_rem(zrecv[other], other)

        grp[x, REM0:GROUP, :] = acc[0:TILE, :].astype(BF16)
        if sent_on:
            pass_on(pl.ds(REM0, TILE))

            @pl.when(x == 0)
            def _():
                xcopy(2, x).start()

    @pl.when(jnp.logical_not(last))
    def _():
        assemble(True)

    cols = D // NTP

    def wcopy(i):
        rows_out = pl.ds(pl.multiple_of((2 * i + 1 - core) * cols, cols), cols)
        return pltpu.make_async_remote_copy(
            src_ref=w.at[rows_out],
            dst_ref=wtwin.at[i],
            send_sem=ws.at[i],
            recv_sem=wr.at[i],
            device_id={"tp": twin},
            device_id_type=MESH,
        )

    def head(ref, h):
        return ref[:, h * HD : (h + 1) * HD]

    def lanes(h):
        return slice(h * TOK, (h + 1) * TOK)

    def sweep_one(keys, vals, s_ref, p_ref, mask, first):
        for h in range(HEADS):
            s = dot(keys, head(q_ref, h), LAST) * SCALE2
            if mask is not None:
                s = jnp.where(mask, s, NEG)
            s_ref[:, lanes(h)] = s
            top = jnp.max(s, axis=0, keepdims=True)
            p = dot(vals, head(g_ref, h), LAST)
            p_ref[:, lanes(h)] = p
            if not first:
                old = m_ref[:, lanes(h)]
                top = jnp.maximum(old, top)
            e = jnp.exp2(s - top)
            total = jnp.sum(e, axis=0, keepdims=True)
            inner = jnp.sum(e * p, axis=0, keepdims=True)
            if not first:
                fade = jnp.exp2(old - top)
                total = total + l_ref[:, lanes(h)] * fade
                inner = inner + d_ref[:, lanes(h)] * fade
            m_ref[:, lanes(h)] = top
            l_ref[:, lanes(h)] = total
            d_ref[:, lanes(h)] = inner

    def sweep_two(s_ref, p_ref, keys_t):
        count = s_ref.shape[0]
        dk = dk_acc.at[0:count]
        dv = dv_acc.at[0:count]
        for h in range(HEADS):
            probs = jnp.exp2(s_ref[:, lanes(h)] - m_ref[:, lanes(h)])
            ds = (probs * (p_ref[:, lanes(h)] - d_ref[:, lanes(h)])).astype(BF16)
            dv_new = dot(probs.astype(BF16), head(g_ref, h))
            dk_new = dot(ds, head(q_ref, h))
            if h:
                dv[...] += dv_new
                dk[...] += dk_new
            else:
                dv[...] = dv_new
                dk[...] = dk_new
            dqt[:, lanes(h)] += dot(keys_t[...], ds)
        return dk[...] * SCALE, dv[...]

    tri = lax.broadcasted_iota(jnp.int32, (TOK, TOK), 0) <= lax.broadcasted_iota(
        jnp.int32, (TOK, TOK), 1
    )
    for copy in loads[1:]:
        copy.wait()
    kt_own[...] = ko_ref[...].astype(F32).T.astype(BF16)
    dqt[...] = jnp.zeros_like(dqt)
    sweep_one(ko_ref[...], vo_ref[...], s_own, p_own, tri, True)

    @pl.when(last)
    def _():
        assemble(False)

    @pl.when(z > 0)
    def _():
        r = lax.broadcasted_iota(jnp.int32, (GROUP, TOK), 0)
        mask = (r < MAIN * z) | ((r >= REM0) & (r < REM0 + REM * z))
        sweep_one(grp[x, :, 0:HD], grp[x, :, HD:W2], s_all.at[x], p_all.at[x], mask, False)

    def full_group(i, carry):
        d = jnp.where(last & (i > 1), 5 - i, i)
        g = x - d
        xcopy(-d, g).wait_recv()
        sweep_one(grp[g, :, 0:HD], grp[g, :, HD:W2], s_all.at[g], p_all.at[g], None, False)
        return carry

    lax.fori_loop(1, x + 1, full_group, 0)

    d_ref[...] = d_ref[...] / l_ref[...]
    m_ref[...] = m_ref[...] + jnp.log2(l_ref[...])

    step = PAIR * MAIN
    pieces = [pl.ds(p * step, step) for p in range(PIECES - 1)]
    pieces.append(pl.ds((PIECES - 1) * step, GROUP - (PIECES - 1) * step))
    split = PIECES // 2

    def hop(g, piece, slot, peer_x):
        return pltpu.make_async_remote_copy(
            src_ref=part.at[g, pieces[piece]],
            dst_ref=xback.at[slot, pieces[piece]],
            send_sem=xbs.at[g, piece],
            recv_sem=xbr.at[slot, piece],
            device_id={"seg": peer_x * NZ + z},
            device_id_type=MESH,
        )

    def hop_out(g, piece):
        around = last & ((g == 0) | ((g == 1) & (piece >= split)))
        slot = jnp.where(around, NX - 1 + g, g)
        up = (x == 2) & (g == 0)
        return hop(g, piece, slot, jnp.where(around, 0, jnp.where(up, NX - 1, x - 1)))

    def hop_add(piece, slot, peer_x):
        hop(0, piece, slot, peer_x).wait_recv()
        rows_in = pieces[piece]
        acc[rows_in, :] += xback[slot, rows_in, :].astype(F32)

    def back_group(i, carry):
        g = jnp.where(last & (i < x), lax.rem(i + 1, x + (x == 0)), i)
        kt[...] = grp[g, :, 0:HD].astype(F32).T.astype(BF16)
        dk, dv = sweep_two(s_all.at[g], p_all.at[g], kt)
        acc[:, 0:HD] = dk
        acc[:, HD:W2] = dv

        @pl.when(g < x)
        def _():
            def put(piece):
                part[g, pieces[piece], :] = acc[pieces[piece], :].astype(BF16)
                hop_out(g, piece).start()

            joined = (x == 2) & (g == 1)
            for piece in range(split, PIECES):

                @pl.when(joined)
                def _(piece=piece):
                    put(piece)

            for piece in range(PIECES):

                @pl.when(last & (g == 0))
                def _(piece=piece):
                    hop_add(piece, 0, 2)

                if piece < split:

                    @pl.when(joined)
                    def _(piece=piece):
                        hop_add(piece, 1, NX - 1)

                @pl.when(jnp.logical_not(joined) | (piece < split))
                def _(piece=piece):
                    put(piece)

        return carry

    lax.fori_loop(0, x + jnp.minimum(z, 1), back_group, 0)
    for i in range(NY):
        wcopy(i).start()

    @pl.when(z == 0)
    def _():
        acc[...] = jnp.zeros_like(acc)

    def zmain_copy(source, target):
        return pltpu.make_async_remote_copy(
            src_ref=zmain.at[target],
            dst_ref=zback.at[source],
            send_sem=zbs.at[0, target],
            recv_sem=zbr.at[0, source],
            device_id={"seg": x * NZ + target},
            device_id_type=MESH,
        )

    def zrem_copy(source, target):
        return pltpu.make_async_remote_copy(
            src_ref=zrem.at[target],
            dst_ref=zback_rem.at[source],
            send_sem=zbs.at[1, target],
            recv_sem=zbr.at[1, source],
            device_id={"seg": x * NZ + target},
            device_id_type=MESH,
        )

    def sends(source, target):
        return (source != target) & (jnp.logical_not(last) | (target < source))

    def relay(piece):
        return pltpu.make_async_remote_copy(
            src_ref=xback.at[NX, pieces[piece]],
            dst_ref=xback.at[NX, pieces[piece]],
            send_sem=xbs.at[1, piece],
            recv_sem=xbr.at[NX, piece],
            device_id={"seg": NZ + z},
            device_id_type=MESH,
        )

    @pl.when(x == 0)
    def _():
        for piece in range(split, PIECES):
            hop(1, piece, NX, NX - 1).wait_recv()
            relay(piece).start()

    for piece in range(PIECES):

        @pl.when(x == 0)
        def _(piece=piece):
            hop_add(piece, 0, 1)
            hop_add(piece, NX - 1, NX - 1)

        @pl.when(x == 1)
        def _(piece=piece):
            hop_add(piece, 1, 2)
            if piece >= split:
                hop_add(piece, NX, 0)

        @pl.when(x == 2)
        def _(piece=piece):
            hop_add(piece, 2, NX - 1)

        for i in range(piece * PAIR, (piece + 1) * PAIR):
            zmain[i] = acc[i * MAIN : (i + 1) * MAIN, :].astype(BF16)

            @pl.when(sends(z, i))
            def _(i=i):
                zmain_copy(z, i).start()

    for i in range(NZ):
        zrem[i] = acc[REM0 + REM * i : REM0 + REM * (i + 1), :].astype(BF16)

        @pl.when(sends(z, i))
        def _(i=i):
            zrem_copy(z, i).start()

    dk, dv = sweep_two(s_own, p_own, kt_own)
    dko_ref[...] = dk.astype(BF16)
    dvo_ref[...] = dv.astype(BF16)
    for h in range(HEADS):
        dq_ref[:, h * HD : (h + 1) * HD] = (dqt[:, lanes(h)] * SCALE).T.astype(BF16)
    stores = [
        pltpu.make_async_copy(src, dst, outsem.at[i])
        for i, (src, dst) in enumerate(((dq_ref, dq_hbm), (dko_ref, dko_hbm), (dvo_ref, dvo_hbm)))
    ]
    for copy in stores:
        copy.start()

    acc[0:MAIN, :] = zmain[z].astype(F32)
    acc[MAIN:M, :] = zrem[z].astype(F32)
    for i in range(NZ):

        @pl.when(sends(i, z))
        def _(i=i):
            zmain_copy(i, z).wait_recv()
            acc[0:MAIN, :] += zback[i].astype(F32)

    for i in range(NZ):

        @pl.when(sends(i, z))
        def _(i=i):
            zrem_copy(i, z).wait_recv()
            acc[MAIN:M, :] += zback_rem[i].astype(F32)

    em[0:MAIN, :] = acc[0:MAIN, :].astype(BF16)
    em[MAIN:BLOCK, :] = jnp.where(
        row == 0, acc[MAIN : MAIN + 1, :], jnp.where(row == 1, acc[MAIN + 1 : M, :], 0.0)
    ).astype(BF16)

    def ecopy():
        return pltpu.make_async_remote_copy(
            src_ref=em,
            dst_ref=etwin,
            send_sem=es,
            recv_sem=er,
            device_id={"tp": twin},
            device_id_type=MESH,
        )

    ecopy().start()
    order = (2, 1, 3, 0)
    for d in order:
        target = y_peer(d)[1]
        chunk = pl.ds(pl.multiple_of(target * cols, cols), cols)
        state[d] = dot(em[...], w[chunk, :], LAST)
    for i in range(NY):
        wcopy(i).wait_recv()
    ecopy().wait_recv()

    half = cols // 2
    lo, hi = slice(0, half), slice(half, cols)
    below, above = y_peer(NY - 1)[1], y_peer(1)[1]
    targets = (below, above, below, below, above, above)
    sources = (above, below, above, above, below, below)

    def tcopy(i, target):
        return pltpu.make_async_remote_copy(
            src_ref=tsend.at[i],
            dst_ref=trecv.at[i],
            send_sem=ts.at[i],
            recv_sem=tr.at[i],
            device_id={"tp": target},
            device_id_type=MESH,
        )

    def put(i, value):
        tsend[i] = value.astype(BF16)
        tcopy(i, targets[i]).start()

    def take(i):
        tcopy(i, sources[i]).wait_recv()
        return trecv[i].astype(F32)

    def both(d):
        return (state[d] + dot(etwin[...], wtwin[y_peer(d)[0]], LAST))[0:M]

    value = both(2)
    put(0, value[:, lo])
    put(1, value[:, hi])
    value = both(NY - 1)
    put(3, value[:, hi])
    state[NY - 1, 0:M, :] = value
    value = both(1)
    put(4, value[:, lo])
    state[1, 0:M, :] = value
    state[0, 0:M, :] = both(0) + sg_ref[...].astype(F32)
    put(2, state[NY - 1, 0:M, lo] + take(0))
    put(5, state[1, 0:M, hi] + take(1))
    out_hi = state[0, 0:M, hi] + take(3)
    out_lo = state[0, 0:M, lo] + take(4)
    out_ref[:, lo] = (out_lo + take(2)).astype(BF16)
    out_ref[:, hi] = (out_hi + take(5)).astype(BF16)

    for copy in stores:
        copy.wait()
    for d in range(1, NZ):
        other, peer = z_peer(x, z, d)

        @pl.when(jnp.logical_not(last) | (other > z))
        def _(d=d, peer=peer):
            for copy in zcopies(d, peer, z):
                copy.wait_send()

    for i in range(NZ):

        @pl.when(sends(z, i))
        def _(i=i):
            zmain_copy(z, i).wait_send()
            zrem_copy(z, i).wait_send()

    lax.fori_loop(1, NX - x, lambda d, c: (xcopy(d, x).wait_send(), c)[1], 0)
    for piece in range(PIECES):
        lax.fori_loop(0, x, lambda g, c: (hop_out(g, piece).wait_send(), c)[1], 0)
    for i in range(NY):
        wcopy(i).wait_send()
    ecopy().wait_send()
    @pl.when(x == 0)
    def _():
        for piece in range(split, PIECES):
            relay(piece).wait_send()

    for i in range(len(targets)):
        tcopy(i, targets[i]).wait_send()


def emit_kernel(count, *refs):
    ins, outs, bufs = refs[:count], refs[count : 2 * count], refs[2 * count : 3 * count]
    sems = refs[3 * count]
    loads = [pltpu.make_async_copy(ins[i], bufs[i], sems.at[0, i]) for i in range(count)]
    stores = [pltpu.make_async_copy(bufs[i], outs[i], sems.at[1, i]) for i in range(count)]
    for copy in loads:
        copy.start()
    for load, store in zip(loads, stores):
        load.wait()
        store.start()
    for copy in stores:
        copy.wait()


def emit(arrays):
    anywhere = pl.BlockSpec(memory_space=pl.ANY)
    count = len(arrays)
    return pl.pallas_call(
        functools.partial(emit_kernel, count),
        name="emit",
        out_shape=tuple(jax.ShapeDtypeStruct(a.shape, a.dtype) for a in arrays),
        in_specs=[anywhere] * count,
        out_specs=(anywhere,) * count,
        scratch_shapes=[pltpu.VMEM(a.shape, a.dtype) for a in arrays]
        + [pltpu.SemaphoreType.DMA((2, count))],
    )(*arrays)


def per_device(
    queries, keys_own, values_own, out_grad, summary_states, w_key, w_value, summary_grad
):
    anywhere = pl.BlockSpec(memory_space=pl.ANY)
    rows = HEADS * TOK
    cols = D // NTP
    dma = pltpu.SemaphoreType.DMA
    arrays = pl.pallas_call(
        layer_kernel,
        name="layer",
        out_shape=(
            jax.ShapeDtypeStruct((TOK, HEADS * HD), BF16),
            jax.ShapeDtypeStruct((TOK, HD), BF16),
            jax.ShapeDtypeStruct((TOK, HD), BF16),
            jax.ShapeDtypeStruct((M, cols), BF16),
        ),
        in_specs=[anywhere] * 8,
        out_specs=(anywhere,) * 3 + (pl.BlockSpec(memory_space=pltpu.VMEM),),
        scratch_shapes=[
            pltpu.VMEM((TOK, HEADS * HD), BF16),
            pltpu.VMEM((TOK, HEADS * HD), BF16),
            pltpu.VMEM((TOK, HD), BF16),
            pltpu.VMEM((TOK, HD), BF16),
            pltpu.VMEM((M, D), BF16),
            pltpu.VMEM((D, W2), BF16),
            pltpu.VMEM((M, cols), BF16),
            pltpu.VMEM((MAIN, W2), BF16),
            pltpu.VMEM((REM, W2), BF16),
            pltpu.VMEM((NZ, REM, W2), BF16),
            pltpu.VMEM((NX, GROUP, W2), BF16),
            pltpu.VMEM((TOK, rows), F32),
            pltpu.VMEM((TOK, rows), F32),
            pltpu.VMEM((NX, GROUP, rows), F32),
            pltpu.VMEM((NX, GROUP, rows), F32),
            pltpu.VMEM((1, rows), F32),
            pltpu.VMEM((1, rows), F32),
            pltpu.VMEM((1, rows), F32),
            pltpu.VMEM((HD, rows), F32),
            pltpu.VMEM((HD, TOK), BF16),
            pltpu.VMEM((HD, GROUP), BF16),
            pltpu.VMEM((GROUP, HD), F32),
            pltpu.VMEM((GROUP, HD), F32),
            pltpu.VMEM((NX, GROUP, W2), BF16),
            pltpu.VMEM((NX + 1, GROUP, W2), BF16),
            pltpu.VMEM((GROUP, W2), F32),
            pltpu.VMEM((NZ, MAIN, W2), BF16),
            pltpu.VMEM((NZ, REM, W2), BF16),
            pltpu.VMEM((NZ, MAIN, W2), BF16),
            pltpu.VMEM((NZ, REM, W2), BF16),
            pltpu.VMEM((BLOCK, W2), BF16),
            pltpu.VMEM((BLOCK, W2), BF16),
            pltpu.VMEM((NY, cols, W2), BF16),
            pltpu.VMEM((NY, BLOCK, cols), F32),
            pltpu.VMEM((6, M, cols // 2), BF16),
            pltpu.VMEM((6, M, cols // 2), BF16),
            pltpu.VMEM((TOK, HEADS * HD), BF16),
            pltpu.VMEM((TOK, HD), BF16),
            pltpu.VMEM((TOK, HD), BF16),
            dma((WCHUNK, 2)),
            dma((6,)),
            dma((3,)),
            dma((2, NZ - 1)),
            dma((2, NZ - 1)),
            dma((NX - 1,)),
            dma((NX - 1,)),
            dma((NX - 1, PIECES)),
            dma((NX + 1, PIECES)),
            dma((2, NZ)),
            dma((2, NZ)),
            dma((6,)),
            dma((6,)),
            dma((NY,)),
            dma((NY,)),
            dma,
            dma,
        ],
        compiler_params=pltpu.CompilerParams(
            collective_id=0, has_side_effects=True, vmem_limit_bytes=58 << 20
        ),
    )(
        queries, out_grad, keys_own, values_own, summary_states, w_key, w_value, summary_grad
    )
    return emit(arrays)


def solution(mesh):
    placed = (
        P("seg", "tp"),
        P("seg", "tp"),
        P("seg", "tp"),
        P("seg", "tp"),
        P("seg", None),
        P(None, "tp"),
        P(None, "tp"),
        P("seg", "tp"),
    )
    return jax.shard_map(
        per_device,
        mesh=mesh,
        in_specs=placed,
        out_specs=(P("seg", "tp"), P("seg", "tp"), P("seg", "tp"), P("seg", "tp")),
        check_vma=False,
    )
```

```python
import functools
import math

import jax
import jax.numpy as jnp
from jax import lax
from jax.experimental import pallas as pl
from jax.experimental.pallas import tpu as pltpu
from jax.sharding import PartitionSpec as P

HD = 128
HEADS = 8
TOK = 256
M = 50
MAIN = 48
REM = M - MAIN
TILE = 16
NX, NZ = 4, 8
NTP = 8
NY = NTP // 2
GROUP = NZ * M
REM0 = NZ * MAIN
BLOCK = MAIN + TILE
HALF = REM0 // 2
D = 8192
W2 = 2 * HD
SCALE = HD ** (-0.5)
SCALE2 = SCALE * math.log2(math.e)
NEG = -1e30
F32 = jnp.float32
BF16 = jnp.bfloat16
MESH = pl.DeviceIdType.MESH
LAST = (((1,), (1,)), ((), ()))
PLAIN = (((1,), (0,)), ((), ()))
WCHUNK = 4


def dot(a, b, dims=PLAIN):
    return lax.dot_general(a, b, dims, preferred_element_type=F32)


def seg_place():
    seg = lax.axis_index("seg")
    return seg // NZ, lax.rem(seg, NZ)


def z_peer(x, z, d):
    other = lax.rem(z + d, NZ)
    return other, x * NZ + other


def x_peer(x, z, d):
    other = lax.rem(x + d, NX)
    return other, other * NZ + z


def greet(peers):
    barrier = pltpu.get_barrier_semaphore()
    for peer in peers:
        pl.semaphore_signal(barrier, inc=1, device_id=peer, device_id_type=MESH)
    return barrier, len(peers)


def load_weights(wk_hbm, wv_hbm, w, sems):
    rows = D // WCHUNK
    copies = []
    for c in range(WCHUNK):
        part = pl.ds(c * rows, rows)
        for i, src in enumerate((wk_hbm, wv_hbm)):
            copy = pltpu.make_async_copy(
                src.at[part], w.at[part, pl.ds(i * HD, HD)], sems.at[c, i]
            )
            copy.start()
            copies.append(copy)
    return copies


def layer_kernel(
    q_hbm, g_hbm, ko_hbm, vo_hbm, st_hbm, wk_hbm, wv_hbm, sg_hbm,
    dq_hbm, dko_hbm, dvo_hbm, out_ref,
    q_ref, g_ref, ko_ref, vo_ref, st, w, sg_ref,
    mine, mine_rem, zrecv, grp, s_own, p_own, s_all, p_all, m_ref, l_ref, d_ref, dqt, kt_own, kt,
    dk_acc, dv_acc, part, xback, acc, zmain, zrem, zback, zback_rem, em, etwin, wtwin, state, tsend, trecv, dq_ref, dko_ref, dvo_ref,
    wsem, insem, outsem, zs, zr, xs, xr, xbs, xbr, zbs, zbr, ts, tr, ws, wr, es, er,
):
    x, z = seg_place()
    tp = lax.axis_index("tp")
    peers = [{"seg": z_peer(x, z, d)[1]} for d in range(1, NZ)]
    peers += [{"seg": x_peer(x, z, d)[1]} for d in range(1, NX)]
    core = lax.rem(tp, 2)
    y = tp // 2
    twin = tp + 1 - 2 * core

    def y_peer(d):
        other = lax.rem(y + d, NY)
        return other, 2 * other + core

    peers += [{"tp": twin}] + [{"tp": y_peer(d)[1]} for d in range(1, NY)]
    last = x == NX - 1
    barrier, count = greet(peers)

    loads = []
    for i, (src, dst) in enumerate(
        (
            (st_hbm, st),
            (q_hbm, q_ref),
            (ko_hbm, ko_ref),
            (g_hbm, g_ref),
            (vo_hbm, vo_ref),
            (sg_hbm, sg_ref),
        )
    ):
        loads.append(pltpu.make_async_copy(src, dst, insem.at[i]))
    loads[0].start()
    wcopies = load_weights(wk_hbm, wv_hbm, w, wsem)
    for copy in loads[1:]:
        copy.start()

    loads[0].wait()
    rows = D // WCHUNK
    total = jnp.zeros((M, W2), F32)
    for c in range(WCHUNK):
        wcopies[2 * c].wait()
        wcopies[2 * c + 1].wait()
        chunk = pl.ds(c * rows, rows)
        total = total + dot(st[:, chunk], w[chunk, :])
    mine[...] = total[0:MAIN].astype(BF16)
    mine_rem[...] = total[MAIN:M].astype(BF16)
    row = lax.broadcasted_iota(jnp.int32, (TILE, W2), 0)
    pl.semaphore_wait(barrier, count)

    def rows_of(i):
        return pl.ds(pl.multiple_of(i * MAIN, TILE), MAIN)

    def zcopies(d, peer, slot):
        own = {"device_id": {"seg": peer}, "device_id_type": MESH}
        return (
            pltpu.make_async_remote_copy(
                src_ref=mine,
                dst_ref=grp.at[x, rows_of(slot)],
                send_sem=zs.at[0, d - 1],
                recv_sem=zr.at[0, d - 1],
                **own,
            ),
            pltpu.make_async_remote_copy(
                src_ref=mine_rem,
                dst_ref=zrecv.at[slot],
                send_sem=zs.at[1, d - 1],
                recv_sem=zr.at[1, d - 1],
                **own,
            ),
        )

    near = (1, 7, 2, 6, 3, 5, 4)
    for d in near:
        other, peer = z_peer(x, z, d)

        @pl.when(jnp.logical_not(last) | (other > z))
        def _(d=d, peer=peer):
            for copy in zcopies(d, peer, z):
                copy.start()

    def xcopy(d, g, part_rows=None):
        other = lax.rem(x + d + NX, NX)
        ref = grp.at[g] if part_rows is None else grp.at[g, part_rows]
        return pltpu.make_async_remote_copy(
            src_ref=ref,
            dst_ref=ref,
            send_sem=xs.at[jnp.abs(d) - 1],
            recv_sem=xr.at[jnp.abs(d) - 1],
            device_id={"seg": other * NZ + z},
            device_id_type=MESH,
        )

    def pass_on(part_rows):
        for d in (3, 1, 2):
            @pl.when((x + d < NX) & ((x > 0) | (d != 2)))
            def _(d=d):
                xcopy(d, x, part_rows).start()

    grp[x, rows_of(z), :] = mine[...]
    pass_on(rows_of(z))

    def assemble(sent_on):
        def place_rem(ref, i):
            two = ref.astype(F32)
            acc[0:TILE, :] = jnp.where(
                row == REM * i,
                two[0:1],
                jnp.where(row == REM * i + 1, two[1:2], acc[0:TILE, :]),
            )

        acc[0:TILE, :] = jnp.zeros((TILE, W2), F32)
        place_rem(mine_rem[...], z)
        for d in near:
            other, peer = z_peer(x, z, NZ - d)
            if sent_on:
                zcopies(d, peer, other)[0].wait_recv()
                pass_on(rows_of(other))
            else:

                @pl.when(other < z)
                def _(d=d, other=other, peer=peer):
                    zcopies(d, peer, other)[0].wait_recv()

                @pl.when(other > z)
                def _(other=other):
                    grp[x, rows_of(other), :] = jnp.zeros((MAIN, W2), BF16)

        for d in near:
            other, peer = z_peer(x, z, NZ - d)

            @pl.when(jnp.bool_(sent_on) | (other < z))
            def _(d=d, other=other, peer=peer):
                zcopies(d, peer, other)[1].wait_recv()
                place_rem(zrecv[other], other)

        grp[x, REM0:GROUP, :] = acc[0:TILE, :].astype(BF16)
        if sent_on:
            pass_on(pl.ds(REM0, TILE))

            @pl.when(x == 0)
            def _():
                xcopy(2, x).start()

    @pl.when(jnp.logical_not(last))
    def _():
        assemble(True)

    cols = D // NTP

    def wcopy(i):
        rows_out = pl.ds(pl.multiple_of((2 * i + 1 - core) * cols, cols), cols)
        return pltpu.make_async_remote_copy(
            src_ref=w.at[rows_out],
            dst_ref=wtwin.at[i],
            send_sem=ws.at[i],
            recv_sem=wr.at[i],
            device_id={"tp": twin},
            device_id_type=MESH,
        )

    for i in range(NY):
        wcopy(i).start()

    def head(ref, h):
        return ref[:, h * HD : (h + 1) * HD]

    def lanes(h):
        return slice(h * TOK, (h + 1) * TOK)

    def sweep_one(keys, vals, s_ref, p_ref, mask, first):
        for h in range(HEADS):
            s = dot(keys, head(q_ref, h), LAST) * SCALE2
            if mask is not None:
                s = jnp.where(mask, s, NEG)
            s_ref[:, lanes(h)] = s
            top = jnp.max(s, axis=0, keepdims=True)
            p = dot(vals, head(g_ref, h), LAST)
            p_ref[:, lanes(h)] = p
            if not first:
                old = m_ref[:, lanes(h)]
                top = jnp.maximum(old, top)
            e = jnp.exp2(s - top)
            total = jnp.sum(e, axis=0, keepdims=True)
            inner = jnp.sum(e * p, axis=0, keepdims=True)
            if not first:
                fade = jnp.exp2(old - top)
                total = total + l_ref[:, lanes(h)] * fade
                inner = inner + d_ref[:, lanes(h)] * fade
            m_ref[:, lanes(h)] = top
            l_ref[:, lanes(h)] = total
            d_ref[:, lanes(h)] = inner

    def sweep_two(s_ref, p_ref, keys_t):
        count = s_ref.shape[0]
        dk = dk_acc.at[0:count]
        dv = dv_acc.at[0:count]
        for h in range(HEADS):
            probs = jnp.exp2(s_ref[:, lanes(h)] - m_ref[:, lanes(h)])
            ds = (probs * (p_ref[:, lanes(h)] - d_ref[:, lanes(h)])).astype(BF16)
            dv_new = dot(probs.astype(BF16), head(g_ref, h))
            dk_new = dot(ds, head(q_ref, h))
            if h:
                dv[...] += dv_new
                dk[...] += dk_new
            else:
                dv[...] = dv_new
                dk[...] = dk_new
            dqt[:, lanes(h)] += dot(keys_t[...], ds)
        return dk[...] * SCALE, dv[...]

    tri = lax.broadcasted_iota(jnp.int32, (TOK, TOK), 0) <= lax.broadcasted_iota(
        jnp.int32, (TOK, TOK), 1
    )
    for copy in loads[1:]:
        copy.wait()
    kt_own[...] = ko_ref[...].astype(F32).T.astype(BF16)
    dqt[...] = jnp.zeros_like(dqt)
    sweep_one(ko_ref[...], vo_ref[...], s_own, p_own, tri, True)

    @pl.when(last)
    def _():
        assemble(False)

    @pl.when(z > 0)
    def _():
        r = lax.broadcasted_iota(jnp.int32, (GROUP, TOK), 0)
        mask = (r < MAIN * z) | ((r >= REM0) & (r < REM0 + REM * z))
        sweep_one(grp[x, :, 0:HD], grp[x, :, HD:W2], s_all.at[x], p_all.at[x], mask, False)

    def full_group(i, carry):
        d = jnp.where(last, lax.rem(i + 1, NX - 1) + 1, i)
        g = x - d
        xcopy(-d, g).wait_recv()
        sweep_one(grp[g, :, 0:HD], grp[g, :, HD:W2], s_all.at[g], p_all.at[g], None, False)
        return carry

    lax.fori_loop(1, x + 1, full_group, 0)

    d_ref[...] = d_ref[...] / l_ref[...]
    m_ref[...] = m_ref[...] + jnp.log2(l_ref[...])

    pieces = (pl.ds(0, HALF), pl.ds(HALF, GROUP - HALF))

    def hop(g, piece, slot, peer_x):
        return pltpu.make_async_remote_copy(
            src_ref=part.at[g, pieces[piece]],
            dst_ref=xback.at[slot, pieces[piece]],
            send_sem=xbs.at[g, piece],
            recv_sem=xbr.at[slot, piece],
            device_id={"seg": peer_x * NZ + z},
            device_id_type=MESH,
        )

    def hop_out(g, piece):
        around = last & ((g == 0) | ((g == 1) & (piece == 1)))
        slot = jnp.where(around, NX - 1 + g, g)
        up = (x == 2) & (g == 0)
        return hop(g, piece, slot, jnp.where(around, 0, jnp.where(up, NX - 1, x - 1)))

    def hop_add(piece, slot, peer_x):
        hop(0, piece, slot, peer_x).wait_recv()
        rows_in = pieces[piece]
        acc[rows_in, :] += xback[slot, rows_in, :].astype(F32)

    def back_group(i, carry):
        g = jnp.where(last & (i < x), lax.rem(i + 1, x + (x == 0)), i)
        kt[...] = grp[g, :, 0:HD].astype(F32).T.astype(BF16)
        dk, dv = sweep_two(s_all.at[g], p_all.at[g], kt)
        acc[:, 0:HD] = dk
        acc[:, HD:W2] = dv

        @pl.when(g < x)
        def _():
            for piece in range(2):

                @pl.when(last & (g == 0))
                def _(piece=piece):
                    hop_add(piece, 0, 2)

                if piece == 0:

                    @pl.when((x == 2) & (g == 1))
                    def _():
                        hop_add(0, 1, NX - 1)

                part[g, pieces[piece], :] = acc[pieces[piece], :].astype(BF16)
                hop_out(g, piece).start()

        return carry

    lax.fori_loop(0, x + jnp.minimum(z, 1), back_group, 0)

    @pl.when(z == 0)
    def _():
        acc[...] = jnp.zeros_like(acc)

    def zmain_copy(source, target):
        return pltpu.make_async_remote_copy(
            src_ref=zmain.at[target],
            dst_ref=zback.at[source],
            send_sem=zbs.at[0, target],
            recv_sem=zbr.at[0, source],
            device_id={"seg": x * NZ + target},
            device_id_type=MESH,
        )

    def zrem_copy(source, target):
        return pltpu.make_async_remote_copy(
            src_ref=zrem.at[target],
            dst_ref=zback_rem.at[source],
            send_sem=zbs.at[1, target],
            recv_sem=zbr.at[1, source],
            device_id={"seg": x * NZ + target},
            device_id_type=MESH,
        )

    def sends(source, target):
        return (source != target) & (jnp.logical_not(last) | (target < source))

    def relay():
        return pltpu.make_async_remote_copy(
            src_ref=xback.at[NX, pieces[1]],
            dst_ref=xback.at[NX, pieces[1]],
            send_sem=xbs.at[1, 1],
            recv_sem=xbr.at[NX, 1],
            device_id={"seg": NZ + z},
            device_id_type=MESH,
        )

    @pl.when(x == 0)
    def _():
        hop(1, 1, NX, NX - 1).wait_recv()
        relay().start()

    for piece in range(2):

        @pl.when(x == 0)
        def _(piece=piece):
            hop_add(piece, 0, 1)
            hop_add(piece, NX - 1, NX - 1)

        @pl.when(x == 1)
        def _(piece=piece):
            hop_add(piece, 1, 2)
            if piece == 1:
                hop_add(1, NX, 0)

        @pl.when(x == 2)
        def _(piece=piece):
            hop_add(piece, 2, NX - 1)

        for i in range(piece * NZ // 2, (piece + 1) * NZ // 2):
            zmain[i] = acc[i * MAIN : (i + 1) * MAIN, :].astype(BF16)

            @pl.when(sends(z, i))
            def _(i=i):
                zmain_copy(z, i).start()

    for i in range(NZ):
        zrem[i] = acc[REM0 + REM * i : REM0 + REM * (i + 1), :].astype(BF16)

        @pl.when(sends(z, i))
        def _(i=i):
            zrem_copy(z, i).start()

    dk, dv = sweep_two(s_own, p_own, kt_own)
    dko_ref[...] = dk.astype(BF16)
    dvo_ref[...] = dv.astype(BF16)
    for h in range(HEADS):
        dq_ref[:, h * HD : (h + 1) * HD] = (dqt[:, lanes(h)] * SCALE).T.astype(BF16)
    stores = [
        pltpu.make_async_copy(src, dst, outsem.at[i])
        for i, (src, dst) in enumerate(((dq_ref, dq_hbm), (dko_ref, dko_hbm), (dvo_ref, dvo_hbm)))
    ]
    for copy in stores:
        copy.start()

    acc[0:MAIN, :] = zmain[z].astype(F32)
    acc[MAIN:M, :] = zrem[z].astype(F32)
    for i in range(NZ):

        @pl.when(sends(i, z))
        def _(i=i):
            zmain_copy(i, z).wait_recv()
            acc[0:MAIN, :] += zback[i].astype(F32)

    for i in range(NZ):

        @pl.when(sends(i, z))
        def _(i=i):
            zrem_copy(i, z).wait_recv()
            acc[MAIN:M, :] += zback_rem[i].astype(F32)

    em[0:MAIN, :] = acc[0:MAIN, :].astype(BF16)
    em[MAIN:BLOCK, :] = jnp.where(
        row == 0, acc[MAIN : MAIN + 1, :], jnp.where(row == 1, acc[MAIN + 1 : M, :], 0.0)
    ).astype(BF16)

    def ecopy():
        return pltpu.make_async_remote_copy(
            src_ref=em,
            dst_ref=etwin,
            send_sem=es,
            recv_sem=er,
            device_id={"tp": twin},
            device_id_type=MESH,
        )

    ecopy().start()
    order = (2, 1, 3, 0)
    for d in order:
        target = y_peer(d)[1]
        chunk = pl.ds(pl.multiple_of(target * cols, cols), cols)
        state[d] = dot(em[...], w[chunk, :], LAST)
    for i in range(NY):
        wcopy(i).wait_recv()
    ecopy().wait_recv()

    half = cols // 2
    lo, hi = slice(0, half), slice(half, cols)
    below, above = y_peer(NY - 1)[1], y_peer(1)[1]
    targets = (below, above, below, below, above, above)
    sources = (above, below, above, above, below, below)

    def tcopy(i, target):
        return pltpu.make_async_remote_copy(
            src_ref=tsend.at[i],
            dst_ref=trecv.at[i],
            send_sem=ts.at[i],
            recv_sem=tr.at[i],
            device_id={"tp": target},
            device_id_type=MESH,
        )

    def put(i, value):
        tsend[i] = value.astype(BF16)
        tcopy(i, targets[i]).start()

    def take(i):
        tcopy(i, sources[i]).wait_recv()
        return trecv[i].astype(F32)

    def both(d):
        return (state[d] + dot(etwin[...], wtwin[y_peer(d)[0]], LAST))[0:M]

    value = both(2)
    put(0, value[:, lo])
    put(1, value[:, hi])
    value = both(NY - 1)
    put(3, value[:, hi])
    state[NY - 1, 0:M, :] = value
    value = both(1)
    put(4, value[:, lo])
    state[1, 0:M, :] = value
    state[0, 0:M, :] = both(0) + sg_ref[...].astype(F32)
    put(2, state[NY - 1, 0:M, lo] + take(0))
    put(5, state[1, 0:M, hi] + take(1))
    out_hi = state[0, 0:M, hi] + take(3)
    out_lo = state[0, 0:M, lo] + take(4)
    out_ref[:, lo] = (out_lo + take(2)).astype(BF16)
    out_ref[:, hi] = (out_hi + take(5)).astype(BF16)

    for copy in stores:
        copy.wait()
    for d in range(1, NZ):
        other, peer = z_peer(x, z, d)

        @pl.when(jnp.logical_not(last) | (other > z))
        def _(d=d, peer=peer):
            for copy in zcopies(d, peer, z):
                copy.wait_send()

    for i in range(NZ):

        @pl.when(sends(z, i))
        def _(i=i):
            zmain_copy(z, i).wait_send()
            zrem_copy(z, i).wait_send()

    lax.fori_loop(1, NX - x, lambda d, c: (xcopy(d, x).wait_send(), c)[1], 0)
    for piece in range(2):
        lax.fori_loop(0, x, lambda g, c: (hop_out(g, piece).wait_send(), c)[1], 0)
    for i in range(NY):
        wcopy(i).wait_send()
    ecopy().wait_send()
    @pl.when(x == 0)
    def _():
        relay().wait_send()

    for i in range(len(targets)):
        tcopy(i, targets[i]).wait_send()


def emit_kernel(count, *refs):
    ins, outs, bufs = refs[:count], refs[count : 2 * count], refs[2 * count : 3 * count]
    sems = refs[3 * count]
    loads = [pltpu.make_async_copy(ins[i], bufs[i], sems.at[0, i]) for i in range(count)]
    stores = [pltpu.make_async_copy(bufs[i], outs[i], sems.at[1, i]) for i in range(count)]
    for copy in loads:
        copy.start()
    for load, store in zip(loads, stores):
        load.wait()
        store.start()
    for copy in stores:
        copy.wait()


def emit(arrays):
    anywhere = pl.BlockSpec(memory_space=pl.ANY)
    count = len(arrays)
    return pl.pallas_call(
        functools.partial(emit_kernel, count),
        name="emit",
        out_shape=tuple(jax.ShapeDtypeStruct(a.shape, a.dtype) for a in arrays),
        in_specs=[anywhere] * count,
        out_specs=(anywhere,) * count,
        scratch_shapes=[pltpu.VMEM(a.shape, a.dtype) for a in arrays]
        + [pltpu.SemaphoreType.DMA((2, count))],
    )(*arrays)


def per_device(
    queries, keys_own, values_own, out_grad, summary_states, w_key, w_value, summary_grad
):
    anywhere = pl.BlockSpec(memory_space=pl.ANY)
    rows = HEADS * TOK
    cols = D // NTP
    dma = pltpu.SemaphoreType.DMA
    arrays = pl.pallas_call(
        layer_kernel,
        name="layer",
        out_shape=(
            jax.ShapeDtypeStruct((TOK, HEADS * HD), BF16),
            jax.ShapeDtypeStruct((TOK, HD), BF16),
            jax.ShapeDtypeStruct((TOK, HD), BF16),
            jax.ShapeDtypeStruct((M, cols), BF16),
        ),
        in_specs=[anywhere] * 8,
        out_specs=(anywhere,) * 3 + (pl.BlockSpec(memory_space=pltpu.VMEM),),
        scratch_shapes=[
            pltpu.VMEM((TOK, HEADS * HD), BF16),
            pltpu.VMEM((TOK, HEADS * HD), BF16),
            pltpu.VMEM((TOK, HD), BF16),
            pltpu.VMEM((TOK, HD), BF16),
            pltpu.VMEM((M, D), BF16),
            pltpu.VMEM((D, W2), BF16),
            pltpu.VMEM((M, cols), BF16),
            pltpu.VMEM((MAIN, W2), BF16),
            pltpu.VMEM((REM, W2), BF16),
            pltpu.VMEM((NZ, REM, W2), BF16),
            pltpu.VMEM((NX, GROUP, W2), BF16),
            pltpu.VMEM((TOK, rows), F32),
            pltpu.VMEM((TOK, rows), F32),
            pltpu.VMEM((NX, GROUP, rows), F32),
            pltpu.VMEM((NX, GROUP, rows), F32),
            pltpu.VMEM((1, rows), F32),
            pltpu.VMEM((1, rows), F32),
            pltpu.VMEM((1, rows), F32),
            pltpu.VMEM((HD, rows), F32),
            pltpu.VMEM((HD, TOK), BF16),
            pltpu.VMEM((HD, GROUP), BF16),
            pltpu.VMEM((GROUP, HD), F32),
            pltpu.VMEM((GROUP, HD), F32),
            pltpu.VMEM((NX, GROUP, W2), BF16),
            pltpu.VMEM((NX + 1, GROUP, W2), BF16),
            pltpu.VMEM((GROUP, W2), F32),
            pltpu.VMEM((NZ, MAIN, W2), BF16),
            pltpu.VMEM((NZ, REM, W2), BF16),
            pltpu.VMEM((NZ, MAIN, W2), BF16),
            pltpu.VMEM((NZ, REM, W2), BF16),
            pltpu.VMEM((BLOCK, W2), BF16),
            pltpu.VMEM((BLOCK, W2), BF16),
            pltpu.VMEM((NY, cols, W2), BF16),
            pltpu.VMEM((NY, BLOCK, cols), F32),
            pltpu.VMEM((6, M, cols // 2), BF16),
            pltpu.VMEM((6, M, cols // 2), BF16),
            pltpu.VMEM((TOK, HEADS * HD), BF16),
            pltpu.VMEM((TOK, HD), BF16),
            pltpu.VMEM((TOK, HD), BF16),
            dma((WCHUNK, 2)),
            dma((6,)),
            dma((3,)),
            dma((2, NZ - 1)),
            dma((2, NZ - 1)),
            dma((NX - 1,)),
            dma((NX - 1,)),
            dma((NX - 1, 2)),
            dma((NX + 1, 2)),
            dma((2, NZ)),
            dma((2, NZ)),
            dma((6,)),
            dma((6,)),
            dma((NY,)),
            dma((NY,)),
            dma,
            dma,
        ],
        compiler_params=pltpu.CompilerParams(
            collective_id=0, has_side_effects=True, vmem_limit_bytes=58 << 20
        ),
    )(
        queries, out_grad, keys_own, values_own, summary_states, w_key, w_value, summary_grad
    )
    return emit(arrays)


def solution(mesh):
    placed = (
        P("seg", "tp"),
        P("seg", "tp"),
        P("seg", "tp"),
        P("seg", "tp"),
        P("seg", None),
        P(None, "tp"),
        P(None, "tp"),
        P("seg", "tp"),
    )
    return jax.shard_map(
        per_device,
        mesh=mesh,
        in_specs=placed,
        out_specs=(P("seg", "tp"), P("seg", "tp"), P("seg", "tp"), P("seg", "tp")),
        check_vma=False,
    )
```
